32 devices in a mesh: dp: 8 (over z, y), ctx: 4 (over x, core).
Axes of the slice: x: 2, y: 2, z: 4, core: 2. Of those that a mesh axis runs over, the one named last changes fastest.
Arguments:
- layer_input: bfloat16 [16, 1024, 1600], P('dp', 'ctx'), may hold values from -6 to 6
- grad_out: bfloat16 [16, 1024, 1600], P('dp', 'ctx'), may hold values from -6 to 6
- segment_ids: int32 [16, 1024], P('dp'), may hold values from 0 to 7, as said below
- qkv_weight: bfloat16 [1600, 4800], P('ctx', 'dp'), may hold values from -0.15625 to 0.15625
- q_bias: bfloat16 [1600], P('dp'), may hold values from -1.796875 to 1.796875
- v_bias: bfloat16 [1600], P('dp'), may hold values from -1.796875 to 1.796875
- out_weight: bfloat16 [1600, 1600], P('ctx', 'dp'), may hold values from -0.875 to 0.875
- out_bias: bfloat16 [1600], P('dp'), may hold values from -1.796875 to 1.796875
- fc_weight: bfloat16 [1600, 6400], P('ctx', 'dp'), may hold values from -0.15625 to 0.15625
- fc_bias: bfloat16 [6400], P('dp'), may hold values from -1.796875 to 1.796875
- proj_weight: bfloat16 [6400, 1600], P('ctx', 'dp'), may hold values from -0.078125 to 0.078125
- proj_bias: bfloat16 [1600], P('dp'), may hold values from -1.796875 to 1.796875
- ln1_gain: bfloat16 [1600], P('dp'), may hold values from 0.5 to 1.5
- ln1_bias: bfloat16 [1600], P('dp'), may hold values from -1.796875 to 1.796875
- ln2_gain: bfloat16 [1600], P('dp'), may hold values from 0.5 to 1.5
- ln2_bias: bfloat16 [1600], P('dp'), may hold values from -1.796875 to 1.796875
Outputs:
- output: bfloat16 [16, 1024, 1600], P('dp', 'ctx')
- input_grad: float32 [16, 1024, 1600], P('dp', 'ctx')
- qkv_weight_grad: float32 [1600, 4800], P('ctx', 'dp')
- q_bias_grad: float32 [1600], P('dp')
- v_bias_grad: float32 [1600], P('dp')
- out_weight_grad: float32 [1600, 1600], P('ctx', 'dp')
- out_bias_grad: float32 [1600], P('dp')
- fc_weight_grad: float32 [1600, 6400], P('ctx', 'dp')
- fc_bias_grad: float32 [6400], P('dp')
- proj_weight_grad: float32 [6400, 1600], P('ctx', 'dp')
- proj_bias_grad: float32 [1600], P('dp')
- ln1_gain_grad: float32 [1600], P('dp')
- ln1_bias_grad: float32 [1600], P('dp')
- ln2_gain_grad: float32 [1600], P('dp')
- ln2_bias_grad: float32 [1600], P('dp')
The draws below stay inside these ranges and needn't reach their ends.
Inputs may be any that keep to these rules, and one draw needn't show every extreme that they name: `segment_ids`: ids start at 0 in every sequence, never fall along it, and rise by at most one from one position to the next.
All inputs are finite; a program needn't handle non-finite values.
Results may differ from the reference program's by a relative error of at most 0.012.
Values may be sent and summed in bfloat16 or wider, within the bound.
A program may use at most 384 MiB of HBM per device.

```python
import jax
import jax.numpy as jnp
from jax import lax

D = 1600
HEADS = 25
HEAD_DIM = 64
FF = 6400
SEQ_LEN = 1024
SEQ_DP = 2
SEQS = 16


def draw_segment_ids(key, part):
    spacing = max(SEQ_LEN // 6, 2)
    cuts = jax.random.randint(jax.random.fold_in(key, 11), (SEQS, SEQ_LEN), 0, spacing) == 0
    position = jnp.arange(SEQ_LEN)[None, :]
    picked = jax.random.randint(jax.random.fold_in(key, 12), (SEQS // SEQ_DP, 1), 0, SEQ_DP)
    group_pick = jnp.repeat(picked, SEQ_DP, axis=0)
    member = (jnp.arange(SEQS) % SEQ_DP)[:, None]
    single = member == group_pick
    busiest = member == (group_pick + 1) % SEQ_DP
    forced = busiest & (position % (SEQ_LEN // 8) == 0)
    cuts = (cuts | forced) & (position > 0) & jnp.logical_not(single)
    return jnp.minimum(jnp.cumsum(cuts.astype(jnp.int32), axis=1), 7).astype(jnp.int32)


def level_of(stream_key, dims, shards, least, high):
    level, own = 1.0, jax.random.fold_in(stream_key, 6)
    for dim, parts in shards:
        draws = jnp.exp(jax.random.uniform(jax.random.fold_in(own, dim), (parts,), jnp.float32, least / len(shards), high / len(shards)))
        level = level * jnp.repeat(draws, dims[dim] // parts).reshape([-1 if axis == dim else 1 for axis in range(len(dims))])
    return level


def scatter_about(rng, extent, deviation, most, cuts=(), held_as=jnp.bfloat16):
    values = jax.random.normal(rng, extent, jnp.float32) * deviation
    if len(cuts) > 0:
        values = level_of(rng, extent, cuts, -0.22, 0.18) * values
    return jnp.clip(values, min=-most, max=most).astype(held_as)


def setup_inputs(seed: int = 0) -> dict:
    streams_of = jax.random.split(jax.random.key(seed), 17)
    layer_input = scatter_about(streams_of[0], (SEQS, SEQ_LEN, D), 1.0, 6.0, ((0, 8), (1, 4)))
    grad_out = scatter_about(streams_of[1], (SEQS, SEQ_LEN, D), 1.0, 6.0, ((0, 8), (1, 4)))
    segment_ids = draw_segment_ids(jax.random.fold_in(streams_of[16], 71), 0)
    qkv_weight = scatter_about(streams_of[3], (D, 3 * D), D ** -0.5, 0.15625, ((0, 4), (1, 8)))
    q_bias = scatter_about(streams_of[4], (D,), 0.3, 1.796875, ((0, 8),))
    v_bias = scatter_about(streams_of[5], (D,), 0.3, 1.796875, ((0, 8),))
    out_weight = scatter_about(streams_of[6], (D, D), (D // 32) ** -0.5, 0.875, ((0, 4), (1, 8)))
    out_bias = scatter_about(streams_of[7], (D,), 0.3, 1.796875, ((0, 8),))
    fc_weight = scatter_about(streams_of[8], (D, FF), D ** -0.5, 0.15625, ((0, 4), (1, 8)))
    fc_bias = scatter_about(streams_of[9], (FF,), 0.3, 1.796875, ((0, 8),))
    proj_weight = scatter_about(streams_of[10], (FF, D), FF ** -0.5, 0.078125, ((0, 4), (1, 8)))
    proj_bias = scatter_about(streams_of[11], (D,), 0.3, 1.796875, ((0, 8),))
    ln1_gain = jnp.clip(1.0 + 0.1 * jax.random.normal(streams_of[12], (D,), jnp.float32), 0.5, 1.5).astype(jnp.bfloat16)
    ln1_bias = scatter_about(streams_of[13], (D,), 0.3, 1.796875, ((0, 8),))
    ln2_gain = jnp.clip(1.0 + 0.1 * jax.random.normal(streams_of[14], (D,), jnp.float32), 0.5, 1.5).astype(jnp.bfloat16)
    ln2_bias = scatter_about(streams_of[15], (D,), 0.3, 1.796875, ((0, 8),))
    return dict(layer_input=layer_input, grad_out=grad_out, segment_ids=segment_ids, qkv_weight=qkv_weight, q_bias=q_bias, v_bias=v_bias, out_weight=out_weight, out_bias=out_bias, fc_weight=fc_weight, fc_bias=fc_bias, proj_weight=proj_weight, proj_bias=proj_bias, ln1_gain=ln1_gain, ln1_bias=ln1_bias, ln2_gain=ln2_gain, ln2_bias=ln2_bias)


EPS = 1e-05
HIGH = lax.Precision.HIGHEST

@jax.custom_vjp
def low(v):
    return lax.optimization_barrier(v.astype(jnp.bfloat16)).astype(jnp.float32)

@jax.custom_vjp
def low_back(v):
    return v

def low_keep(v):
    return (low(v), None)

def low_pass(kept, grad):
    return (grad,)

def back_keep(v):
    return (v, None)

def back_low(kept, grad):
    return (low(grad),)
low.defvjp(low_keep, low_pass)
low_back.defvjp(back_keep, back_low)

def layer_norm(values, gain, shift):
    center = values - lax.optimization_barrier(jnp.mean(values, axis=-1, keepdims=True))
    factor = lax.rsqrt(lax.optimization_barrier(jnp.mean(center * center, axis=-1, keepdims=True)) + EPS)
    return center * factor * gain + shift

def gelu_tanh(values):
    return 0.5 * values * (1.0 + jnp.tanh(0.7978845608028654 * (values + 0.044715 * values * values * values)))

def block_forward(params, values, segments):
    qkv_weight, q_bias, v_bias, out_weight, out_bias, fc_weight, fc_bias, proj_weight, proj_bias, ln1_gain, ln1_bias, ln2_gain, ln2_bias = params
    length = values.shape[0]
    model_width = q_bias.shape[0]
    normed1 = low(layer_norm(values, ln1_gain, ln1_bias))
    joined_bias = jnp.concatenate([q_bias, jnp.zeros_like(q_bias), v_bias])
    projected = low(low_back(jnp.dot(normed1, qkv_weight, precision=HIGH) + joined_bias))
    queries = projected[:, :model_width].reshape(length, HEADS, HEAD_DIM)
    key_rows = projected[:, model_width:2 * model_width].reshape(length, HEADS, HEAD_DIM)
    value_rows = projected[:, 2 * model_width:].reshape(length, HEADS, HEAD_DIM)
    scores = low_back(jnp.einsum('qhd,khd->hqk', queries, key_rows, precision=HIGH) * 0.125)
    position = jnp.arange(length)
    allowed = (position[None, :] <= position[:, None]) & (segments[None, :] == segments[:, None])
    scores = jnp.where(allowed[None], scores, -jnp.inf)
    attn_weights = low(jax.nn.softmax(scores, axis=-1))
    attended = jnp.einsum('hqk,khd->qhd', attn_weights, value_rows, precision=HIGH).reshape(length, model_width)
    attended = low(low_back(attended))
    branch = low_back(jnp.dot(attended, out_weight, precision=HIGH) + out_bias)
    hidden = values + branch
    normed2 = low(layer_norm(hidden, ln2_gain, ln2_bias))
    inner = low_back(jnp.dot(normed2, fc_weight, precision=HIGH) + fc_bias)
    activated = low(gelu_tanh(inner))
    mlp_out = low_back(jnp.dot(activated, proj_weight, precision=HIGH) + proj_bias)
    return hidden + mlp_out

def reference(layer_input, grad_out, segment_ids, qkv_weight, q_bias, v_bias, out_weight, out_bias, fc_weight, fc_bias, proj_weight, proj_bias, ln1_gain, ln1_bias, ln2_gain, ln2_bias):
    params = tuple((weight.astype(jnp.float32) for weight in (qkv_weight, q_bias, v_bias, out_weight, out_bias, fc_weight, fc_bias, proj_weight, proj_bias, ln1_gain, ln1_bias, ln2_gain, ln2_bias)))

    def per_sequence(grad_totals, sample):
        values, cotangent, segments = sample

        def forward_of(inputs, weights):
            return block_forward(weights, inputs, segments)
        result, pullback = jax.vjp(forward_of, values.astype(jnp.float32), params)
        value_grad, param_grads = pullback(cotangent.astype(jnp.float32))
        grad_totals = jax.tree.map(lambda first, second: first + second, grad_totals, param_grads)
        return (grad_totals, (result.astype(jnp.bfloat16), value_grad))
    zero_grads = jax.tree.map(jnp.zeros_like, params)
    grad_totals, (results, input_grads) = lax.scan(per_sequence, zero_grads, (layer_input, grad_out, segment_ids))
    return (results, input_grads) + tuple(grad_totals)
```

```python
import functools

import jax
import jax.numpy as jnp
from jax import lax
from jax.experimental import pallas as pl
from jax.experimental.pallas import tpu as pltpu
from jax.sharding import PartitionSpec as P

HEADS = 25
HEAD_DIM = 64
LANES = 128
EPS = 1e-05
NEG_FILL = -1e30
GELU_C = 0.7978845608028654
GELU_A = 0.044715

bf16 = jnp.bfloat16
f32 = jnp.float32
VMEM_LIMIT = 58 * 1024 * 1024


def layer_norm(values, gain, shift):
    center = values - jnp.mean(values, axis=-1, keepdims=True)
    factor = lax.rsqrt(jnp.mean(center * center, axis=-1, keepdims=True) + EPS)
    return center * factor * gain + shift


def dot_nn(a, b):
    return lax.dot_general(a, b, (((1,), (0,)), ((), ())), preferred_element_type=f32)


def dot_nt(a, b):
    return lax.dot_general(a, b, (((1,), (1,)), ((), ())), preferred_element_type=f32)


def dot_tn(a, b):
    return lax.dot_general(a, b, (((0,), (0,)), ((), ())), preferred_element_type=f32)


def params(n_axes=1):
    return pltpu.CompilerParams(
        dimension_semantics=("arbitrary",) * n_axes, vmem_limit_bytes=VMEM_LIMIT
    )


def cost(flops, read, transcendentals=0):
    return pl.CostEstimate(
        flops=int(flops), bytes_accessed=int(read), transcendentals=int(transcendentals)
    )


def qkv_project(normed, weight, bias):
    tokens, width = normed.shape
    parts, _, n = weight.shape

    def kernel(x_ref, w_ref, b_ref, *out_refs):
        part = pl.program_id(0)
        y = (dot_nn(x_ref[...], w_ref[0]) + b_ref[0]).astype(bf16)
        for d in range(parts):

            @pl.when(part == d)
            def _():
                first, last = d * n, (d + 1) * n
                for g in range(3):
                    lo, hi = max(first, g * width), min(last, (g + 1) * width)
                    if lo < hi:
                        out_refs[g][:, lo - g * width : hi - g * width] = y[
                            :, lo - first : hi - first
                        ]

    whole = pl.BlockSpec((tokens, width), lambda d: (0, 0))
    return pl.pallas_call(
        kernel,
        grid=(parts,),
        in_specs=[
            whole,
            pl.BlockSpec((1, width, n), lambda d: (d, 0, 0)),
            pl.BlockSpec((1, 1, n), lambda d: (d, 0, 0)),
        ],
        out_specs=[whole] * 3,
        out_shape=[jax.ShapeDtypeStruct((tokens, width), bf16)] * 3,
        compiler_params=params(),
        cost_estimate=cost(2 * tokens * width * parts * n, 2 * width * parts * n),
        name="qkv",
    )(normed, weight, bias)


def pair_masks(pair, width):
    lane = lax.broadcasted_iota(jnp.int32, (1, LANES), 1)
    inside = lane + pair * LANES < width
    return inside & (lane < HEAD_DIM), inside & (lane >= HEAD_DIM), inside


def attention_forward(bounds, queries, pairs_full, seg_col, seg_row):
    seqs, rows, width = queries.shape
    blocks = pairs_full.shape[0]
    pairs = pl.cdiv(width, LANES)

    def kernel(bounds_ref, q_ref, kv_ref, sc_ref, sr_ref, o_ref, of_ref, lse_ref):
        seq, pair = pl.program_id(0), pl.program_id(1)
        mine, start = bounds_ref[0], bounds_ref[1 + seq]
        low, high, inside = pair_masks(pair, width)
        scaled = q_ref[0] * jnp.asarray(0.125, bf16)
        q_heads = (
            jnp.where(low, scaled, jnp.zeros_like(scaled)),
            jnp.where(high, scaled, jnp.zeros_like(scaled)),
        )
        seg_q = sc_ref[0]

        def block(j, diagonal, carry):
            k = jnp.where(inside, kv_ref[j, 0, 0], jnp.zeros((rows, LANES), bf16))
            v = jnp.where(inside, kv_ref[j, 1, 0], jnp.zeros((rows, LANES), bf16))
            allowed = sr_ref[0, j] == seg_q
            if diagonal:
                at_row = lax.broadcasted_iota(jnp.int32, (rows, rows), 0)
                at_col = lax.broadcasted_iota(jnp.int32, (rows, rows), 1)
                allowed = allowed & (at_col <= at_row)
            out = []
            for head in range(2):
                s = jnp.where(allowed, dot_nt(q_heads[head], k), NEG_FILL)
                top = jnp.max(s, axis=1, keepdims=True)
                if carry is None:
                    p = jnp.exp(s - top)
                    out += [top, jnp.sum(p, axis=1, keepdims=True), dot_nn(p.astype(bf16), v)]
                else:
                    m, l, acc = carry[3 * head : 3 * head + 3]
                    new = jnp.maximum(m, top)
                    scale = jnp.exp(m - new)
                    p = jnp.exp(s - new)
                    out += [
                        new,
                        l * scale + jnp.sum(p, axis=1, keepdims=True),
                        acc * scale + dot_nn(p.astype(bf16), v),
                    ]
            return tuple(out)

        carry = block(mine, True, None)
        carry = lax.fori_loop(start, mine, lambda j, c: block(j, False, c), carry)
        m0, l0, a0, m1, l1, a1 = carry
        result = jnp.where(low, a0 / l0, a1 / l1)
        o_ref[0] = result.astype(bf16)
        of_ref[0] = result
        lse_ref[0] = jnp.where(low, m0 + jnp.log(l0), m1 + jnp.log(l1))

    tile = pl.BlockSpec((1, rows, LANES), lambda s, p, b: (s, 0, p))
    return pl.pallas_call(
        kernel,
        grid_spec=pltpu.PrefetchScalarGridSpec(
            num_scalar_prefetch=1,
            grid=(seqs, pairs),
            in_specs=[
                tile,
                pl.BlockSpec((blocks, 2, 1, rows, LANES), lambda s, p, b: (0, 0, s, 0, p)),
                pl.BlockSpec((1, rows, 1), lambda s, p, b: (s, 0, 0)),
                pl.BlockSpec((1, blocks, 1, rows), lambda s, p, b: (s, 0, 0, 0)),
            ],
            out_specs=[tile, tile, tile],
        ),
        out_shape=[
            jax.ShapeDtypeStruct((seqs, rows, width), bf16),
            jax.ShapeDtypeStruct((seqs, rows, width), f32),
            jax.ShapeDtypeStruct((seqs, rows, width), f32),
        ],
        compiler_params=params(2),
        cost_estimate=cost(
            4 * seqs * rows * rows * blocks * width, 4 * seqs * rows * blocks * width
        ),
        name="attn_fwd",
    )(bounds, queries, pairs_full, seg_col, seg_row)


def attention_backward(
    bounds, queries, pairs_full, seg_col, seg_row, out_grad, out_full, log_total
):
    seqs, rows, width = queries.shape
    blocks = pairs_full.shape[0]
    pairs = pl.cdiv(width, LANES)

    def kernel(bounds_ref, q_ref, kv_ref, sc_ref, sr_ref, g_ref, of_ref, lse_ref, dq_ref, dkv_ref):
        seq, pair = pl.program_id(0), pl.program_id(1)
        mine, start = bounds_ref[0], bounds_ref[1 + seq]
        low, high, inside = pair_masks(pair, width)
        zero = jnp.zeros((rows, LANES), bf16)
        scaled = q_ref[0] * jnp.asarray(0.125, bf16)
        grad = g_ref[0]
        q_heads = (jnp.where(low, scaled, zero), jnp.where(high, scaled, zero))
        g_heads = (jnp.where(low, grad, zero), jnp.where(high, grad, zero))
        product = jnp.where(inside, grad.astype(f32) * of_ref[0], 0.0)
        lse = jnp.where(inside, lse_ref[0], 0.0)
        product_t = product.T
        lse_t = lse.T
        delta = (
            jnp.sum(product_t[:HEAD_DIM], axis=0, keepdims=True),
            jnp.sum(product_t[HEAD_DIM:], axis=0, keepdims=True),
        )
        log_row = (lse_t[0:1], lse_t[HEAD_DIM : HEAD_DIM + 1])
        seg_q = sr_ref[0]
        dkv_ref[...] = jnp.zeros_like(dkv_ref)

        def block(j, diagonal, total):
            k = jnp.where(inside, kv_ref[j, 0, 0], zero)
            v = jnp.where(inside, kv_ref[j, 1, 0], zero)
            allowed = sc_ref[0, j] == seg_q
            if diagonal:
                at_key = lax.broadcasted_iota(jnp.int32, (rows, rows), 0)
                at_query = lax.broadcasted_iota(jnp.int32, (rows, rows), 1)
                allowed = allowed & (at_key <= at_query)
            key_grad, value_grad = None, None
            for head in range(2):
                k_head = jnp.where((low, high)[head], k, zero)
                s = jnp.where(allowed, dot_nt(k, q_heads[head]), NEG_FILL)
                p = jnp.exp(s - log_row[head])
                pushed = dot_nt(v, g_heads[head])
                ds = (p * (pushed - delta[head])).astype(bf16)
                dv = dot_nn(p.astype(bf16), g_heads[head])
                dk = dot_nn(ds, q_heads[head])
                dq = dot_tn(ds, k_head)
                key_grad = dk if key_grad is None else key_grad + dk
                value_grad = dv if value_grad is None else value_grad + dv
                total = dq if total is None else total + dq
            dkv_ref[j, 0, 0] = key_grad.astype(bf16)
            dkv_ref[j, 1, 0] = value_grad.astype(bf16)
            return total

        total = block(mine, True, None)
        total = lax.fori_loop(start, mine, lambda j, c: block(j, False, c), total)
        dq_ref[0] = (total * 0.125).astype(bf16)

    tile = pl.BlockSpec((1, rows, LANES), lambda s, p, b: (s, 0, p))
    many = pl.BlockSpec((blocks, 2, 1, rows, LANES), lambda s, p, b: (0, 0, s, 0, p))
    return pl.pallas_call(
        kernel,
        grid_spec=pltpu.PrefetchScalarGridSpec(
            num_scalar_prefetch=1,
            grid=(seqs, pairs),
            in_specs=[
                tile,
                many,
                pl.BlockSpec((1, blocks, rows, 1), lambda s, p, b: (s, 0, 0, 0)),
                pl.BlockSpec((1, 1, rows), lambda s, p, b: (s, 0, 0)),
                tile,
                tile,
                tile,
            ],
            out_specs=[tile, many],
        ),
        out_shape=[
            jax.ShapeDtypeStruct((seqs, rows, width), bf16),
            jax.ShapeDtypeStruct(pairs_full.shape, bf16),
        ],
        compiler_params=params(2),
        cost_estimate=cost(
            10 * seqs * rows * rows * blocks * width, 8 * seqs * rows * blocks * width
        ),
        name="attn_bwd",
    )(bounds, queries, pairs_full, seg_col, seg_row, out_grad, out_full, log_total)


def feed_in(normed, weight, bias, groups):
    tokens, width = normed.shape
    parts, _, n = weight.shape
    ratio = parts // groups

    def kernel(x_ref, w_ref, b_ref, inner_ref, act_ref):
        place = lax.rem(pl.program_id(0), ratio)
        u = dot_nn(x_ref[...], w_ref[0]) + b_ref[0]
        act = (0.5 * u * (1.0 + jnp.tanh(GELU_C * (u + GELU_A * u * u * u)))).astype(bf16)
        for r in range(ratio):

            @pl.when(place == r)
            def _():
                inner_ref[0, :, r * n : (r + 1) * n] = u
                act_ref[0, :, r * n : (r + 1) * n] = act

    out = pl.BlockSpec((1, tokens, ratio * n), lambda d: (d // ratio, 0, 0))
    return pl.pallas_call(
        kernel,
        grid=(parts,),
        in_specs=[
            pl.BlockSpec((tokens, width), lambda d: (0, 0)),
            pl.BlockSpec((1, width, n), lambda d: (d, 0, 0)),
            pl.BlockSpec((1, 1, n), lambda d: (d, 0, 0)),
        ],
        out_specs=[out, out],
        out_shape=[
            jax.ShapeDtypeStruct((groups, tokens, ratio * n), f32),
            jax.ShapeDtypeStruct((groups, tokens, ratio * n), bf16),
        ],
        compiler_params=params(),
        cost_estimate=cost(2 * tokens * width * parts * n, 2 * width * parts * n),
        name="fc",
    )(normed, weight, bias)


def feed_out(act, weight, hidden, bias):
    groups, tokens, f = act.shape
    width = weight.shape[1]

    def kernel(a_ref, w_ref, h_ref, b_ref, o_ref, acc_ref):
        step = pl.program_id(0)

        @pl.when(step == 0)
        def _():
            acc_ref[...] = h_ref[...] + b_ref[...]

        acc_ref[...] += dot_nt(a_ref[0], w_ref[0])

        @pl.when(step == groups - 1)
        def _():
            o_ref[...] = acc_ref[...].astype(bf16)

    return pl.pallas_call(
        kernel,
        grid=(groups,),
        in_specs=[
            pl.BlockSpec((1, tokens, f), lambda c: (c, 0, 0)),
            pl.BlockSpec((1, width, f), lambda c: (c, 0, 0)),
            pl.BlockSpec((tokens, width), lambda c: (0, 0)),
            pl.BlockSpec((1, width), lambda c: (0, 0)),
        ],
        out_specs=pl.BlockSpec((tokens, width), lambda c: (0, 0)),
        out_shape=jax.ShapeDtypeStruct((tokens, width), bf16),
        scratch_shapes=[pltpu.VMEM((tokens, width), f32)],
        compiler_params=params(),
        cost_estimate=cost(2 * groups * tokens * width * f, 2 * groups * width * f),
        name="proj",
    )(act, weight, hidden, bias)


def feed_back(grad, weight, inner, parts):
    groups, tokens, f = inner.shape
    width = weight.shape[1]
    ratio = parts // groups
    n = f // ratio

    def kernel(g_ref, w_ref, u_ref, o_ref, s_ref):
        u = u_ref[0]
        t = jnp.tanh(GELU_C * (u + GELU_A * u * u * u))
        slope = 0.5 * (1.0 + t) + 0.5 * u * (1.0 - t * t) * (
            GELU_C * (1.0 + 3.0 * GELU_A * u * u)
        )
        out = (dot_nn(g_ref[...], w_ref[0]) * slope).astype(bf16)
        total = jnp.sum(out.astype(f32), axis=0, keepdims=True)
        for r in range(ratio):
            o_ref[r] = out[:, r * n : (r + 1) * n]
            s_ref[r] = total[:, r * n : (r + 1) * n]

    return pl.pallas_call(
        kernel,
        grid=(groups,),
        in_specs=[
            pl.BlockSpec((tokens, width), lambda c: (0, 0)),
            pl.BlockSpec((1, width, f), lambda c: (c, 0, 0)),
            pl.BlockSpec((1, tokens, f), lambda c: (c, 0, 0)),
        ],
        out_specs=[
            pl.BlockSpec((ratio, tokens, n), lambda c: (c, 0, 0)),
            pl.BlockSpec((ratio, 1, n), lambda c: (c, 0, 0)),
        ],
        out_shape=[
            jax.ShapeDtypeStruct((parts, tokens, n), bf16),
            jax.ShapeDtypeStruct((parts, 1, n), f32),
        ],
        compiler_params=params(),
        cost_estimate=cost(2 * groups * tokens * width * f, 6 * groups * width * f),
        name="act_bwd",
    )(grad, weight, inner)


def back_project(grads, weight):
    parts, tokens, n = grads.shape
    width = weight.shape[1]

    def kernel(g_ref, w_ref, o_ref):
        @pl.when(pl.program_id(0) == 0)
        def _():
            o_ref[...] = dot_nt(g_ref[0], w_ref[0])

        @pl.when(pl.program_id(0) > 0)
        def _():
            o_ref[...] += dot_nt(g_ref[0], w_ref[0])

    return pl.pallas_call(
        kernel,
        grid=(parts,),
        in_specs=[
            pl.BlockSpec((1, tokens, n), lambda d: (d, 0, 0)),
            pl.BlockSpec((1, width, n), lambda d: (d, 0, 0)),
        ],
        out_specs=pl.BlockSpec((tokens, width), lambda d: (0, 0)),
        out_shape=jax.ShapeDtypeStruct((tokens, width), f32),
        compiler_params=params(),
        cost_estimate=cost(2 * parts * tokens * width * n, 2 * parts * width * n),
        name="back",
    )(grads, weight)


def weight_grad(left, right, picks, arrived=None):
    rows, tokens = left.shape
    n = right.shape[2]
    count = picks.shape[0]

    def kernel(picks_ref, a_ref, b_ref, *refs):
        y = dot_nn(a_ref[...], b_ref[0])
        if arrived is not None:
            y = y + refs[0][0].astype(f32)
        refs[-1][0] = y.astype(bf16)

    block = pl.BlockSpec((1, rows, n), lambda j, picks: (j, 0, 0))
    return pl.pallas_call(
        kernel,
        grid_spec=pltpu.PrefetchScalarGridSpec(
            num_scalar_prefetch=1,
            grid=(count,),
            in_specs=[
                pl.BlockSpec((rows, tokens), lambda j, picks: (0, 0)),
                pl.BlockSpec((1, tokens, n), lambda j, picks: (picks[j], 0, 0)),
            ]
            + ([block] if arrived is not None else []),
            out_specs=block,
        ),
        out_shape=jax.ShapeDtypeStruct((count, rows, n), bf16),
        compiler_params=params(),
        cost_estimate=cost(2 * count * rows * tokens * n, 2 * count * rows * n),
        name="wgrad",
    )(picks, left, right, *(() if arrived is None else (arrived,)))


MESH = pl.DeviceIdType.MESH


def far_first(k, z, nz):
    low = z < nz // 2
    me = jnp.where(low, z, nz - 1 - z)
    got = jnp.where(k < nz - 1 - me, nz - 1 - k, jnp.where(k == nz - 1, me, nz - 2 - k))
    return jnp.where(low, got, nz - 1 - got)


def summed_grads(grid, collective_id, operands, unit, shape, cut, name):
    rows, n = shape
    ra, rb = cut, rows - cut
    nz = grid.nz
    count = len(operands)

    def kernel(*refs):
        ins, out = refs[:count], refs[count]
        (sa, sb, ga, gb, oa, ob, xa, yb, ta, tb, ya, xb, la, lb, za, zb, ua, ub, da, db, ss, rs, zr) = refs[count + 1 :]
        d, c = lax.axis_index("dp"), lax.axis_index("ctx")
        z, y = d // grid.ny, d % grid.ny
        x, core = c // 2, c % 2
        at_sib = (d, c + 1 - 2 * core)
        at_x = (d, (1 - x) * 2 + core)
        at_y = (z * grid.ny + 1 - y, c)
        at_up = ((z + 1) * grid.ny + y, c)
        at_down = ((z - 1) * grid.ny + y, c)
        has_up, has_down = z < nz - 1, z > 0

        barrier = pltpu.get_barrier_semaphore()
        for target in (at_sib, at_x, at_y):
            pl.semaphore_signal(barrier, inc=1, device_id=target, device_id_type=MESH)

        @pl.when(has_up)
        def _():
            pl.semaphore_signal(barrier, inc=1, device_id=at_up, device_id_type=MESH)

        @pl.when(has_down)
        def _():
            pl.semaphore_signal(barrier, inc=1, device_id=at_down, device_id_type=MESH)

        pl.semaphore_wait(barrier, 3 + has_up.astype(jnp.int32) + has_down.astype(jnp.int32))

        def copy(src, dst, kind, k, target):
            return pltpu.make_async_remote_copy(
                src_ref=src,
                dst_ref=dst,
                send_sem=ss.at[kind, k],
                recv_sem=rs.at[kind, k],
                device_id=target,
                device_id_type=MESH,
            )

        def sib(k):
            s = k % 2
            return copy(sa.at[s], ga.at[k], 0, k, at_sib), copy(sb.at[s], gb.at[k], 1, k, at_sib)

        def first(k):
            s = k % 2
            return (
                copy(oa.at[s, 1 - x], xa.at[k], 2, k, at_x),
                copy(ob.at[s, 1 - y], yb.at[k], 3, k, at_y),
            )

        def second(k):
            s = k % 2
            return copy(ta.at[s], ya.at[k], 4, k, at_y), copy(tb.at[s], xb.at[k], 5, k, at_x)

        def line(k, to, up):
            dst = (ua, ub) if up else (da, db)
            target = at_up if up else at_down
            way = 0 if up else 1
            return [
                pltpu.make_async_remote_copy(
                    src_ref=(za, zb)[h].at[k],
                    dst_ref=dst[h].at[to],
                    send_sem=ss.at[6 + h, k],
                    recv_sem=zr.at[way, h, to],
                    device_id=target,
                    device_id_type=MESH,
                )
                for h in range(2)
            ]

        def step(t, _):
            @pl.when(t < nz)
            def _():
                k, s = t, t % 2
                to = far_first(k, z, nz)

                @pl.when(k >= 2)
                def _():
                    for cp in sib(k - 2):
                        cp.wait_send()
                    for cp in first(k - 2):
                        cp.wait_send()

                def store_sib(y_to, x_to, value):
                    sa[s, x_to, y_to] = value[:ra].astype(bf16)
                    sb[s, y_to, x_to] = value[ra:].astype(bf16)

                unit(ins, 1 - core, to, store_sib)
                for cp in sib(k):
                    cp.start()
                waits = sib(k)
                done = []

                def store_own(y_to, x_to, value):
                    if not done:
                        done.append(True)
                        for cp in waits:
                            cp.wait_recv()
                    oa[s, x_to, y_to] = (value[:ra] + ga[k, x_to, y_to].astype(f32)).astype(bf16)
                    ob[s, y_to, x_to] = (value[ra:] + gb[k, y_to, x_to].astype(f32)).astype(bf16)

                unit(ins, core, to, store_own)
                for cp in first(k):
                    cp.start()

            @pl.when((t >= 1) & (t <= nz))
            def _():
                k, s = t - 1, (t - 1) % 2

                @pl.when(k >= 2)
                def _():
                    for cp in second(k - 2):
                        cp.wait_send()

                one, two = first(k)
                one.wait_recv()
                ta[s] = (oa[s, x, 1 - y].astype(f32) + xa[k, 1 - y].astype(f32)).astype(bf16)
                go_a, go_b = second(k)
                go_a.start()
                la[s] = oa[s, x, y].astype(f32) + xa[k, y].astype(f32)
                two.wait_recv()
                tb[s] = (ob[s, y, 1 - x].astype(f32) + yb[k, 1 - x].astype(f32)).astype(bf16)
                go_b.start()
                lb[s] = ob[s, y, x].astype(f32) + yb[k, x].astype(f32)

            @pl.when(t >= 2)
            def _():
                k, s = t - 2, t % 2
                to = far_first(k, z, nz)
                one, two = second(k)
                one.wait_recv()
                two.wait_recv()
                la[s] = la[s] + ya[k].astype(f32)
                lb[s] = lb[s] + xb[k].astype(f32)
                for up in (True, False):
                    behind = has_down if up else has_up

                    @pl.when(((to > z) if up else (to < z)) & behind)
                    def _():
                        for cp in line(k, to, up):
                            cp.wait_recv()
                        la[s] = la[s] + (ua, da)[0 if up else 1][to].astype(f32)
                        lb[s] = lb[s] + (ub, db)[0 if up else 1][to].astype(f32)

                    @pl.when((to > z) if up else (to < z))
                    def _():
                        za[k] = la[s].astype(bf16)
                        zb[k] = lb[s].astype(bf16)
                        for cp in line(k, to, up):
                            cp.start()

            return 0

        lax.fori_loop(0, nz + 2, step, 0)
        last = (nz - 1) % 2
        for up in (True, False):

            @pl.when(has_down if up else has_up)
            def _():
                for cp in line(nz - 1, z, up):
                    cp.wait_recv()
                la[last] = la[last] + (ua, da)[0 if up else 1][z].astype(f32)
                lb[last] = lb[last] + (ub, db)[0 if up else 1][z].astype(f32)

        out[:ra] = la[last]
        out[ra:] = lb[last]
        for k in range(nz - 2, nz):
            for cp in (*sib(k), *first(k), *second(k)):
                cp.wait_send()
        for k in range(nz - 1):
            for cp in line(k, 0, True):
                cp.wait_send()

    def vm(*dims, dtype=bf16):
        return pltpu.VMEM(dims, dtype)

    halves = [
        *(vm(2, 2, 2, h, n) for h in (ra, rb)),
        *(vm(nz, 2, 2, h, n) for h in (ra, rb)),
        *(vm(2, 2, 2, h, n) for h in (ra, rb)),
        *(vm(nz, 2, h, n) for h in (ra, rb)),
        *(vm(2, h, n) for h in (ra, rb)),
        *(vm(nz, h, n) for h in (ra, rb)),
        *(vm(2, h, n, dtype=f32) for h in (ra, rb)),
        *(vm(nz, h, n) for h in (ra, rb)),
        *(vm(nz, h, n) for h in (ra, rb)),
        *(vm(nz, h, n) for h in (ra, rb)),
    ]
    flops = sum(2 * 2 * 2 * nz * grid.ny * rows * n * 512 for _ in range(1))
    return pl.pallas_call(
        kernel,
        out_shape=jax.ShapeDtypeStruct((rows, n), f32),
        in_specs=[pl.BlockSpec(memory_space=pltpu.VMEM)] * count,
        out_specs=pl.BlockSpec(memory_space=pltpu.VMEM),
        scratch_shapes=[
            *halves,
            pltpu.SemaphoreType.DMA((8, nz)),
            pltpu.SemaphoreType.DMA((6, nz)),
            pltpu.SemaphoreType.DMA((2, 2, nz)),
        ],
        compiler_params=pltpu.CompilerParams(
            collective_id=collective_id, has_side_effects=True, vmem_limit_bytes=VMEM_LIMIT
        ),
        cost_estimate=cost(flops, 100_000_000),
        name=name,
    )(*operands)


def pick(array, index, axis):
    return lax.dynamic_index_in_dim(array, index, axis, keepdims=False)


def add_low(first, second):
    return (first.astype(f32) + second.astype(f32)).astype(bf16)


class Grid:
    def __init__(self, dp, ctx):
        self.dp, self.ctx = dp, ctx
        self.nx = max(ctx // 2, 1)
        self.ny = self.nx
        self.nz = dp // self.ny
        self.paired = self.nx == 2 and ctx == 4 and dp % 2 == 0

    def place(self):
        d, c = lax.axis_index("dp"), lax.axis_index("ctx")
        self.d, self.c = d, c
        self.z, self.y = d // self.ny, d % self.ny
        self.x, self.core = c // 2, c % 2

    def swap_core(self, v):
        return lax.ppermute(v, "ctx", [(i, i ^ 1) for i in range(self.ctx)])


def on_device(grid, *args):
    (
        layer_input,
        grad_out,
        segment_ids,
        qkv_weight,
        q_bias,
        v_bias,
        out_weight,
        out_bias,
        fc_weight,
        fc_bias,
        proj_weight,
        proj_bias,
        ln1_gain,
        ln1_bias,
        ln2_gain,
        ln2_bias,
    ) = args
    seqs, rows, width = layer_input.shape
    tokens = seqs * rows
    parts, groups = grid.dp, grid.ctx
    both = ("dp", "ctx")
    grid.place()

    vectors = (q_bias, v_bias, out_bias, proj_bias, ln1_gain, ln1_bias, ln2_gain, ln2_bias, fc_bias)
    sizes = [v.shape[0] for v in vectors]
    packed = lax.all_gather(jnp.concatenate(vectors), "dp", axis=0)
    spread, at = [], 0
    for size in sizes:
        spread.append(packed[:, at : at + size].astype(f32))
        at += size
    q_all, v_all, ob_all, pb_all, g1, b1, g2, b2 = [v.reshape(-1) for v in spread[:8]]
    fcb = spread[8][:, None, :]

    def gather(block, axes):
        return lax.all_gather(block, axes, axis=0)

    n_qkv, n_out, n_fc = qkv_weight.shape[1], out_weight.shape[1], fc_weight.shape[1]
    slab, hidden_slab = qkv_weight.shape[0], proj_weight.shape[0]
    w_qkv = gather(qkv_weight, both).reshape(parts, width, n_qkv)
    w_out = gather(out_weight, both).reshape(parts, width, n_out)
    w_fc = gather(fc_weight, both).reshape(parts, width, n_fc)
    w_proj = gather(proj_weight.T, ("ctx", "dp")).reshape(groups, width, hidden_slab)
    out_full = w_out.transpose(1, 0, 2).reshape(width, width)

    values = layer_input.reshape(tokens, width).astype(f32)
    normed1 = layer_norm(values, g1, b1).astype(bf16)
    joined = jnp.concatenate([q_all, jnp.zeros((width,), f32), v_all]).reshape(parts, 1, n_qkv)
    queries, key_rows, value_rows = qkv_project(normed1, w_qkv, joined)
    queries = queries.reshape(seqs, rows, width)
    own = jnp.stack([key_rows, value_rows]).reshape(2, seqs, rows, width)
    if grid.paired:
        other = lax.ppermute(own, "ctx", [(0, 2), (1, 3)])
        column = jnp.where(grid.x == 0, jnp.stack([own, own]), jnp.stack([other, own]))
        sibling = grid.swap_core(column)
        even = jnp.where(grid.core == 0, column, sibling)
        odd = jnp.where(grid.core == 0, sibling, column)
        pairs_full = jnp.stack([even, odd], axis=1).reshape(groups, 2, seqs, rows, width)
    else:
        pairs_full = lax.all_gather(own, "ctx", axis=0)

    seg_blocks = segment_ids.reshape(seqs, groups, rows)
    seg_mine = pick(seg_blocks, grid.c, 1)
    needed = seg_blocks[:, :, -1] >= seg_mine[:, :1]
    start = jnp.minimum(jnp.argmax(needed, axis=1).astype(jnp.int32), grid.c)
    bounds = jnp.concatenate([grid.c[None].astype(jnp.int32), start])
    attended, attended_f32, log_total = attention_forward(
        bounds, queries, pairs_full, seg_mine[:, :, None], seg_blocks[:, :, None, :]
    )
    attended = attended.reshape(tokens, width)
    hidden = values + jnp.dot(attended, out_full, preferred_element_type=f32) + ob_all
    normed2 = layer_norm(hidden, g2, b2).astype(bf16)
    inner, activated = feed_in(normed2, w_fc, fcb, groups)
    output = feed_out(activated, w_proj, hidden, pb_all[None])

    mlp_grad = grad_out.reshape(tokens, width)
    cotangent = mlp_grad.astype(f32)
    proj_bias_grad = jnp.sum(cotangent, axis=0)
    inner_grad, fc_bias_grad = feed_back(mlp_grad, w_proj, inner, parts)

    def tall_cut(size):
        return (size // 2 + 15) // 16 * 16

    def by_columns(refs, core, z, store):
        for y_to in range(2):
            for x_to in range(2):
                at = pl.ds(pl.multiple_of((2 * x_to + core) * slab, 16), slab)
                terms = [
                    dot_nn(left[at, :], right[z * grid.ny + y_to])
                    for left, right in zip(refs[::2], refs[1::2])
                ]
                store(y_to, x_to, jnp.concatenate(terms, axis=1) if len(terms) > 1 else terms[0])

    def by_rows(refs, core, z, store):
        left, right = refs
        cols = width // parts
        at = pl.ds(pl.multiple_of(z * (grid.ny * cols), 16), grid.ny * cols)
        for x_to in range(2):
            term = dot_nn(left[at, :], right[2 * x_to + core])
            for y_to in range(2):
                store(y_to, x_to, term[y_to * cols : (y_to + 1) * cols])

    def reduced(pairs, collective_id, name):
        if not grid.paired:
            everything = jnp.arange(parts, dtype=jnp.int32)
            results = []
            for left, right in pairs:
                whole = weight_grad(left.T, right, everything)
                whole = whole.reshape(parts * groups, slab, right.shape[2])
                results.append(lax.psum_scatter(whole, both, scatter_dimension=0).astype(f32))
            return results
        operands, ends = [], [0]
        for left, right in pairs:
            n = right.shape[2]
            full = n if len(ends) == len(pairs) else pl.cdiv(n, LANES) * LANES
            operands += [left.T, jnp.pad(right, ((0, 0), (0, 0), (0, full - n)))]
            ends.append(ends[-1] + full)
        total = summed_grads(
            grid, collective_id, operands, by_columns, (slab, ends[-1]), tall_cut(slab), name
        )
        return [total[:, at : at + pair[1].shape[2]] for at, pair in zip(ends, pairs)]

    def reduced_proj(left, right):
        f = right.shape[2]
        cols = width // parts
        if not grid.paired:
            whole = weight_grad(left.T, right, jnp.arange(groups, dtype=jnp.int32))
            whole = whole.reshape(groups * parts, cols, f)
            return lax.psum_scatter(whole, ("ctx", "dp"), scatter_dimension=0).astype(f32)
        return summed_grads(grid, 1, [left.T, right], by_rows, (cols, f), tall_cut(cols), "rs_proj")

    proj_weight_grad = reduced_proj(mlp_grad, activated).T
    (fc_weight_grad,) = reduced([(normed2, inner_grad)], 2, "rs_fc")

    normed2_grad = back_project(inner_grad, w_fc)
    norm2_out, norm2_pull = jax.vjp(layer_norm, hidden, g2, b2)
    hidden_ln, g2_grad, b2_grad = norm2_pull(normed2_grad)
    hidden_grad = cotangent + hidden_ln
    branch_grad = hidden_grad.astype(bf16)
    out_bias_grad = jnp.sum(branch_grad, axis=0, dtype=f32)
    attended_grad = jnp.einsum(
        "nd,ed->ne", branch_grad, out_full, preferred_element_type=f32
    ).astype(bf16)
    branch_parts = branch_grad.reshape(tokens, parts, n_out).transpose(1, 0, 2)

    query_grad, pairs_grad = attention_backward(
        bounds,
        queries,
        pairs_full,
        seg_blocks[:, :, :, None],
        seg_mine[:, None, :],
        attended_grad.reshape(seqs, rows, width),
        attended_f32,
        log_total,
    )
    if grid.paired:
        by_chip = pairs_grad.reshape(2, 2, 2, seqs, rows, width)
        plane = add_low(
            pick(by_chip, grid.core, 1), grid.swap_core(pick(by_chip, 1 - grid.core, 1))
        )
        came = lax.ppermute(plane[0], "ctx", [(2, 0), (3, 1)])
        pair_grad = add_low(pick(plane, grid.x, 0), came)
    else:
        pair_grad = lax.psum_scatter(pairs_grad, "ctx", scatter_dimension=0)
    pair_grad = pair_grad.reshape(2, tokens, width)
    projected_grad = jnp.concatenate(
        [query_grad.reshape(tokens, width), pair_grad[0], pair_grad[1]], axis=1
    )
    q_bias_grad = jnp.sum(query_grad.reshape(tokens, width), axis=0, dtype=f32)
    v_bias_grad = jnp.sum(pair_grad[1], axis=0, dtype=f32)
    by_part = projected_grad.reshape(tokens, parts, n_qkv).transpose(1, 0, 2)
    out_weight_grad, qkv_weight_grad = reduced(
        [(attended, branch_parts), (normed1, by_part)], 3, "rs_qkv"
    )
    normed1_grad = back_project(by_part, w_qkv)
    norm1_out, norm1_pull = jax.vjp(layer_norm, values, g1, b1)
    values_ln, g1_grad, b1_grad = norm1_pull(normed1_grad)
    input_grad = hidden_grad + values_ln

    sums = [q_bias_grad, v_bias_grad, out_bias_grad, proj_bias_grad, g1_grad, b1_grad, g2_grad, b2_grad]
    stacked = jnp.concatenate(
        [v.reshape(parts, -1) for v in sums] + [fc_bias_grad.reshape(parts, -1)], axis=1
    )
    total = pick(lax.psum(stacked, both), grid.d, 0)
    vec, at = [], 0
    for size in sizes:
        vec.append(total[at : at + size])
        at += size
    return (
        output.reshape(seqs, rows, width),
        input_grad.reshape(seqs, rows, width),
        qkv_weight_grad,
        vec[0],
        vec[1],
        out_weight_grad,
        vec[2],
        fc_weight_grad,
        vec[8],
        proj_weight_grad,
        vec[3],
        vec[4],
        vec[5],
        vec[6],
        vec[7],
    )


def solution(mesh):
    rows3, mat, vec = P("dp", "ctx", None), P("ctx", "dp"), P("dp")
    grid = Grid(mesh.shape["dp"], mesh.shape["ctx"])
    return jax.shard_map(
        functools.partial(on_device, grid),
        mesh=mesh,
        in_specs=(
            rows3,
            rows3,
            P("dp", None),
            mat,
            vec,
            vec,
            mat,
            vec,
            mat,
            vec,
            mat,
            vec,
            vec,
            vec,
            vec,
            vec,
        ),
        out_specs=(
            rows3,
            rows3,
            mat,
            vec,
            vec,
            mat,
            vec,
            mat,
            vec,
            mat,
            vec,
            vec,
            vec,
            vec,
            vec,
        ),
        check_vma=False,
    )
```

```python
import functools

import jax
import jax.numpy as jnp
from jax import lax
from jax.experimental import pallas as pl
from jax.experimental.pallas import tpu as pltpu
from jax.sharding import PartitionSpec as P

HEADS = 25
HEAD_DIM = 64
LANES = 128
EPS = 1e-05
NEG_FILL = -1e30
GELU_C = 0.7978845608028654
GELU_A = 0.044715

bf16 = jnp.bfloat16
f32 = jnp.float32
VMEM_LIMIT = 58 * 1024 * 1024


def layer_norm(values, gain, shift):
    center = values - jnp.mean(values, axis=-1, keepdims=True)
    factor = lax.rsqrt(jnp.mean(center * center, axis=-1, keepdims=True) + EPS)
    return center * factor * gain + shift


def dot_nn(a, b):
    return lax.dot_general(a, b, (((1,), (0,)), ((), ())), preferred_element_type=f32)


def dot_nt(a, b):
    return lax.dot_general(a, b, (((1,), (1,)), ((), ())), preferred_element_type=f32)


def dot_tn(a, b):
    return lax.dot_general(a, b, (((0,), (0,)), ((), ())), preferred_element_type=f32)


def params(n_axes=1):
    return pltpu.CompilerParams(
        dimension_semantics=("arbitrary",) * n_axes, vmem_limit_bytes=VMEM_LIMIT
    )


def cost(flops, read, transcendentals=0):
    return pl.CostEstimate(
        flops=int(flops), bytes_accessed=int(read), transcendentals=int(transcendentals)
    )


def qkv_project(normed, weight, bias):
    tokens, width = normed.shape
    parts, _, n = weight.shape

    def kernel(x_ref, w_ref, b_ref, *out_refs):
        part = pl.program_id(0)
        y = (dot_nn(x_ref[...], w_ref[0]) + b_ref[0]).astype(bf16)
        for d in range(parts):

            @pl.when(part == d)
            def _():
                first, last = d * n, (d + 1) * n
                for g in range(3):
                    lo, hi = max(first, g * width), min(last, (g + 1) * width)
                    if lo < hi:
                        out_refs[g][:, lo - g * width : hi - g * width] = y[
                            :, lo - first : hi - first
                        ]

    whole = pl.BlockSpec((tokens, width), lambda d: (0, 0))
    return pl.pallas_call(
        kernel,
        grid=(parts,),
        in_specs=[
            whole,
            pl.BlockSpec((1, width, n), lambda d: (d, 0, 0)),
            pl.BlockSpec((1, 1, n), lambda d: (d, 0, 0)),
        ],
        out_specs=[whole] * 3,
        out_shape=[jax.ShapeDtypeStruct((tokens, width), bf16)] * 3,
        compiler_params=params(),
        cost_estimate=cost(2 * tokens * width * parts * n, 2 * width * parts * n),
        name="qkv",
    )(normed, weight, bias)


def pair_masks(pair, width):
    lane = lax.broadcasted_iota(jnp.int32, (1, LANES), 1)
    inside = lane + pair * LANES < width
    return inside & (lane < HEAD_DIM), inside & (lane >= HEAD_DIM), inside


def attention_forward(bounds, queries, pairs_full, seg_col, seg_row):
    seqs, rows, width = queries.shape
    blocks = pairs_full.shape[0]
    pairs = pl.cdiv(width, LANES)

    def kernel(bounds_ref, q_ref, kv_ref, sc_ref, sr_ref, o_ref, of_ref, lse_ref):
        seq, pair = pl.program_id(0), pl.program_id(1)
        mine, start = bounds_ref[0], bounds_ref[1 + seq]
        low, high, inside = pair_masks(pair, width)
        scaled = q_ref[0] * jnp.asarray(0.125, bf16)
        q_heads = (
            jnp.where(low, scaled, jnp.zeros_like(scaled)),
            jnp.where(high, scaled, jnp.zeros_like(scaled)),
        )
        seg_q = sc_ref[0]

        def block(j, diagonal, carry):
            k = jnp.where(inside, kv_ref[j, 0, 0], jnp.zeros((rows, LANES), bf16))
            v = jnp.where(inside, kv_ref[j, 1, 0], jnp.zeros((rows, LANES), bf16))
            allowed = sr_ref[0, j] == seg_q
            if diagonal:
                at_row = lax.broadcasted_iota(jnp.int32, (rows, rows), 0)
                at_col = lax.broadcasted_iota(jnp.int32, (rows, rows), 1)
                allowed = allowed & (at_col <= at_row)
            out = []
            for head in range(2):
                s = jnp.where(allowed, dot_nt(q_heads[head], k), NEG_FILL)
                top = jnp.max(s, axis=1, keepdims=True)
                if carry is None:
                    p = jnp.exp(s - top)
                    out += [top, jnp.sum(p, axis=1, keepdims=True), dot_nn(p.astype(bf16), v)]
                else:
                    m, l, acc = carry[3 * head : 3 * head + 3]
                    new = jnp.maximum(m, top)
                    scale = jnp.exp(m - new)
                    p = jnp.exp(s - new)
                    out += [
                        new,
                        l * scale + jnp.sum(p, axis=1, keepdims=True),
                        acc * scale + dot_nn(p.astype(bf16), v),
                    ]
            return tuple(out)

        carry = block(mine, True, None)
        carry = lax.fori_loop(start, mine, lambda j, c: block(j, False, c), carry)
        m0, l0, a0, m1, l1, a1 = carry
        result = jnp.where(low, a0 / l0, a1 / l1)
        o_ref[0] = result.astype(bf16)
        of_ref[0] = result
        lse_ref[0] = jnp.where(low, m0 + jnp.log(l0), m1 + jnp.log(l1))

    tile = pl.BlockSpec((1, rows, LANES), lambda s, p, b: (s, 0, p))
    return pl.pallas_call(
        kernel,
        grid_spec=pltpu.PrefetchScalarGridSpec(
            num_scalar_prefetch=1,
            grid=(seqs, pairs),
            in_specs=[
                tile,
                pl.BlockSpec((blocks, 2, 1, rows, LANES), lambda s, p, b: (0, 0, s, 0, p)),
                pl.BlockSpec((1, rows, 1), lambda s, p, b: (s, 0, 0)),
                pl.BlockSpec((1, blocks, 1, rows), lambda s, p, b: (s, 0, 0, 0)),
            ],
            out_specs=[tile, tile, tile],
        ),
        out_shape=[
            jax.ShapeDtypeStruct((seqs, rows, width), bf16),
            jax.ShapeDtypeStruct((seqs, rows, width), f32),
            jax.ShapeDtypeStruct((seqs, rows, width), f32),
        ],
        compiler_params=params(2),
        cost_estimate=cost(
            4 * seqs * rows * rows * blocks * width, 4 * seqs * rows * blocks * width
        ),
        name="attn_fwd",
    )(bounds, queries, pairs_full, seg_col, seg_row)


def attention_backward(
    bounds, queries, pairs_full, seg_col, seg_row, out_grad, out_full, log_total
):
    seqs, rows, width = queries.shape
    blocks = pairs_full.shape[0]
    pairs = pl.cdiv(width, LANES)

    def kernel(bounds_ref, q_ref, kv_ref, sc_ref, sr_ref, g_ref, of_ref, lse_ref, dq_ref, dkv_ref):
        seq, pair = pl.program_id(0), pl.program_id(1)
        mine, start = bounds_ref[0], bounds_ref[1 + seq]
        low, high, inside = pair_masks(pair, width)
        zero = jnp.zeros((rows, LANES), bf16)
        scaled = q_ref[0] * jnp.asarray(0.125, bf16)
        grad = g_ref[0]
        q_heads = (jnp.where(low, scaled, zero), jnp.where(high, scaled, zero))
        g_heads = (jnp.where(low, grad, zero), jnp.where(high, grad, zero))
        product = jnp.where(inside, grad.astype(f32) * of_ref[0], 0.0)
        lse = jnp.where(inside, lse_ref[0], 0.0)
        product_t = product.T
        lse_t = lse.T
        delta = (
            jnp.sum(product_t[:HEAD_DIM], axis=0, keepdims=True),
            jnp.sum(product_t[HEAD_DIM:], axis=0, keepdims=True),
        )
        log_row = (lse_t[0:1], lse_t[HEAD_DIM : HEAD_DIM + 1])
        seg_q = sr_ref[0]
        dkv_ref[...] = jnp.zeros_like(dkv_ref)

        def block(j, diagonal, total):
            k = jnp.where(inside, kv_ref[j, 0, 0], zero)
            v = jnp.where(inside, kv_ref[j, 1, 0], zero)
            allowed = sc_ref[0, j] == seg_q
            if diagonal:
                at_key = lax.broadcasted_iota(jnp.int32, (rows, rows), 0)
                at_query = lax.broadcasted_iota(jnp.int32, (rows, rows), 1)
                allowed = allowed & (at_key <= at_query)
            key_grad, value_grad = None, None
            for head in range(2):
                k_head = jnp.where((low, high)[head], k, zero)
                s = jnp.where(allowed, dot_nt(k, q_heads[head]), NEG_FILL)
                p = jnp.exp(s - log_row[head])
                pushed = dot_nt(v, g_heads[head])
                ds = (p * (pushed - delta[head])).astype(bf16)
                dv = dot_nn(p.astype(bf16), g_heads[head])
                dk = dot_nn(ds, q_heads[head])
                dq = dot_tn(ds, k_head)
                key_grad = dk if key_grad is None else key_grad + dk
                value_grad = dv if value_grad is None else value_grad + dv
                total = dq if total is None else total + dq
            dkv_ref[j, 0, 0] = key_grad.astype(bf16)
            dkv_ref[j, 1, 0] = value_grad.astype(bf16)
            return total

        total = block(mine, True, None)
        total = lax.fori_loop(start, mine, lambda j, c: block(j, False, c), total)
        dq_ref[0] = (total * 0.125).astype(bf16)

    tile = pl.BlockSpec((1, rows, LANES), lambda s, p, b: (s, 0, p))
    many = pl.BlockSpec((blocks, 2, 1, rows, LANES), lambda s, p, b: (0, 0, s, 0, p))
    return pl.pallas_call(
        kernel,
        grid_spec=pltpu.PrefetchScalarGridSpec(
            num_scalar_prefetch=1,
            grid=(seqs, pairs),
            in_specs=[
                tile,
                many,
                pl.BlockSpec((1, blocks, rows, 1), lambda s, p, b: (s, 0, 0, 0)),
                pl.BlockSpec((1, 1, rows), lambda s, p, b: (s, 0, 0)),
                tile,
                tile,
                tile,
            ],
            out_specs=[tile, many],
        ),
        out_shape=[
            jax.ShapeDtypeStruct((seqs, rows, width), bf16),
            jax.ShapeDtypeStruct(pairs_full.shape, bf16),
        ],
        compiler_params=params(2),
        cost_estimate=cost(
            10 * seqs * rows * rows * blocks * width, 8 * seqs * rows * blocks * width
        ),
        name="attn_bwd",
    )(bounds, queries, pairs_full, seg_col, seg_row, out_grad, out_full, log_total)


def causal(rows, transposed=False):
    first = lax.broadcasted_iota(jnp.int32, (rows, rows), 0)
    second = lax.broadcasted_iota(jnp.int32, (rows, rows), 1)
    return first <= second if transposed else second <= first


def pair_forward(extra, q, k, v, sk, sv, seg_q, seg_k, seg_sk, masks):
    low, high, inside = masks
    rows = q(0).shape[0]
    zero = jnp.zeros((rows, LANES), bf16)
    tri = causal(rows)

    def heads_of(value):
        scaled = value * jnp.asarray(0.125, bf16)
        return jnp.where(low, scaled, zero), jnp.where(high, scaled, zero)

    def clean(value):
        return jnp.where(inside, value, zero)

    def unit(q_heads, keys, values, allowed, state):
        out = []
        for head in range(2):
            s = jnp.where(allowed, dot_nt(q_heads[head], keys), NEG_FILL)
            top = jnp.max(s, axis=1, keepdims=True)
            if state is None:
                p = jnp.exp(s - top)
                out.append((top, jnp.sum(p, axis=1, keepdims=True), dot_nn(p.astype(bf16), values)))
            else:
                m, l, acc = state[head]
                new = jnp.maximum(m, top)
                scale = jnp.exp(m - new)
                p = jnp.exp(s - new)
                out.append(
                    (
                        new,
                        l * scale + jnp.sum(p, axis=1, keepdims=True),
                        acc * scale + dot_nn(p.astype(bf16), values),
                    )
                )
        return out

    more = unit(
        heads_of(q(extra)), clean(sk(extra)), clean(sv(extra)), seg_sk(extra) == seg_q(extra), None
    )
    results = []
    for slot in range(2):
        here = extra == slot
        state = [
            (jnp.where(here, m, NEG_FILL), jnp.where(here, l, 0.0), jnp.where(here, acc, 0.0))
            for m, l, acc in more
        ]
        q_heads = heads_of(q(slot))
        state = unit(
            q_heads, clean(k(slot)), clean(v(slot)), (seg_k(slot) == seg_q(slot)) & tri, state
        )
        if slot == 1:
            state = unit(q_heads, clean(k(0)), clean(v(0)), seg_k(0) == seg_q(1), state)
            state = unit(q_heads, clean(sk(0)), clean(sv(0)), seg_sk(0) == seg_q(1), state)
        (m0, l0, a0), (m1, l1, a1) = state
        results.append(
            (jnp.where(low, a0 / l0, a1 / l1), jnp.where(low, m0 + jnp.log(l0), m1 + jnp.log(l1)))
        )
    return results


def pair_backward(extra, q, k, v, sk, sv, g, o, lse, seg_q, seg_k, seg_sk, masks):
    low, high, inside = masks
    rows = q(0).shape[0]
    zero = jnp.zeros((rows, LANES), bf16)
    tri = causal(rows, transposed=True)

    def halves(value):
        return jnp.where(low, value, zero), jnp.where(high, value, zero)

    def queries(slot):
        grad = g(slot)
        product = jnp.where(inside, grad.astype(f32) * o(slot), 0.0).T
        sums = jnp.where(inside, lse(slot), 0.0).T
        return (
            halves(q(slot) * jnp.asarray(0.125, bf16)),
            halves(grad),
            (
                jnp.sum(product[:HEAD_DIM], axis=0, keepdims=True),
                jnp.sum(product[HEAD_DIM:], axis=0, keepdims=True),
            ),
            (sums[0:1], sums[HEAD_DIM : HEAD_DIM + 1]),
        )

    def unit(side, keys, values, allowed):
        q_heads, g_heads, delta, logs = side
        keys, values = jnp.where(inside, keys, zero), jnp.where(inside, values, zero)
        k_heads = halves(keys)
        dq = dk = dv = None
        for head in range(2):
            s = jnp.where(allowed, dot_nt(keys, q_heads[head]), NEG_FILL)
            p = jnp.exp(s - logs[head])
            ds = (p * (dot_nt(values, g_heads[head]) - delta[head])).astype(bf16)
            terms = (
                dot_tn(ds, k_heads[head]),
                dot_nn(ds, q_heads[head]),
                dot_nn(p.astype(bf16), g_heads[head]),
            )
            dq, dk, dv = terms if dq is None else (dq + terms[0], dk + terms[1], dv + terms[2])
        return dq, dk, dv

    sides = [queries(0), queries(1)]
    first = unit(sides[0], k(0), v(0), (seg_k(0) == seg_q(0)) & tri)
    second = unit(sides[1], k(1), v(1), (seg_k(1) == seg_q(1)) & tri)
    third = unit(sides[1], k(0), v(0), seg_k(0) == seg_q(1))
    fourth = unit(sides[1], sk(0), sv(0), seg_sk(0) == seg_q(1))
    fifth = unit(queries(extra), sk(extra), sv(extra), seg_sk(extra) == seg_q(extra))
    at_one = extra == 1

    def when(flag, value):
        return jnp.where(flag, value, 0.0)

    dq0 = first[0] + when(~at_one, fifth[0])
    dq1 = second[0] + third[0] + fourth[0] + when(at_one, fifth[0])
    own = [(first[1] + third[1], first[2] + third[2]), second[1:]]
    other = [
        tuple(fourth[i] + when(~at_one, fifth[i]) for i in (1, 2)),
        tuple(when(at_one, fifth[i]) for i in (1, 2)),
    ]
    return (dq0 * 0.125, dq1 * 0.125), own, other


def chip_attention_back(extra, queries, keys, values, other, grad, out, logs, seg_q, seg_k, seg_sk):
    _, rows, width = grad.shape
    pairs = pl.cdiv(width, LANES)

    def kernel(
        extra_ref, q_ref, k_ref, v_ref, s_ref, g_ref, of_ref, lse_ref, rq_ref, ck_ref, cs_ref, dq_ref, own_ref, oth_ref
    ):
        masks = pair_masks(pl.program_id(0), width)
        dq, own, oth = pair_backward(
            extra_ref[0],
            lambda i: q_ref[i],
            lambda i: k_ref[i],
            lambda i: v_ref[i],
            lambda i: s_ref[0, i],
            lambda i: s_ref[1, i],
            lambda i: g_ref[i],
            lambda i: of_ref[i],
            lambda i: lse_ref[i],
            lambda i: rq_ref[i],
            lambda i: ck_ref[i],
            lambda i: cs_ref[i],
            masks,
        )
        for slot in range(2):
            dq_ref[slot] = dq[slot].astype(bf16)
            for kind in range(2):
                own_ref[kind, slot] = own[slot][kind]
                oth_ref[kind, slot] = oth[slot][kind].astype(bf16)

    tile = pl.BlockSpec((2, rows, LANES), lambda p, e: (0, 0, p))
    both = pl.BlockSpec((2, 2, rows, LANES), lambda p, e: (0, 0, 0, p))
    col = pl.BlockSpec((2, rows, 1), lambda p, e: (0, 0, 0))
    return pl.pallas_call(
        kernel,
        grid_spec=pltpu.PrefetchScalarGridSpec(
            num_scalar_prefetch=1,
            grid=(pairs,),
            in_specs=[
                tile,
                tile,
                tile,
                both,
                tile,
                tile,
                tile,
                pl.BlockSpec((2, 1, rows), lambda p, e: (0, 0, 0)),
                col,
                col,
            ],
            out_specs=[tile, both, both],
        ),
        out_shape=[
            jax.ShapeDtypeStruct((2, rows, width), bf16),
            jax.ShapeDtypeStruct((2, 2, rows, width), f32),
            jax.ShapeDtypeStruct((2, 2, rows, width), bf16),
        ],
        compiler_params=params(),
        cost_estimate=cost(100 * rows * rows * width, 60 * rows * width),
        name="chip_attn_back",
    )(extra, queries, keys, values, other, grad, out, logs, seg_q, seg_k, seg_sk)


def feed_in(normed, weight, bias, groups):
    tokens, width = normed.shape
    parts, _, n = weight.shape
    ratio = parts // groups

    def kernel(x_ref, w_ref, b_ref, inner_ref, act_ref):
        place = lax.rem(pl.program_id(0), ratio)
        u = dot_nn(x_ref[...], w_ref[0]) + b_ref[0]
        act = (0.5 * u * (1.0 + jnp.tanh(GELU_C * (u + GELU_A * u * u * u)))).astype(bf16)
        for r in range(ratio):

            @pl.when(place == r)
            def _():
                inner_ref[0, :, r * n : (r + 1) * n] = u
                act_ref[0, :, r * n : (r + 1) * n] = act

    out = pl.BlockSpec((1, tokens, ratio * n), lambda d: (d // ratio, 0, 0))
    return pl.pallas_call(
        kernel,
        grid=(parts,),
        in_specs=[
            pl.BlockSpec((tokens, width), lambda d: (0, 0)),
            pl.BlockSpec((1, width, n), lambda d: (d, 0, 0)),
            pl.BlockSpec((1, 1, n), lambda d: (d, 0, 0)),
        ],
        out_specs=[out, out],
        out_shape=[
            jax.ShapeDtypeStruct((groups, tokens, ratio * n), f32),
            jax.ShapeDtypeStruct((groups, tokens, ratio * n), bf16),
        ],
        compiler_params=params(),
        cost_estimate=cost(2 * tokens * width * parts * n, 2 * width * parts * n),
        name="fc",
    )(normed, weight, bias)


def feed_out(act, weight, hidden, bias):
    groups, tokens, f = act.shape
    width = weight.shape[1]

    def kernel(a_ref, w_ref, h_ref, b_ref, o_ref, acc_ref):
        step = pl.program_id(0)

        @pl.when(step == 0)
        def _():
            acc_ref[...] = h_ref[...] + b_ref[...]

        acc_ref[...] += dot_nt(a_ref[0], w_ref[0])

        @pl.when(step == groups - 1)
        def _():
            o_ref[...] = acc_ref[...].astype(bf16)

    return pl.pallas_call(
        kernel,
        grid=(groups,),
        in_specs=[
            pl.BlockSpec((1, tokens, f), lambda c: (c, 0, 0)),
            pl.BlockSpec((1, width, f), lambda c: (c, 0, 0)),
            pl.BlockSpec((tokens, width), lambda c: (0, 0)),
            pl.BlockSpec((1, width), lambda c: (0, 0)),
        ],
        out_specs=pl.BlockSpec((tokens, width), lambda c: (0, 0)),
        out_shape=jax.ShapeDtypeStruct((tokens, width), bf16),
        scratch_shapes=[pltpu.VMEM((tokens, width), f32)],
        compiler_params=params(),
        cost_estimate=cost(2 * groups * tokens * width * f, 2 * groups * width * f),
        name="proj",
    )(act, weight, hidden, bias)


def feed_back(grad, weight, inner, parts):
    groups, tokens, f = inner.shape
    width = weight.shape[1]
    ratio = parts // groups
    n = f // ratio

    def kernel(g_ref, w_ref, u_ref, o_ref, s_ref):
        u = u_ref[0]
        t = jnp.tanh(GELU_C * (u + GELU_A * u * u * u))
        slope = 0.5 * (1.0 + t) + 0.5 * u * (1.0 - t * t) * (
            GELU_C * (1.0 + 3.0 * GELU_A * u * u)
        )
        out = (dot_nn(g_ref[...], w_ref[0]) * slope).astype(bf16)
        total = jnp.sum(out.astype(f32), axis=0, keepdims=True)
        for r in range(ratio):
            o_ref[r] = out[:, r * n : (r + 1) * n]
            s_ref[r] = total[:, r * n : (r + 1) * n]

    return pl.pallas_call(
        kernel,
        grid=(groups,),
        in_specs=[
            pl.BlockSpec((tokens, width), lambda c: (0, 0)),
            pl.BlockSpec((1, width, f), lambda c: (c, 0, 0)),
            pl.BlockSpec((1, tokens, f), lambda c: (c, 0, 0)),
        ],
        out_specs=[
            pl.BlockSpec((ratio, tokens, n), lambda c: (c, 0, 0)),
            pl.BlockSpec((ratio, 1, n), lambda c: (c, 0, 0)),
        ],
        out_shape=[
            jax.ShapeDtypeStruct((parts, tokens, n), bf16),
            jax.ShapeDtypeStruct((parts, 1, n), f32),
        ],
        compiler_params=params(),
        cost_estimate=cost(2 * groups * tokens * width * f, 6 * groups * width * f),
        name="act_bwd",
    )(grad, weight, inner)


def back_project(grads, weight):
    parts, tokens, n = grads.shape
    width = weight.shape[1]

    def kernel(g_ref, w_ref, o_ref):
        @pl.when(pl.program_id(0) == 0)
        def _():
            o_ref[...] = dot_nt(g_ref[0], w_ref[0])

        @pl.when(pl.program_id(0) > 0)
        def _():
            o_ref[...] += dot_nt(g_ref[0], w_ref[0])

    return pl.pallas_call(
        kernel,
        grid=(parts,),
        in_specs=[
            pl.BlockSpec((1, tokens, n), lambda d: (d, 0, 0)),
            pl.BlockSpec((1, width, n), lambda d: (d, 0, 0)),
        ],
        out_specs=pl.BlockSpec((tokens, width), lambda d: (0, 0)),
        out_shape=jax.ShapeDtypeStruct((tokens, width), f32),
        compiler_params=params(),
        cost_estimate=cost(2 * parts * tokens * width * n, 2 * parts * width * n),
        name="back",
    )(grads, weight)


def weight_grad(left, right, picks, arrived=None):
    rows, tokens = left.shape
    n = right.shape[2]
    count = picks.shape[0]

    def kernel(picks_ref, a_ref, b_ref, *refs):
        y = dot_nn(a_ref[...], b_ref[0])
        if arrived is not None:
            y = y + refs[0][0].astype(f32)
        refs[-1][0] = y.astype(bf16)

    block = pl.BlockSpec((1, rows, n), lambda j, picks: (j, 0, 0))
    return pl.pallas_call(
        kernel,
        grid_spec=pltpu.PrefetchScalarGridSpec(
            num_scalar_prefetch=1,
            grid=(count,),
            in_specs=[
                pl.BlockSpec((rows, tokens), lambda j, picks: (0, 0)),
                pl.BlockSpec((1, tokens, n), lambda j, picks: (picks[j], 0, 0)),
            ]
            + ([block] if arrived is not None else []),
            out_specs=block,
        ),
        out_shape=jax.ShapeDtypeStruct((count, rows, n), bf16),
        compiler_params=params(),
        cost_estimate=cost(2 * count * rows * tokens * n, 2 * count * rows * n),
        name="wgrad",
    )(picks, left, right, *(() if arrived is None else (arrived,)))


MESH = pl.DeviceIdType.MESH


def far_first(k, z, nz):
    low = z < nz // 2
    me = jnp.where(low, z, nz - 1 - z)
    got = jnp.where(k < nz - 1 - me, nz - 1 - k, jnp.where(k == nz - 1, me, nz - 2 - k))
    return jnp.where(low, got, nz - 1 - got)


def summed_grads(grid, collective_id, operands, unit, shape, cut, name):
    rows, n = shape
    ra, rb = cut, rows - cut
    nz = grid.nz
    count = len(operands)

    def kernel(*refs):
        ins, out = refs[:count], refs[count]
        (sa, sb, ga, gb, oa, ob, xa, yb, ta, tb, ya, xb, la, lb, za, zb, ua, ub, da, db, ss, rs, zr) = refs[count + 1 :]
        d, c = lax.axis_index("dp"), lax.axis_index("ctx")
        z, y = d // grid.ny, d % grid.ny
        x, core = c // 2, c % 2
        at_sib = (d, c + 1 - 2 * core)
        at_x = (d, (1 - x) * 2 + core)
        at_y = (z * grid.ny + 1 - y, c)
        at_up = ((z + 1) * grid.ny + y, c)
        at_down = ((z - 1) * grid.ny + y, c)
        has_up, has_down = z < nz - 1, z > 0

        barrier = pltpu.get_barrier_semaphore()
        for target in (at_sib, at_x, at_y):
            pl.semaphore_signal(barrier, inc=1, device_id=target, device_id_type=MESH)

        @pl.when(has_up)
        def _():
            pl.semaphore_signal(barrier, inc=1, device_id=at_up, device_id_type=MESH)

        @pl.when(has_down)
        def _():
            pl.semaphore_signal(barrier, inc=1, device_id=at_down, device_id_type=MESH)

        pl.semaphore_wait(barrier, 3 + has_up.astype(jnp.int32) + has_down.astype(jnp.int32))

        def copy(src, dst, kind, k, target):
            return pltpu.make_async_remote_copy(
                src_ref=src,
                dst_ref=dst,
                send_sem=ss.at[kind, k],
                recv_sem=rs.at[kind, k],
                device_id=target,
                device_id_type=MESH,
            )

        def sib(k):
            s = k % 2
            return copy(sa.at[s], ga.at[k], 0, k, at_sib), copy(sb.at[s], gb.at[k], 1, k, at_sib)

        def first(k):
            s = k % 2
            return (
                copy(oa.at[s, 1 - x], xa.at[k], 2, k, at_x),
                copy(ob.at[s, 1 - y], yb.at[k], 3, k, at_y),
            )

        def second(k):
            s = k % 2
            return copy(ta.at[s], ya.at[k], 4, k, at_y), copy(tb.at[s], xb.at[k], 5, k, at_x)

        def line(k, to, up):
            dst = (ua, ub) if up else (da, db)
            target = at_up if up else at_down
            way = 0 if up else 1
            return [
                pltpu.make_async_remote_copy(
                    src_ref=(za, zb)[h].at[k],
                    dst_ref=dst[h].at[to],
                    send_sem=ss.at[6 + h, k],
                    recv_sem=zr.at[way, h, to],
                    device_id=target,
                    device_id_type=MESH,
                )
                for h in range(2)
            ]

        def step(t, _):
            @pl.when(t < nz)
            def _():
                k, s = t, t % 2
                to = far_first(k, z, nz)

                @pl.when(k >= 2)
                def _():
                    for cp in sib(k - 2):
                        cp.wait_send()
                    for cp in first(k - 2):
                        cp.wait_send()

                def store_sib(y_to, x_to, value):
                    sa[s, x_to, y_to] = value[:ra].astype(bf16)
                    sb[s, y_to, x_to] = value[ra:].astype(bf16)

                unit(ins, 1 - core, to, store_sib)
                for cp in sib(k):
                    cp.start()
                waits = sib(k)
                done = []

                def store_own(y_to, x_to, value):
                    if not done:
                        done.append(True)
                        for cp in waits:
                            cp.wait_recv()
                    oa[s, x_to, y_to] = (value[:ra] + ga[k, x_to, y_to].astype(f32)).astype(bf16)
                    ob[s, y_to, x_to] = (value[ra:] + gb[k, y_to, x_to].astype(f32)).astype(bf16)

                unit(ins, core, to, store_own)
                for cp in first(k):
                    cp.start()

            @pl.when((t >= 1) & (t <= nz))
            def _():
                k, s = t - 1, (t - 1) % 2

                @pl.when(k >= 2)
                def _():
                    for cp in second(k - 2):
                        cp.wait_send()

                one, two = first(k)
                one.wait_recv()
                ta[s] = (oa[s, x, 1 - y].astype(f32) + xa[k, 1 - y].astype(f32)).astype(bf16)
                go_a, go_b = second(k)
                go_a.start()
                la[s] = oa[s, x, y].astype(f32) + xa[k, y].astype(f32)
                two.wait_recv()
                tb[s] = (ob[s, y, 1 - x].astype(f32) + yb[k, 1 - x].astype(f32)).astype(bf16)
                go_b.start()
                lb[s] = ob[s, y, x].astype(f32) + yb[k, x].astype(f32)

            @pl.when(t >= 2)
            def _():
                k, s = t - 2, t % 2
                to = far_first(k, z, nz)
                one, two = second(k)
                one.wait_recv()
                two.wait_recv()
                la[s] = la[s] + ya[k].astype(f32)
                lb[s] = lb[s] + xb[k].astype(f32)
                for up in (True, False):
                    behind = has_down if up else has_up

                    @pl.when(((to > z) if up else (to < z)) & behind)
                    def _():
                        for cp in line(k, to, up):
                            cp.wait_recv()
                        la[s] = la[s] + (ua, da)[0 if up else 1][to].astype(f32)
                        lb[s] = lb[s] + (ub, db)[0 if up else 1][to].astype(f32)

                    @pl.when((to > z) if up else (to < z))
                    def _():
                        za[k] = la[s].astype(bf16)
                        zb[k] = lb[s].astype(bf16)
                        for cp in line(k, to, up):
                            cp.start()

            return 0

        lax.fori_loop(0, nz + 2, step, 0)
        last = (nz - 1) % 2
        for up in (True, False):

            @pl.when(has_down if up else has_up)
            def _():
                for cp in line(nz - 1, z, up):
                    cp.wait_recv()
                la[last] = la[last] + (ua, da)[0 if up else 1][z].astype(f32)
                lb[last] = lb[last] + (ub, db)[0 if up else 1][z].astype(f32)

        out[:ra] = la[last]
        out[ra:] = lb[last]
        for k in range(nz - 2, nz):
            for cp in (*sib(k), *first(k), *second(k)):
                cp.wait_send()
        for k in range(nz - 1):
            for cp in line(k, 0, True):
                cp.wait_send()

    def vm(*dims, dtype=bf16):
        return pltpu.VMEM(dims, dtype)

    halves = [
        *(vm(2, 2, 2, h, n) for h in (ra, rb)),
        *(vm(nz, 2, 2, h, n) for h in (ra, rb)),
        *(vm(2, 2, 2, h, n) for h in (ra, rb)),
        *(vm(nz, 2, h, n) for h in (ra, rb)),
        *(vm(2, h, n) for h in (ra, rb)),
        *(vm(nz, h, n) for h in (ra, rb)),
        *(vm(2, h, n, dtype=f32) for h in (ra, rb)),
        *(vm(nz, h, n) for h in (ra, rb)),
        *(vm(nz, h, n) for h in (ra, rb)),
        *(vm(nz, h, n) for h in (ra, rb)),
    ]
    flops = sum(2 * 2 * 2 * nz * grid.ny * rows * n * 512 for _ in range(1))
    return pl.pallas_call(
        kernel,
        out_shape=jax.ShapeDtypeStruct((rows, n), f32),
        in_specs=[pl.BlockSpec(memory_space=pltpu.VMEM)] * count,
        out_specs=pl.BlockSpec(memory_space=pltpu.VMEM),
        scratch_shapes=[
            *halves,
            pltpu.SemaphoreType.DMA((8, nz)),
            pltpu.SemaphoreType.DMA((6, nz)),
            pltpu.SemaphoreType.DMA((2, 2, nz)),
        ],
        compiler_params=pltpu.CompilerParams(
            collective_id=collective_id, has_side_effects=True, vmem_limit_bytes=VMEM_LIMIT
        ),
        cost_estimate=cost(flops, 100_000_000),
        name=name,
    )(*operands)


def near_first(k, z, nz):
    return far_first(nz - 1 - k, z, nz)


def forward_gather(grid, x_in, weights, vectors, seg_col, seg_row, seg_other):
    _, rows, width = x_in.shape
    tokens = 2 * rows
    nz = grid.nz
    parts, groups = grid.dp, grid.ctx
    wide = pl.cdiv(width, LANES) * LANES
    pairs = wide // LANES
    n_qkv, n_out, n_fc = (w.shape[1] for w in weights[:3])
    slab = weights[0].shape[0]
    ff = weights[3].shape[1]
    n_vec = vectors.shape[1]
    n_bias = n_out
    n_slots = 4 * nz

    def kernel(
        x_ref, wq_in, wo_in, wf_in, wp_in, vec_in, sc_ref, sr_ref, so_ref,
        gq, go, gf, gp, vec_out, inner_out, act_out, sib_out,
        n1_ref, q_ref, k_ref, v_ref, att_ref, of_ref, lse_ref, hid_ref, n2_ref,
        sib, vbuf, rowbuf, jrow, wqkv, wbig, wout, stage_u, stage_a, mq, mo, mf, mp,
        s_z, r_z, s_p, r_p, s_vz, r_vz, s_vy, r_vy, s_kv, r_kv, s_loc, s_w, s_st,
    ):
        d, c = lax.axis_index("dp"), lax.axis_index("ctx")
        z, y = d // grid.ny, d % grid.ny
        x, core = c // 2, c % 2
        extra = 1 - core
        at_sib = (d, c + 1 - 2 * core)
        at_x = (d, (1 - x) * 2 + core)
        at_y = (z * grid.ny + 1 - y, c)
        at_up = ((z + 1) * grid.ny + y, c)
        at_down = ((z - 1) * grid.ny + y, c)
        has_up, has_down = z < nz - 1, z > 0
        gathered = (gq, go, gf, gp)
        mine = (mq, mo, mf, mp)
        cuts = [(w.shape[0] // 2 + 7) // 8 * 8 for w in weights]

        def piece(w, zz, yy, xx, cc, half=None):
            h = weights[w].shape[0]
            tail = () if half is None else ((pl.ds(0, cuts[w]) if half == 0 else pl.ds(cuts[w], h - cuts[w])),)
            index = (zz, yy, xx, cc) if w < 3 else (xx, cc, zz, yy)
            return gathered[w].at[(*index, *tail)]

        def remote(src, dst, send, recv, target):
            return pltpu.make_async_remote_copy(
                src_ref=src, dst_ref=dst, send_sem=send, recv_sem=recv, device_id=target, device_id_type=MESH
            )

        every = slice(None)

        def part_copy(w, kind, j):
            zz = near_first(j, z, nz)
            src, target = (
                (piece(w, zz, y, x, core, 0), at_y),
                (piece(w, zz, y, x, core, 1), at_x),
                (piece(w, zz, every, x, core, 0), at_x),
                (piece(w, zz, y, every, core, 1), at_y),
                (piece(w, zz, every, every, core), at_sib),
            )[kind]
            return remote(src, src, s_p.at[w, kind, j], r_p.at[w, kind, j], target)

        def z_copy(w, zz, way, j):
            src = piece(w, zz, y, x, core)
            return remote(src, src, s_z.at[w, way, j], r_z.at[w, zz], (at_up, at_down)[way])

        def vz_copy(zz, way, j):
            src = vbuf.at[zz, y]
            return remote(src, src, s_vz.at[way, j], r_vz.at[zz], (at_up, at_down)[way])

        def vy_copy(j):
            src = vbuf.at[near_first(j, z, nz), y]
            return remote(src, src, s_vy.at[j], r_vy.at[j], at_y)

        def passes_on(j):
            zz = near_first(j, z, nz)
            return zz, (zz < z) & has_up, (zz > z) & has_down

        def z_arrived(w, j):
            zz = near_first(j, z, nz)
            z_copy(w, zz, 0, j).wait_recv()
            if w == 0:
                vz_copy(zz, 0, j).wait_recv()

        def z_send(w, zz, way, j):
            z_copy(w, zz, way, j).start()
            if w == 0:
                vz_copy(zz, way, j).start()

        def pass_on(i):
            w, j = divmod(i, nz)
            if j == 0:

                @pl.when(has_up)
                def _():
                    z_send(w, z, 0, 0)

                @pl.when(has_down)
                def _():
                    z_send(w, z, 1, 0)

                return
            zz, up, down = passes_on(j)
            for way, flag in ((0, up), (1, down)):

                @pl.when(flag)
                def _():
                    z_arrived(w, j)
                    z_send(w, zz, way, j)

        def tick(i):
            if i < n_slots:
                w, j = divmod(i, nz)
                if j > 0:
                    _, up, down = passes_on(j)

                    @pl.when(jnp.logical_not(up | down))
                    def _():
                        z_arrived(w, j)

                part_copy(w, 0, j).start()
                part_copy(w, 1, j).start()
                if w == 0:
                    vy_copy(j).start()
            if 0 <= i - 1 < n_slots:
                w, j = divmod(i - 1, nz)
                part_copy(w, 0, j).wait_recv()
                part_copy(w, 2, j).start()
                part_copy(w, 1, j).wait_recv()
                part_copy(w, 3, j).start()
            if 0 <= i - 2 < n_slots:
                w, j = divmod(i - 2, nz)
                part_copy(w, 2, j).wait_recv()
                part_copy(w, 3, j).wait_recv()
                part_copy(w, 4, j).start()
            if i + 1 < n_slots:
                pass_on(i + 1)

        def complete(w):
            for j in range(nz):
                part_copy(w, 4, j).wait_recv()

        barrier = pltpu.get_barrier_semaphore()
        for target in (at_sib, at_x, at_y):
            pl.semaphore_signal(barrier, inc=1, device_id=target, device_id_type=MESH)

        @pl.when(has_up)
        def _():
            pl.semaphore_signal(barrier, inc=1, device_id=at_up, device_id_type=MESH)

        @pl.when(has_down)
        def _():
            pl.semaphore_signal(barrier, inc=1, device_id=at_down, device_id_type=MESH)

        sources = (wq_in, wo_in, wf_in, wp_in)
        into = [pltpu.make_async_copy(src, mine[w], s_loc.at[w]) for w, src in enumerate(sources)]
        into.append(pltpu.make_async_copy(vec_in, vbuf.at[z, y], s_loc.at[4]))
        for cp in into:
            cp.start()
        for ref in (q_ref, k_ref, v_ref):
            ref[:, :, wide - LANES :] = jnp.zeros((2, rows, LANES), bf16)
        jrow[...] = jnp.zeros_like(jrow)
        for cp in into:
            cp.wait()
        local = [
            pltpu.make_async_copy(mine[w], piece(w, z, y, x, core), s_loc.at[w]) for w in range(4)
        ]
        for cp in local:
            cp.start()
        for cp in local:
            cp.wait()
        pl.semaphore_wait(barrier, 3 + has_up.astype(jnp.int32) + has_down.astype(jnp.int32))

        pass_on(0)
        for i in range(nz + 1):
            tick(i)
        for j in range(nz):
            vy_copy(j).wait_recv()

        for part in range(parts):
            line = vbuf[part // grid.ny, part % grid.ny]
            cols = slice(part * n_bias, (part + 1) * n_bias)
            for v in range(8):
                term = line[0:1, n_fc + v * n_bias : n_fc + (v + 1) * n_bias]
                if v < 2:
                    jrow[0:1, 2 * v * width + cols.start : 2 * v * width + cols.stop] = term
                else:
                    rowbuf[v : v + 1, cols] = term
        for s in range(2):
            values = x_ref[s].astype(f32)
            n1_ref[s] = layer_norm(values, rowbuf[4:5, :], rowbuf[5:6, :]).astype(bf16)

        for i in range(nz + 1, nz + 3):
            tick(i)
        complete(0)

        def stream(source, buffer, body, hooks):
            def load(part):
                return pltpu.make_async_copy(
                    source.at[part // grid.ny, part % grid.ny], buffer.at[part % 2], s_w.at[part % 2]
                )

            load(0).start()

            def step(part, _):
                load(part).wait()

                @pl.when(part + 1 < parts)
                def _():
                    load(part + 1).start()

                body(part, part % 2)
                for when, todo in hooks.items():

                    @pl.when(part == when)
                    def _():
                        for i in todo:
                            tick(i)

                return 0

            lax.fori_loop(0, parts, step, 0)

        def project(part, slot):
            left = n1_ref[...].reshape(tokens, width)
            product = dot_nn(left, wqkv[slot].reshape(width, n_qkv))
            for p in range(parts):

                @pl.when(part == p)
                def _():
                    first, last = p * n_qkv, (p + 1) * n_qkv
                    out = (product + jrow[0:1, first:last]).astype(bf16).reshape(2, rows, n_qkv)
                    for g, ref in enumerate((q_ref, k_ref, v_ref)):
                        lo, hi = max(first, g * width), min(last, (g + 1) * width)
                        if lo < hi:
                            ref[:, :, lo - g * width : hi - g * width] = out[:, :, lo - first : hi - first]

        stream(gq, wqkv, project, {0: [nz + 3], 4: [nz + 4]})
        swaps = [
            remote(ref, sib.at[kind], s_kv.at[kind], r_kv.at[kind], at_sib)
            for kind, ref in enumerate((k_ref, v_ref))
        ]
        for cp in swaps:
            cp.start()
        for cp in swaps:
            cp.wait_recv()
        tick(nz + 5)

        def attend(p, _):
            lanes = pl.ds(pl.multiple_of(p * LANES, LANES), LANES)
            got = pair_forward(
                extra,
                lambda i: q_ref[i, :, lanes],
                lambda i: k_ref[i, :, lanes],
                lambda i: v_ref[i, :, lanes],
                lambda i: sib[0, i, :, lanes],
                lambda i: sib[1, i, :, lanes],
                lambda i: sc_ref[i],
                lambda i: sr_ref[i],
                lambda i: so_ref[i],
                pair_masks(p, width),
            )
            for slot, (out, logs) in enumerate(got):
                att_ref[slot, :, lanes] = out.astype(bf16)
                of_ref[slot, :, lanes] = out
                lse_ref[slot, :, lanes] = logs

            @pl.when(p == pairs // 2)
            def _():
                tick(nz + 6)

            return 0

        lax.fori_loop(0, pairs, attend, 0)
        keep = pltpu.make_async_copy(sib, sib_out, s_loc.at[0])
        keep.start()
        complete(1)

        def branch(part, slot):
            product = dot_nn(
                att_ref[:, :, :width].reshape(tokens, width), wout[slot].reshape(width, n_out)
            ).reshape(2, rows, n_out)
            for p in range(parts):

                @pl.when(part == p)
                def _():
                    hid_ref[:, :, p * n_out : (p + 1) * n_out] = product

        stream(go, wout, branch, {0: [nz + 7]})
        for s in range(2):
            hidden = x_ref[s].astype(f32) + hid_ref[s] + rowbuf[2:3, :]
            hid_ref[s] = hidden
            n2_ref[s] = layer_norm(hidden, rowbuf[6:7, :], rowbuf[7:8, :]).astype(bf16)
        tick(nz + 8)
        tick(nz + 9)
        complete(2)

        ratio = parts // groups

        def saves(group):
            slot = group % 2
            return (
                pltpu.make_async_copy(stage_u.at[slot], inner_out.at[group], s_st.at[0, slot]),
                pltpu.make_async_copy(stage_a.at[slot], act_out.at[group], s_st.at[1, slot]),
            )

        def feed(part, slot):
            group, place = part // ratio, part % ratio

            @pl.when((place == 0) & (group >= 2))
            def _():
                for cp in saves(group - 2):
                    cp.wait()

            left = n2_ref[...].reshape(tokens, width)
            u = dot_nn(left, wbig[slot].reshape(width, n_fc))
            u = u + vbuf[part // grid.ny, part % grid.ny][0:1, :n_fc]
            act = (0.5 * u * (1.0 + jnp.tanh(GELU_C * (u + GELU_A * u * u * u)))).astype(bf16)
            for r in range(ratio):

                @pl.when(place == r)
                def _():
                    stage_u[group % 2, :, r * n_fc : (r + 1) * n_fc] = u
                    stage_a[group % 2, :, r * n_fc : (r + 1) * n_fc] = act

            @pl.when(place == ratio - 1)
            def _():
                for cp in saves(group):
                    cp.start()

        stream(gf, wbig, feed, {1: [nz + 10], 5: [nz + 11]})
        tick(nz + 12)
        tick(nz + 13)
        save_vec = pltpu.make_async_copy(vbuf, vec_out, s_loc.at[1])
        save_vec.start()
        for group in range(groups - 2, groups):
            for cp in saves(group):
                cp.wait()
        keep.wait()
        save_vec.wait()
        complete(3)
        for cp in swaps:
            cp.wait_send()

        def finish(j, _):
            zz, up, down = passes_on(j)
            up, down = up | ((j == 0) & has_up), down | ((j == 0) & has_down)
            vy_copy(j).wait_send()
            for w in range(4):
                for kind in range(5):
                    part_copy(w, kind, j).wait_send()
                for way, flag in ((0, up), (1, down)):

                    @pl.when(flag)
                    def _():
                        z_copy(w, zz, way, j).wait_send()
                        if w == 0:
                            vz_copy(zz, way, j).wait_send()

            return 0

        lax.fori_loop(0, nz, finish, 0)

    any_, vm = pl.BlockSpec(memory_space=pl.ANY), pl.BlockSpec(memory_space=pltpu.VMEM)
    dma = pltpu.SemaphoreType.DMA
    columns = [
        jax.ShapeDtypeStruct((nz, grid.ny, grid.nx, 2, *w.shape), bf16) for w in weights[:3]
    ]
    wide_low = jax.ShapeDtypeStruct((2, rows, wide), bf16)
    wide_full = jax.ShapeDtypeStruct((2, rows, wide), f32)
    low = jax.ShapeDtypeStruct((2, rows, width), bf16)
    out_shape = [
        *columns,
        jax.ShapeDtypeStruct((grid.nx, 2, nz, grid.ny, *weights[3].shape), bf16),
        jax.ShapeDtypeStruct((nz, grid.ny, 8, n_vec), f32),
        jax.ShapeDtypeStruct((groups, tokens, ff), f32),
        jax.ShapeDtypeStruct((groups, tokens, ff), bf16),
        jax.ShapeDtypeStruct((2, 2, rows, wide), bf16),
        low,
        wide_low,
        wide_low,
        wide_low,
        wide_low,
        wide_full,
        wide_full,
        jax.ShapeDtypeStruct((2, rows, width), f32),
        low,
    ]
    return pl.pallas_call(
        kernel,
        out_shape=out_shape,
        in_specs=[vm] + [any_] * 4 + [any_] + [vm] * 3,
        out_specs=[any_] * 8 + [vm] * 9,
        scratch_shapes=[
            pltpu.VMEM((2, 2, rows, wide), bf16),
            pltpu.VMEM((nz, grid.ny, 8, n_vec), f32),
            pltpu.VMEM((8, width), f32),
            pltpu.VMEM((8, 3 * width), f32),
            pltpu.VMEM((2, grid.nx, 2, slab, n_qkv), bf16),
            pltpu.VMEM((2, grid.nx, 2, slab, n_fc), bf16),
            pltpu.VMEM((2, grid.nx, 2, slab, n_out), bf16),
            pltpu.VMEM((2, tokens, ff), f32),
            pltpu.VMEM((2, tokens, ff), bf16),
            *(pltpu.VMEM(w.shape, bf16) for w in weights),
            dma((4, 2, nz)),
            dma((4, nz)),
            dma((4, 5, nz)),
            dma((4, 5, nz)),
            dma((2, nz)),
            dma((nz,)),
            dma((nz,)),
            dma((nz,)),
            dma((2,)),
            dma((2,)),
            dma((5,)),
            dma((2,)),
            dma((2, 2)),
        ],
        compiler_params=pltpu.CompilerParams(
            collective_id=4, has_side_effects=True, vmem_limit_bytes=VMEM_LIMIT
        ),
        cost_estimate=cost(30e9, 150e6),
        name="forward",
    )(x_in, *weights, vectors, seg_col, seg_row, seg_other)


def pick(array, index, axis):
    return lax.dynamic_index_in_dim(array, index, axis, keepdims=False)


def add_low(first, second):
    return (first.astype(f32) + second.astype(f32)).astype(bf16)


class Grid:
    def __init__(self, dp, ctx):
        self.dp, self.ctx = dp, ctx
        self.nx = max(ctx // 2, 1)
        self.ny = self.nx
        self.nz = dp // self.ny
        self.paired = self.nx == 2 and ctx == 4 and dp % 2 == 0

    def place(self):
        d, c = lax.axis_index("dp"), lax.axis_index("ctx")
        self.d, self.c = d, c
        self.z, self.y = d // self.ny, d % self.ny
        self.x, self.core = c // 2, c % 2

    def swap_core(self, v):
        return lax.ppermute(v, "ctx", [(i, i ^ 1) for i in range(self.ctx)])

    ACROSS = ((0, 2), (1, 3), (2, 1), (3, 0))
    WITHIN = ((2, 3), (3, 2))

    def by_sequence(self, v):
        first = self.x == 0
        across = lax.ppermute(pick(v, 1 - self.x, 0), "ctx", self.ACROSS)
        within = lax.ppermute(v[1], "ctx", self.WITHIN)
        return jnp.stack([jnp.where(first, v[0], across), jnp.where(first, across, within)])

    def by_position(self, v):
        first = self.x == 0
        across = lax.ppermute(pick(v, 1 - self.x, 0), "ctx", [(b, a) for a, b in self.ACROSS])
        within = lax.ppermute(v[1], "ctx", self.WITHIN)
        return jnp.stack([jnp.where(first, v[0], across), jnp.where(first, across, within)])


def on_device(grid, *args):
    (
        layer_input,
        grad_out,
        segment_ids,
        qkv_weight,
        q_bias,
        v_bias,
        out_weight,
        out_bias,
        fc_weight,
        fc_bias,
        proj_weight,
        proj_bias,
        ln1_gain,
        ln1_bias,
        ln2_gain,
        ln2_bias,
    ) = args
    seqs, rows, width = layer_input.shape
    tokens = seqs * rows
    parts, groups = grid.dp, grid.ctx
    both = ("dp", "ctx")
    grid.place()

    n_qkv, n_out, n_fc = qkv_weight.shape[1], out_weight.shape[1], fc_weight.shape[1]
    slab, hidden_slab = qkv_weight.shape[0], proj_weight.shape[0]
    paired = grid.paired and seqs == 2
    seg_blocks = segment_ids.reshape(seqs, groups, rows)
    vectors = (fc_bias, q_bias, v_bias, out_bias, proj_bias, ln1_gain, ln1_bias, ln2_gain, ln2_bias)
    sizes = [v.shape[0] for v in vectors]

    def unpack(packed):
        spread, at = [], 0
        for size in sizes:
            spread.append(packed[:, at : at + size].astype(f32))
            at += size
        return [v.reshape(-1) for v in spread]

    if paired:
        layer_input, grad_out = grid.by_sequence(layer_input), grid.by_sequence(grad_out)
        extra = 1 - grid.core
        chip_seg = pick(seg_blocks, grid.x, 0)
        seg_own = jnp.stack([pick(chip_seg, grid.core, 0), pick(chip_seg, 3 - grid.core, 0)])
        seg_other = jnp.stack([pick(chip_seg, extra, 0), pick(chip_seg, 3 - extra, 0)])
        packed = jnp.concatenate(vectors).astype(f32)[None]
        (
            w_qkv, w_out, w_fc, w_proj, packed, inner, activated, other,
            normed1, queries, keys, vals, attended, attended_f32, log_total, hidden, normed2,
        ) = forward_gather(
            grid,
            layer_input,
            (qkv_weight, out_weight, fc_weight, proj_weight.T),
            jnp.broadcast_to(packed, (8, packed.shape[1])),
            seg_own[:, :, None],
            seg_own[:, None, :],
            seg_other[:, None, :],
        )
        _, _, _, _, pb_all, g1, b1, g2, b2 = unpack(packed[:, :, 0].reshape(parts, -1))
        w_qkv = w_qkv.reshape(parts, width, n_qkv)
        w_fc = w_fc.reshape(parts, width, n_fc)
        w_proj = w_proj.reshape(groups, width, hidden_slab)
        out_full = w_out.reshape(parts, width, n_out).transpose(1, 0, 2).reshape(width, width)
        normed1, normed2, hidden = (v.reshape(tokens, width) for v in (normed1, normed2, hidden))
        attended = attended[:, :, :width].reshape(tokens, width)
        values = layer_input.reshape(tokens, width).astype(f32)
    else:
        packed = lax.all_gather(jnp.concatenate(vectors), "dp", axis=0)
        fcb, q_all, v_all, ob_all, pb_all, g1, b1, g2, b2 = unpack(packed)

        def gather(block, axes):
            return lax.all_gather(block, axes, axis=0)

        w_qkv = gather(qkv_weight, both).reshape(parts, width, n_qkv)
        w_out = gather(out_weight, both).reshape(parts, width, n_out)
        w_fc = gather(fc_weight, both).reshape(parts, width, n_fc)
        w_proj = gather(proj_weight.T, ("ctx", "dp")).reshape(groups, width, hidden_slab)
        out_full = w_out.transpose(1, 0, 2).reshape(width, width)
        values = layer_input.reshape(tokens, width).astype(f32)
        normed1 = layer_norm(values, g1, b1).astype(bf16)
        joined = jnp.concatenate([q_all, jnp.zeros((width,), f32), v_all])
        queries, key_rows, value_rows = qkv_project(normed1, w_qkv, joined.reshape(parts, 1, n_qkv))
        queries = queries.reshape(seqs, rows, width)
        own = jnp.stack([key_rows, value_rows]).reshape(2, seqs, rows, width)
        pairs_full = lax.all_gather(own, "ctx", axis=0)
        seg_mine = pick(seg_blocks, grid.c, 1)
        needed = seg_blocks[:, :, -1] >= seg_mine[:, :1]
        start = jnp.minimum(jnp.argmax(needed, axis=1).astype(jnp.int32), grid.c)
        bounds = jnp.concatenate([grid.c[None].astype(jnp.int32), start])
        attended, attended_f32, log_total = attention_forward(
            bounds, queries, pairs_full, seg_mine[:, :, None], seg_blocks[:, :, None, :]
        )
        attended = attended.reshape(tokens, width)
        hidden = values + jnp.dot(attended, out_full, preferred_element_type=f32) + ob_all
        normed2 = layer_norm(hidden, g2, b2).astype(bf16)
        inner, activated = feed_in(normed2, w_fc, fcb.reshape(parts, 1, n_fc), groups)
    output = feed_out(activated, w_proj, hidden, pb_all[None])

    mlp_grad = grad_out.reshape(tokens, width)
    cotangent = mlp_grad.astype(f32)
    proj_bias_grad = jnp.sum(cotangent, axis=0)
    inner_grad, fc_bias_grad = feed_back(mlp_grad, w_proj, inner, parts)

    def tall_cut(size):
        return (size // 2 + 15) // 16 * 16

    def by_columns(refs, core, z, store):
        for y_to in range(2):
            for x_to in range(2):
                at = pl.ds(pl.multiple_of((2 * x_to + core) * slab, 16), slab)
                terms = [
                    dot_nn(left[at, :], right[z * grid.ny + y_to])
                    for left, right in zip(refs[::2], refs[1::2])
                ]
                store(y_to, x_to, jnp.concatenate(terms, axis=1) if len(terms) > 1 else terms[0])

    def by_rows(refs, core, z, store):
        left, right = refs
        cols = width // parts
        at = pl.ds(pl.multiple_of(z * (grid.ny * cols), 16), grid.ny * cols)
        for x_to in range(2):
            term = dot_nn(left[at, :], right[2 * x_to + core])
            for y_to in range(2):
                store(y_to, x_to, term[y_to * cols : (y_to + 1) * cols])

    def reduced(pairs, collective_id, name):
        if not paired:
            everything = jnp.arange(parts, dtype=jnp.int32)
            results = []
            for left, right in pairs:
                whole = weight_grad(left.T, right, everything)
                whole = whole.reshape(parts * groups, slab, right.shape[2])
                results.append(lax.psum_scatter(whole, both, scatter_dimension=0).astype(f32))
            return results
        operands, ends = [], [0]
        for left, right in pairs:
            n = right.shape[2]
            full = n if len(ends) == len(pairs) else pl.cdiv(n, LANES) * LANES
            operands += [left.T, jnp.pad(right, ((0, 0), (0, 0), (0, full - n)))]
            ends.append(ends[-1] + full)
        total = summed_grads(
            grid, collective_id, operands, by_columns, (slab, ends[-1]), tall_cut(slab), name
        )
        return [total[:, at : at + pair[1].shape[2]] for at, pair in zip(ends, pairs)]

    def reduced_proj(left, right):
        f = right.shape[2]
        cols = width // parts
        if not paired:
            whole = weight_grad(left.T, right, jnp.arange(groups, dtype=jnp.int32))
            whole = whole.reshape(groups * parts, cols, f)
            return lax.psum_scatter(whole, ("ctx", "dp"), scatter_dimension=0).astype(f32)
        return summed_grads(grid, 1, [left.T, right], by_rows, (cols, f), tall_cut(cols), "rs_proj")

    proj_weight_grad = reduced_proj(mlp_grad, activated).T
    (fc_weight_grad,) = reduced([(normed2, inner_grad)], 2, "rs_fc")

    normed2_grad = back_project(inner_grad, w_fc)
    norm2_out, norm2_pull = jax.vjp(layer_norm, hidden, g2, b2)
    hidden_ln, g2_grad, b2_grad = norm2_pull(normed2_grad)
    hidden_grad = cotangent + hidden_ln
    branch_grad = hidden_grad.astype(bf16)
    out_bias_grad = jnp.sum(branch_grad, axis=0, dtype=f32)
    attended_grad = jnp.einsum(
        "nd,ed->ne", branch_grad, out_full, preferred_element_type=f32
    ).astype(bf16)
    branch_parts = branch_grad.reshape(tokens, parts, n_out).transpose(1, 0, 2)

    attended_grad = attended_grad.reshape(seqs, rows, width)
    if paired:
        query_grad, own_grad, other_grad = chip_attention_back(
            extra.astype(jnp.int32)[None],
            queries,
            keys,
            vals,
            other,
            attended_grad,
            attended_f32,
            log_total,
            seg_own[:, None, :],
            seg_own[:, :, None],
            seg_other[:, :, None],
        )
        pair_grad = add_low(own_grad, grid.swap_core(other_grad))
    else:
        query_grad, pairs_grad = attention_backward(
            bounds,
            queries,
            pairs_full,
            seg_blocks[:, :, :, None],
            seg_mine[:, None, :],
            attended_grad,
            attended_f32,
            log_total,
        )
        pair_grad = lax.psum_scatter(pairs_grad, "ctx", scatter_dimension=0)
    pair_grad = pair_grad.reshape(2, tokens, width)
    projected_grad = jnp.concatenate(
        [query_grad.reshape(tokens, width), pair_grad[0], pair_grad[1]], axis=1
    )
    q_bias_grad = jnp.sum(query_grad.reshape(tokens, width), axis=0, dtype=f32)
    v_bias_grad = jnp.sum(pair_grad[1], axis=0, dtype=f32)
    by_part = projected_grad.reshape(tokens, parts, n_qkv).transpose(1, 0, 2)
    out_weight_grad, qkv_weight_grad = reduced(
        [(attended, branch_parts), (normed1, by_part)], 3, "rs_qkv"
    )
    normed1_grad = back_project(by_part, w_qkv)
    norm1_out, norm1_pull = jax.vjp(layer_norm, values, g1, b1)
    values_ln, g1_grad, b1_grad = norm1_pull(normed1_grad)
    input_grad = hidden_grad + values_ln

    output, input_grad = (v.reshape(seqs, rows, width) for v in (output, input_grad))
    if paired:
        output, input_grad = grid.by_position(output), grid.by_position(input_grad)

    sums = [
        fc_bias_grad,
        q_bias_grad,
        v_bias_grad,
        out_bias_grad,
        proj_bias_grad,
        g1_grad,
        b1_grad,
        g2_grad,
        b2_grad,
    ]
    stacked = jnp.concatenate([v.reshape(parts, -1) for v in sums], axis=1)
    total = pick(lax.psum(stacked, both), grid.d, 0)
    vec, at = [], 0
    for size in sizes:
        vec.append(total[at : at + size])
        at += size
    return (
        output,
        input_grad,
        qkv_weight_grad,
        vec[1],
        vec[2],
        out_weight_grad,
        vec[3],
        fc_weight_grad,
        vec[0],
        proj_weight_grad,
        vec[4],
        vec[5],
        vec[6],
        vec[7],
        vec[8],
    )


def solution(mesh):
    rows3, mat, vec = P("dp", "ctx", None), P("ctx", "dp"), P("dp")
    grid = Grid(mesh.shape["dp"], mesh.shape["ctx"])
    return jax.shard_map(
        functools.partial(on_device, grid),
        mesh=mesh,
        in_specs=(
            rows3,
            rows3,
            P("dp", None),
            mat,
            vec,
            vec,
            mat,
            vec,
            mat,
            vec,
            mat,
            vec,
            vec,
            vec,
            vec,
            vec,
        ),
        out_specs=(
            rows3,
            rows3,
            mat,
            vec,
            vec,
            mat,
            vec,
            mat,
            vec,
            mat,
            vec,
            vec,
            vec,
            vec,
            vec,
        ),
        check_vma=False,
    )
```

```python
import functools

import jax
import jax.numpy as jnp
from jax import lax
from jax.experimental import pallas as pl
from jax.experimental.pallas import tpu as pltpu
from jax.sharding import PartitionSpec as P

HEADS = 25
HEAD_DIM = 64
LANES = 128
EPS = 1e-05
NEG_FILL = -1e30
GELU_C = 0.7978845608028654
GELU_A = 0.044715

bf16 = jnp.bfloat16
f32 = jnp.float32
VMEM_LIMIT = 58 * 1024 * 1024


def layer_norm(values, gain, shift):
    center = values - jnp.mean(values, axis=-1, keepdims=True)
    factor = lax.rsqrt(jnp.mean(center * center, axis=-1, keepdims=True) + EPS)
    return center * factor * gain + shift


def dot_nn(a, b):
    return lax.dot_general(a, b, (((1,), (0,)), ((), ())), preferred_element_type=f32)


def dot_nt(a, b):
    return lax.dot_general(a, b, (((1,), (1,)), ((), ())), preferred_element_type=f32)


def dot_tn(a, b):
    return lax.dot_general(a, b, (((0,), (0,)), ((), ())), preferred_element_type=f32)


def params(n_axes=1):
    return pltpu.CompilerParams(
        dimension_semantics=("arbitrary",) * n_axes, vmem_limit_bytes=VMEM_LIMIT
    )


def cost(flops, read, transcendentals=0):
    return pl.CostEstimate(
        flops=int(flops), bytes_accessed=int(read), transcendentals=int(transcendentals)
    )


def qkv_project(normed, weight, bias):
    tokens, width = normed.shape
    parts, _, n = weight.shape

    def kernel(x_ref, w_ref, b_ref, *out_refs):
        part = pl.program_id(0)
        y = (dot_nn(x_ref[...], w_ref[0]) + b_ref[0]).astype(bf16)
        for d in range(parts):

            @pl.when(part == d)
            def _():
                first, last = d * n, (d + 1) * n
                for g in range(3):
                    lo, hi = max(first, g * width), min(last, (g + 1) * width)
                    if lo < hi:
                        out_refs[g][:, lo - g * width : hi - g * width] = y[
                            :, lo - first : hi - first
                        ]

    whole = pl.BlockSpec((tokens, width), lambda d: (0, 0))
    return pl.pallas_call(
        kernel,
        grid=(parts,),
        in_specs=[
            whole,
            pl.BlockSpec((1, width, n), lambda d: (d, 0, 0)),
            pl.BlockSpec((1, 1, n), lambda d: (d, 0, 0)),
        ],
        out_specs=[whole] * 3,
        out_shape=[jax.ShapeDtypeStruct((tokens, width), bf16)] * 3,
        compiler_params=params(),
        cost_estimate=cost(2 * tokens * width * parts * n, 2 * width * parts * n),
        name="qkv",
    )(normed, weight, bias)


def pair_masks(pair, width):
    lane = lax.broadcasted_iota(jnp.int32, (1, LANES), 1)
    inside = lane + pair * LANES < width
    return inside & (lane < HEAD_DIM), inside & (lane >= HEAD_DIM), inside


def attention_forward(bounds, queries, pairs_full, seg_col, seg_row):
    seqs, rows, width = queries.shape
    blocks = pairs_full.shape[0]
    pairs = pl.cdiv(width, LANES)

    def kernel(bounds_ref, q_ref, kv_ref, sc_ref, sr_ref, o_ref, of_ref, lse_ref):
        seq, pair = pl.program_id(0), pl.program_id(1)
        mine, start = bounds_ref[0], bounds_ref[1 + seq]
        low, high, inside = pair_masks(pair, width)
        scaled = q_ref[0] * jnp.asarray(0.125, bf16)
        q_heads = (
            jnp.where(low, scaled, jnp.zeros_like(scaled)),
            jnp.where(high, scaled, jnp.zeros_like(scaled)),
        )
        seg_q = sc_ref[0]

        def block(j, diagonal, carry):
            k = jnp.where(inside, kv_ref[j, 0, 0], jnp.zeros((rows, LANES), bf16))
            v = jnp.where(inside, kv_ref[j, 1, 0], jnp.zeros((rows, LANES), bf16))
            allowed = sr_ref[0, j] == seg_q
            if diagonal:
                at_row = lax.broadcasted_iota(jnp.int32, (rows, rows), 0)
                at_col = lax.broadcasted_iota(jnp.int32, (rows, rows), 1)
                allowed = allowed & (at_col <= at_row)
            out = []
            for head in range(2):
                s = jnp.where(allowed, dot_nt(q_heads[head], k), NEG_FILL)
                top = jnp.max(s, axis=1, keepdims=True)
                if carry is None:
                    p = jnp.exp(s - top)
                    out += [top, jnp.sum(p, axis=1, keepdims=True), dot_nn(p.astype(bf16), v)]
                else:
                    m, l, acc = carry[3 * head : 3 * head + 3]
                    new = jnp.maximum(m, top)
                    scale = jnp.exp(m - new)
                    p = jnp.exp(s - new)
                    out += [
                        new,
                        l * scale + jnp.sum(p, axis=1, keepdims=True),
                        acc * scale + dot_nn(p.astype(bf16), v),
                    ]
            return tuple(out)

        carry = block(mine, True, None)
        carry = lax.fori_loop(start, mine, lambda j, c: block(j, False, c), carry)
        m0, l0, a0, m1, l1, a1 = carry
        result = jnp.where(low, a0 / l0, a1 / l1)
        o_ref[0] = result.astype(bf16)
        of_ref[0] = result
        lse_ref[0] = jnp.where(low, m0 + jnp.log(l0), m1 + jnp.log(l1))

    tile = pl.BlockSpec((1, rows, LANES), lambda s, p, b: (s, 0, p))
    return pl.pallas_call(
        kernel,
        grid_spec=pltpu.PrefetchScalarGridSpec(
            num_scalar_prefetch=1,
            grid=(seqs, pairs),
            in_specs=[
                tile,
                pl.BlockSpec((blocks, 2, 1, rows, LANES), lambda s, p, b: (0, 0, s, 0, p)),
                pl.BlockSpec((1, rows, 1), lambda s, p, b: (s, 0, 0)),
                pl.BlockSpec((1, blocks, 1, rows), lambda s, p, b: (s, 0, 0, 0)),
            ],
            out_specs=[tile, tile, tile],
        ),
        out_shape=[
            jax.ShapeDtypeStruct((seqs, rows, width), bf16),
            jax.ShapeDtypeStruct((seqs, rows, width), f32),
            jax.ShapeDtypeStruct((seqs, rows, width), f32),
        ],
        compiler_params=params(2),
        cost_estimate=cost(
            4 * seqs * rows * rows * blocks * width, 4 * seqs * rows * blocks * width
        ),
        name="attn_fwd",
    )(bounds, queries, pairs_full, seg_col, seg_row)


def attention_backward(
    bounds, queries, pairs_full, seg_col, seg_row, out_grad, out_full, log_total
):
    seqs, rows, width = queries.shape
    blocks = pairs_full.shape[0]
    pairs = pl.cdiv(width, LANES)

    def kernel(bounds_ref, q_ref, kv_ref, sc_ref, sr_ref, g_ref, of_ref, lse_ref, dq_ref, dkv_ref):
        seq, pair = pl.program_id(0), pl.program_id(1)
        mine, start = bounds_ref[0], bounds_ref[1 + seq]
        low, high, inside = pair_masks(pair, width)
        zero = jnp.zeros((rows, LANES), bf16)
        scaled = q_ref[0] * jnp.asarray(0.125, bf16)
        grad = g_ref[0]
        q_heads = (jnp.where(low, scaled, zero), jnp.where(high, scaled, zero))
        g_heads = (jnp.where(low, grad, zero), jnp.where(high, grad, zero))
        product = jnp.where(inside, grad.astype(f32) * of_ref[0], 0.0)
        lse = jnp.where(inside, lse_ref[0], 0.0)
        product_t = product.T
        lse_t = lse.T
        delta = (
            jnp.sum(product_t[:HEAD_DIM], axis=0, keepdims=True),
            jnp.sum(product_t[HEAD_DIM:], axis=0, keepdims=True),
        )
        log_row = (lse_t[0:1], lse_t[HEAD_DIM : HEAD_DIM + 1])
        seg_q = sr_ref[0]
        dkv_ref[...] = jnp.zeros_like(dkv_ref)

        def block(j, diagonal, total):
            k = jnp.where(inside, kv_ref[j, 0, 0], zero)
            v = jnp.where(inside, kv_ref[j, 1, 0], zero)
            allowed = sc_ref[0, j] == seg_q
            if diagonal:
                at_key = lax.broadcasted_iota(jnp.int32, (rows, rows), 0)
                at_query = lax.broadcasted_iota(jnp.int32, (rows, rows), 1)
                allowed = allowed & (at_key <= at_query)
            key_grad, value_grad = None, None
            for head in range(2):
                k_head = jnp.where((low, high)[head], k, zero)
                s = jnp.where(allowed, dot_nt(k, q_heads[head]), NEG_FILL)
                p = jnp.exp(s - log_row[head])
                pushed = dot_nt(v, g_heads[head])
                ds = (p * (pushed - delta[head])).astype(bf16)
                dv = dot_nn(p.astype(bf16), g_heads[head])
                dk = dot_nn(ds, q_heads[head])
                dq = dot_tn(ds, k_head)
                key_grad = dk if key_grad is None else key_grad + dk
                value_grad = dv if value_grad is None else value_grad + dv
                total = dq if total is None else total + dq
            dkv_ref[j, 0, 0] = key_grad.astype(bf16)
            dkv_ref[j, 1, 0] = value_grad.astype(bf16)
            return total

        total = block(mine, True, None)
        total = lax.fori_loop(start, mine, lambda j, c: block(j, False, c), total)
        dq_ref[0] = (total * 0.125).astype(bf16)

    tile = pl.BlockSpec((1, rows, LANES), lambda s, p, b: (s, 0, p))
    many = pl.BlockSpec((blocks, 2, 1, rows, LANES), lambda s, p, b: (0, 0, s, 0, p))
    return pl.pallas_call(
        kernel,
        grid_spec=pltpu.PrefetchScalarGridSpec(
            num_scalar_prefetch=1,
            grid=(seqs, pairs),
            in_specs=[
                tile,
                many,
                pl.BlockSpec((1, blocks, rows, 1), lambda s, p, b: (s, 0, 0, 0)),
                pl.BlockSpec((1, 1, rows), lambda s, p, b: (s, 0, 0)),
                tile,
                tile,
                tile,
            ],
            out_specs=[tile, many],
        ),
        out_shape=[
            jax.ShapeDtypeStruct((seqs, rows, width), bf16),
            jax.ShapeDtypeStruct(pairs_full.shape, bf16),
        ],
        compiler_params=params(2),
        cost_estimate=cost(
            10 * seqs * rows * rows * blocks * width, 8 * seqs * rows * blocks * width
        ),
        name="attn_bwd",
    )(bounds, queries, pairs_full, seg_col, seg_row, out_grad, out_full, log_total)


def causal(rows, transposed=False):
    first = lax.broadcasted_iota(jnp.int32, (rows, rows), 0)
    second = lax.broadcasted_iota(jnp.int32, (rows, rows), 1)
    return first <= second if transposed else second <= first


def pair_forward(extra, q, k, v, sk, sv, seg_q, seg_k, seg_sk, masks):
    low, high, inside = masks
    rows = q(0).shape[0]
    zero = jnp.zeros((rows, LANES), bf16)
    tri = causal(rows)

    def heads_of(value):
        scaled = value * jnp.asarray(0.125, bf16)
        return jnp.where(low, scaled, zero), jnp.where(high, scaled, zero)

    def clean(value):
        return jnp.where(inside, value, zero)

    def unit(q_heads, keys, values, allowed, state):
        out = []
        for head in range(2):
            s = jnp.where(allowed, dot_nt(q_heads[head], keys), NEG_FILL)
            top = jnp.max(s, axis=1, keepdims=True)
            if state is None:
                p = jnp.exp(s - top)
                out.append((top, jnp.sum(p, axis=1, keepdims=True), dot_nn(p.astype(bf16), values)))
            else:
                m, l, acc = state[head]
                new = jnp.maximum(m, top)
                scale = jnp.exp(m - new)
                p = jnp.exp(s - new)
                out.append(
                    (
                        new,
                        l * scale + jnp.sum(p, axis=1, keepdims=True),
                        acc * scale + dot_nn(p.astype(bf16), values),
                    )
                )
        return out

    more = unit(
        heads_of(q(extra)), clean(sk(extra)), clean(sv(extra)), seg_sk(extra) == seg_q(extra), None
    )
    results = []
    for slot in range(2):
        here = extra == slot
        state = [
            (jnp.where(here, m, NEG_FILL), jnp.where(here, l, 0.0), jnp.where(here, acc, 0.0))
            for m, l, acc in more
        ]
        q_heads = heads_of(q(slot))
        state = unit(
            q_heads, clean(k(slot)), clean(v(slot)), (seg_k(slot) == seg_q(slot)) & tri, state
        )
        if slot == 1:
            state = unit(q_heads, clean(k(0)), clean(v(0)), seg_k(0) == seg_q(1), state)
            state = unit(q_heads, clean(sk(0)), clean(sv(0)), seg_sk(0) == seg_q(1), state)
        (m0, l0, a0), (m1, l1, a1) = state
        results.append(
            (jnp.where(low, a0 / l0, a1 / l1), jnp.where(low, m0 + jnp.log(l0), m1 + jnp.log(l1)))
        )
    return results


def pair_backward(extra, q, k, v, sk, sv, g, o, lse, seg_q, seg_k, seg_sk, masks):
    low, high, inside = masks
    rows = q(0).shape[0]
    zero = jnp.zeros((rows, LANES), bf16)
    tri = causal(rows, transposed=True)

    def halves(value):
        return jnp.where(low, value, zero), jnp.where(high, value, zero)

    def queries(slot):
        grad = g(slot)
        product = jnp.where(inside, grad.astype(f32) * o(slot), 0.0).T
        sums = jnp.where(inside, lse(slot), 0.0).T
        return (
            halves(q(slot) * jnp.asarray(0.125, bf16)),
            halves(grad),
            (
                jnp.sum(product[:HEAD_DIM], axis=0, keepdims=True),
                jnp.sum(product[HEAD_DIM:], axis=0, keepdims=True),
            ),
            (sums[0:1], sums[HEAD_DIM : HEAD_DIM + 1]),
        )

    def unit(side, keys, values, allowed):
        q_heads, g_heads, delta, logs = side
        keys, values = jnp.where(inside, keys, zero), jnp.where(inside, values, zero)
        k_heads = halves(keys)
        dq = dk = dv = None
        for head in range(2):
            s = jnp.where(allowed, dot_nt(keys, q_heads[head]), NEG_FILL)
            p = jnp.exp(s - logs[head])
            ds = (p * (dot_nt(values, g_heads[head]) - delta[head])).astype(bf16)
            terms = (
                dot_tn(ds, k_heads[head]),
                dot_nn(ds, q_heads[head]),
                dot_nn(p.astype(bf16), g_heads[head]),
            )
            dq, dk, dv = terms if dq is None else (dq + terms[0], dk + terms[1], dv + terms[2])
        return dq, dk, dv

    sides = [queries(0), queries(1)]
    first = unit(sides[0], k(0), v(0), (seg_k(0) == seg_q(0)) & tri)
    second = unit(sides[1], k(1), v(1), (seg_k(1) == seg_q(1)) & tri)
    third = unit(sides[1], k(0), v(0), seg_k(0) == seg_q(1))
    fourth = unit(sides[1], sk(0), sv(0), seg_sk(0) == seg_q(1))
    fifth = unit(queries(extra), sk(extra), sv(extra), seg_sk(extra) == seg_q(extra))
    at_one = extra == 1

    def when(flag, value):
        return jnp.where(flag, value, 0.0)

    dq0 = first[0] + when(~at_one, fifth[0])
    dq1 = second[0] + third[0] + fourth[0] + when(at_one, fifth[0])
    own = [(first[1] + third[1], first[2] + third[2]), second[1:]]
    other = [
        tuple(fourth[i] + when(~at_one, fifth[i]) for i in (1, 2)),
        tuple(when(at_one, fifth[i]) for i in (1, 2)),
    ]
    return (dq0 * 0.125, dq1 * 0.125), own, other


def feed_in(normed, weight, bias, groups):
    tokens, width = normed.shape
    parts, _, n = weight.shape
    ratio = parts // groups

    def kernel(x_ref, w_ref, b_ref, inner_ref, act_ref):
        place = lax.rem(pl.program_id(0), ratio)
        u = dot_nn(x_ref[...], w_ref[0]) + b_ref[0]
        act = (0.5 * u * (1.0 + jnp.tanh(GELU_C * (u + GELU_A * u * u * u)))).astype(bf16)
        for r in range(ratio):

            @pl.when(place == r)
            def _():
                inner_ref[0, :, r * n : (r + 1) * n] = u
                act_ref[0, :, r * n : (r + 1) * n] = act

    out = pl.BlockSpec((1, tokens, ratio * n), lambda d: (d // ratio, 0, 0))
    return pl.pallas_call(
        kernel,
        grid=(parts,),
        in_specs=[
            pl.BlockSpec((tokens, width), lambda d: (0, 0)),
            pl.BlockSpec((1, width, n), lambda d: (d, 0, 0)),
            pl.BlockSpec((1, 1, n), lambda d: (d, 0, 0)),
        ],
        out_specs=[out, out],
        out_shape=[
            jax.ShapeDtypeStruct((groups, tokens, ratio * n), f32),
            jax.ShapeDtypeStruct((groups, tokens, ratio * n), bf16),
        ],
        compiler_params=params(),
        cost_estimate=cost(2 * tokens * width * parts * n, 2 * width * parts * n),
        name="fc",
    )(normed, weight, bias)


def feed_out(act, weight, hidden, bias):
    groups, tokens, f = act.shape
    width = weight.shape[1]

    def kernel(a_ref, w_ref, h_ref, b_ref, o_ref, acc_ref):
        step = pl.program_id(0)

        @pl.when(step == 0)
        def _():
            acc_ref[...] = h_ref[...] + b_ref[...]

        acc_ref[...] += dot_nt(a_ref[0], w_ref[0])

        @pl.when(step == groups - 1)
        def _():
            o_ref[...] = acc_ref[...].astype(bf16)

    return pl.pallas_call(
        kernel,
        grid=(groups,),
        in_specs=[
            pl.BlockSpec((1, tokens, f), lambda c: (c, 0, 0)),
            pl.BlockSpec((1, width, f), lambda c: (c, 0, 0)),
            pl.BlockSpec((tokens, width), lambda c: (0, 0)),
            pl.BlockSpec((1, width), lambda c: (0, 0)),
        ],
        out_specs=pl.BlockSpec((tokens, width), lambda c: (0, 0)),
        out_shape=jax.ShapeDtypeStruct((tokens, width), bf16),
        scratch_shapes=[pltpu.VMEM((tokens, width), f32)],
        compiler_params=params(),
        cost_estimate=cost(2 * groups * tokens * width * f, 2 * groups * width * f),
        name="proj",
    )(act, weight, hidden, bias)


def feed_back(grad, weight, inner, parts):
    groups, tokens, f = inner.shape
    width = weight.shape[1]
    ratio = parts // groups
    n = f // ratio

    def kernel(g_ref, w_ref, u_ref, o_ref, s_ref):
        u = u_ref[0]
        t = jnp.tanh(GELU_C * (u + GELU_A * u * u * u))
        slope = 0.5 * (1.0 + t) + 0.5 * u * (1.0 - t * t) * (
            GELU_C * (1.0 + 3.0 * GELU_A * u * u)
        )
        out = (dot_nn(g_ref[...], w_ref[0]) * slope).astype(bf16)
        total = jnp.sum(out.astype(f32), axis=0, keepdims=True)
        for r in range(ratio):
            o_ref[r] = out[:, r * n : (r + 1) * n]
            s_ref[r] = total[:, r * n : (r + 1) * n]

    return pl.pallas_call(
        kernel,
        grid=(groups,),
        in_specs=[
            pl.BlockSpec((tokens, width), lambda c: (0, 0)),
            pl.BlockSpec((1, width, f), lambda c: (c, 0, 0)),
            pl.BlockSpec((1, tokens, f), lambda c: (c, 0, 0)),
        ],
        out_specs=[
            pl.BlockSpec((ratio, tokens, n), lambda c: (c, 0, 0)),
            pl.BlockSpec((ratio, 1, n), lambda c: (c, 0, 0)),
        ],
        out_shape=[
            jax.ShapeDtypeStruct((parts, tokens, n), bf16),
            jax.ShapeDtypeStruct((parts, 1, n), f32),
        ],
        compiler_params=params(),
        cost_estimate=cost(2 * groups * tokens * width * f, 6 * groups * width * f),
        name="act_bwd",
    )(grad, weight, inner)


def back_project(grads, weight):
    parts, tokens, n = grads.shape
    width = weight.shape[1]

    def kernel(g_ref, w_ref, o_ref):
        @pl.when(pl.program_id(0) == 0)
        def _():
            o_ref[...] = dot_nt(g_ref[0], w_ref[0])

        @pl.when(pl.program_id(0) > 0)
        def _():
            o_ref[...] += dot_nt(g_ref[0], w_ref[0])

    return pl.pallas_call(
        kernel,
        grid=(parts,),
        in_specs=[
            pl.BlockSpec((1, tokens, n), lambda d: (d, 0, 0)),
            pl.BlockSpec((1, width, n), lambda d: (d, 0, 0)),
        ],
        out_specs=pl.BlockSpec((tokens, width), lambda d: (0, 0)),
        out_shape=jax.ShapeDtypeStruct((tokens, width), f32),
        compiler_params=params(),
        cost_estimate=cost(2 * parts * tokens * width * n, 2 * parts * width * n),
        name="back",
    )(grads, weight)


def weight_grad(left, right, picks, arrived=None):
    rows, tokens = left.shape
    n = right.shape[2]
    count = picks.shape[0]

    def kernel(picks_ref, a_ref, b_ref, *refs):
        y = dot_nn(a_ref[...], b_ref[0])
        if arrived is not None:
            y = y + refs[0][0].astype(f32)
        refs[-1][0] = y.astype(bf16)

    block = pl.BlockSpec((1, rows, n), lambda j, picks: (j, 0, 0))
    return pl.pallas_call(
        kernel,
        grid_spec=pltpu.PrefetchScalarGridSpec(
            num_scalar_prefetch=1,
            grid=(count,),
            in_specs=[
                pl.BlockSpec((rows, tokens), lambda j, picks: (0, 0)),
                pl.BlockSpec((1, tokens, n), lambda j, picks: (picks[j], 0, 0)),
            ]
            + ([block] if arrived is not None else []),
            out_specs=block,
        ),
        out_shape=jax.ShapeDtypeStruct((count, rows, n), bf16),
        compiler_params=params(),
        cost_estimate=cost(2 * count * rows * tokens * n, 2 * count * rows * n),
        name="wgrad",
    )(picks, left, right, *(() if arrived is None else (arrived,)))


MESH = pl.DeviceIdType.MESH


def far_first(k, z, nz):
    low = z < nz // 2
    me = jnp.where(low, z, nz - 1 - z)
    got = jnp.where(k < nz - 1 - me, nz - 1 - k, jnp.where(k == nz - 1, me, nz - 2 - k))
    return jnp.where(low, got, nz - 1 - got)


def summed_grads(grid, collective_id, operands, unit, shape, cut, name):
    rows, n = shape
    ra, rb = cut, rows - cut
    nz = grid.nz
    count = len(operands)

    def kernel(*refs):
        ins, out = refs[:count], refs[count]
        (sa, sb, ga, gb, oa, ob, xa, yb, ta, tb, ya, xb, la, lb, za, zb, ua, ub, da, db, ss, rs, zr) = refs[count + 1 :]
        d, c = lax.axis_index("dp"), lax.axis_index("ctx")
        z, y = d // grid.ny, d % grid.ny
        x, core = c // 2, c % 2
        at_sib = (d, c + 1 - 2 * core)
        at_x = (d, (1 - x) * 2 + core)
        at_y = (z * grid.ny + 1 - y, c)
        at_up = ((z + 1) * grid.ny + y, c)
        at_down = ((z - 1) * grid.ny + y, c)
        has_up, has_down = z < nz - 1, z > 0

        barrier = pltpu.get_barrier_semaphore()
        for target in (at_sib, at_x, at_y):
            pl.semaphore_signal(barrier, inc=1, device_id=target, device_id_type=MESH)

        @pl.when(has_up)
        def _():
            pl.semaphore_signal(barrier, inc=1, device_id=at_up, device_id_type=MESH)

        @pl.when(has_down)
        def _():
            pl.semaphore_signal(barrier, inc=1, device_id=at_down, device_id_type=MESH)

        pl.semaphore_wait(barrier, 3 + has_up.astype(jnp.int32) + has_down.astype(jnp.int32))

        def copy(src, dst, kind, k, target):
            return pltpu.make_async_remote_copy(
                src_ref=src,
                dst_ref=dst,
                send_sem=ss.at[kind, k],
                recv_sem=rs.at[kind, k],
                device_id=target,
                device_id_type=MESH,
            )

        def sib(k):
            s = k % 2
            return copy(sa.at[s], ga.at[k], 0, k, at_sib), copy(sb.at[s], gb.at[k], 1, k, at_sib)

        def first(k):
            s = k % 2
            return (
                copy(oa.at[s, 1 - x], xa.at[k], 2, k, at_x),
                copy(ob.at[s, 1 - y], yb.at[k], 3, k, at_y),
            )

        def second(k):
            s = k % 2
            return copy(ta.at[s], ya.at[k], 4, k, at_y), copy(tb.at[s], xb.at[k], 5, k, at_x)

        def line(k, to, up):
            dst = (ua, ub) if up else (da, db)
            target = at_up if up else at_down
            way = 0 if up else 1
            return [
                pltpu.make_async_remote_copy(
                    src_ref=(za, zb)[h].at[k],
                    dst_ref=dst[h].at[to],
                    send_sem=ss.at[6 + h, k],
                    recv_sem=zr.at[way, h, to],
                    device_id=target,
                    device_id_type=MESH,
                )
                for h in range(2)
            ]

        def step(t, _):
            @pl.when(t < nz)
            def _():
                k, s = t, t % 2
                to = far_first(k, z, nz)

                @pl.when(k >= 2)
                def _():
                    for cp in sib(k - 2):
                        cp.wait_send()
                    for cp in first(k - 2):
                        cp.wait_send()

                def store_sib(y_to, x_to, value):
                    sa[s, x_to, y_to] = value[:ra].astype(bf16)
                    sb[s, y_to, x_to] = value[ra:].astype(bf16)

                unit(ins, 1 - core, to, store_sib)
                for cp in sib(k):
                    cp.start()
                waits = sib(k)
                done = []

                def store_own(y_to, x_to, value):
                    if not done:
                        done.append(True)
                        for cp in waits:
                            cp.wait_recv()
                    oa[s, x_to, y_to] = (value[:ra] + ga[k, x_to, y_to].astype(f32)).astype(bf16)
                    ob[s, y_to, x_to] = (value[ra:] + gb[k, y_to, x_to].astype(f32)).astype(bf16)

                unit(ins, core, to, store_own)
                for cp in first(k):
                    cp.start()

            @pl.when((t >= 1) & (t <= nz))
            def _():
                k, s = t - 1, (t - 1) % 2

                @pl.when(k >= 2)
                def _():
                    for cp in second(k - 2):
                        cp.wait_send()

                one, two = first(k)
                one.wait_recv()
                ta[s] = (oa[s, x, 1 - y].astype(f32) + xa[k, 1 - y].astype(f32)).astype(bf16)
                go_a, go_b = second(k)
                go_a.start()
                la[s] = oa[s, x, y].astype(f32) + xa[k, y].astype(f32)
                two.wait_recv()
                tb[s] = (ob[s, y, 1 - x].astype(f32) + yb[k, 1 - x].astype(f32)).astype(bf16)
                go_b.start()
                lb[s] = ob[s, y, x].astype(f32) + yb[k, x].astype(f32)

            @pl.when(t >= 2)
            def _():
                k, s = t - 2, t % 2
                to = far_first(k, z, nz)
                one, two = second(k)
                one.wait_recv()
                two.wait_recv()
                la[s] = la[s] + ya[k].astype(f32)
                lb[s] = lb[s] + xb[k].astype(f32)
                for up in (True, False):
                    behind = has_down if up else has_up

                    @pl.when(((to > z) if up else (to < z)) & behind)
                    def _():
                        for cp in line(k, to, up):
                            cp.wait_recv()
                        la[s] = la[s] + (ua, da)[0 if up else 1][to].astype(f32)
                        lb[s] = lb[s] + (ub, db)[0 if up else 1][to].astype(f32)

                    @pl.when((to > z) if up else (to < z))
                    def _():
                        za[k] = la[s].astype(bf16)
                        zb[k] = lb[s].astype(bf16)
                        for cp in line(k, to, up):
                            cp.start()

            return 0

        lax.fori_loop(0, nz + 2, step, 0)
        last = (nz - 1) % 2
        for up in (True, False):

            @pl.when(has_down if up else has_up)
            def _():
                for cp in line(nz - 1, z, up):
                    cp.wait_recv()
                la[last] = la[last] + (ua, da)[0 if up else 1][z].astype(f32)
                lb[last] = lb[last] + (ub, db)[0 if up else 1][z].astype(f32)

        out[:ra] = la[last]
        out[ra:] = lb[last]
        for k in range(nz - 2, nz):
            for cp in (*sib(k), *first(k), *second(k)):
                cp.wait_send()
        for k in range(nz - 1):
            for cp in line(k, 0, True):
                cp.wait_send()

    def vm(*dims, dtype=bf16):
        return pltpu.VMEM(dims, dtype)

    halves = [
        *(vm(2, 2, 2, h, n) for h in (ra, rb)),
        *(vm(nz, 2, 2, h, n) for h in (ra, rb)),
        *(vm(2, 2, 2, h, n) for h in (ra, rb)),
        *(vm(nz, 2, h, n) for h in (ra, rb)),
        *(vm(2, h, n) for h in (ra, rb)),
        *(vm(nz, h, n) for h in (ra, rb)),
        *(vm(2, h, n, dtype=f32) for h in (ra, rb)),
        *(vm(nz, h, n) for h in (ra, rb)),
        *(vm(nz, h, n) for h in (ra, rb)),
        *(vm(nz, h, n) for h in (ra, rb)),
    ]
    flops = sum(2 * 2 * 2 * nz * grid.ny * rows * n * 512 for _ in range(1))
    return pl.pallas_call(
        kernel,
        out_shape=jax.ShapeDtypeStruct((rows, n), f32),
        in_specs=[pl.BlockSpec(memory_space=pltpu.VMEM)] * count,
        out_specs=pl.BlockSpec(memory_space=pltpu.VMEM),
        scratch_shapes=[
            *halves,
            pltpu.SemaphoreType.DMA((8, nz)),
            pltpu.SemaphoreType.DMA((6, nz)),
            pltpu.SemaphoreType.DMA((2, 2, nz)),
        ],
        compiler_params=pltpu.CompilerParams(
            collective_id=collective_id, has_side_effects=True, vmem_limit_bytes=VMEM_LIMIT
        ),
        cost_estimate=cost(flops, 100_000_000),
        name=name,
    )(*operands)


def near_first(k, z, nz):
    return far_first(nz - 1 - k, z, nz)


def forward_gather(grid, x_in, g_in, weights, vectors, seg_col, seg_row, seg_other):
    _, rows, width = x_in.shape
    tokens = 2 * rows
    nz = grid.nz
    parts, groups = grid.dp, grid.ctx
    wide = pl.cdiv(width, LANES) * LANES
    pairs = wide // LANES
    n_qkv, n_out, n_fc = (w.shape[1] for w in weights[:3])
    slab = weights[0].shape[0]
    ff = weights[3].shape[1]
    n_vec = vectors.shape[1]
    n_bias = n_out
    n_slots = 4 * nz

    def kernel(
        x_own, g_own, wq_in, wo_in, wf_in, wp_in, vec_in, sc_ref, sr_ref, so_ref,
        gq, go, gf, gp, vec_out, slope_out, act_out, sib_out, x_out, g_out, n1t_out, n2t_out, att_out, dw_out,
        q_out, k_out, v_out, of_out, lse_out, hid_out,
        q_ref, k_ref, v_ref, of_ref, lse_ref, hid_ref, x_ref, n1_ref, att_ref, flip, sib, vbuf, rowbuf, jrow, wqkv, wbig, wout, stage_u, stage_a, stage_w, mq, mo, mf, mp,
        s_z, r_z, s_p, r_p, s_vz, r_vz, s_vy, r_vy, s_kv, r_kv, s_loc, s_w, s_st, s_sh, r_sh, s_fl, s_out, s_dw,
    ):
        d, c = lax.axis_index("dp"), lax.axis_index("ctx")
        z, y = d // grid.ny, d % grid.ny
        x, core = c // 2, c % 2
        extra = 1 - core
        at_sib = (d, c + 1 - 2 * core)
        at_x = (d, (1 - x) * 2 + core)
        at_y = (z * grid.ny + 1 - y, c)
        at_up = ((z + 1) * grid.ny + y, c)
        at_down = ((z - 1) * grid.ny + y, c)
        has_up, has_down = z < nz - 1, z > 0
        gathered = (gq, go, gf, gp)
        mine = (mq, mo, mf, mp)
        cuts = [(w.shape[0] * 2 // 5 + 7) // 8 * 8 for w in weights]
        at_cross = (d, (1 - x) * 2 + 1 - core)
        n2_ref = n1_ref

        def piece(w, zz, yy, xx, cc, half=None):
            h = weights[w].shape[0]
            tail = () if half is None else ((pl.ds(0, cuts[w]) if half == 0 else pl.ds(cuts[w], h - cuts[w])),)
            index = (zz, yy, xx, cc) if w < 3 else (xx, cc, zz, yy)
            return gathered[w].at[(*index, *tail)]

        def remote(src, dst, send, recv, target):
            return pltpu.make_async_remote_copy(
                src_ref=src, dst_ref=dst, send_sem=send, recv_sem=recv, device_id=target, device_id_type=MESH
            )

        every = slice(None)

        def part_copy(w, kind, j):
            zz = near_first(j, z, nz)
            src, target = (
                (piece(w, zz, y, x, core, 0), at_y),
                (piece(w, zz, y, x, core, 1), at_x),
                (piece(w, zz, every, x, core, 0), at_x),
                (piece(w, zz, y, every, core, 1), at_y),
                (piece(w, zz, every, every, core), at_sib),
            )[kind]
            return remote(src, src, s_p.at[w, kind, j], r_p.at[w, kind, j], target)

        def z_copy(w, zz, way, j):
            src = piece(w, zz, y, x, core)
            return remote(src, src, s_z.at[w, way, j], r_z.at[w, zz], (at_up, at_down)[way])

        def vz_copy(zz, way, j):
            src = vbuf.at[zz, y]
            return remote(src, src, s_vz.at[way, j], r_vz.at[zz], (at_up, at_down)[way])

        def vy_copy(j):
            src = vbuf.at[near_first(j, z, nz), y]
            return remote(src, src, s_vy.at[j], r_vy.at[j], at_y)

        def passes_on(j):
            zz = near_first(j, z, nz)
            return zz, (zz < z) & has_up, (zz > z) & has_down

        def z_arrived(w, j):
            zz = near_first(j, z, nz)
            z_copy(w, zz, 0, j).wait_recv()
            if w == 0:
                vz_copy(zz, 0, j).wait_recv()

        def z_send(w, zz, way, j):
            z_copy(w, zz, way, j).start()
            if w == 0:
                vz_copy(zz, way, j).start()

        def pass_on(i):
            w, j = divmod(i, nz)
            if j == 0:

                @pl.when(has_up)
                def _():
                    z_send(w, z, 0, 0)

                @pl.when(has_down)
                def _():
                    z_send(w, z, 1, 0)

                return
            zz, up, down = passes_on(j)
            for way, flag in ((0, up), (1, down)):

                @pl.when(flag)
                def _():
                    z_arrived(w, j)
                    z_send(w, zz, way, j)

        def across(kind, p, target):
            src, dst = moved[kind]
            at = pl.ds(p * (rows // nz), rows // nz)
            return remote(src.at[1 - x, at], dst.at[x, at], s_sh.at[kind, p], r_sh.at[kind, p], target)

        def within(kind):
            src, dst = moved[kind]
            return remote(src.at[1], dst.at[1], s_sh.at[kind, nz], r_sh.at[kind, nz], at_sib)

        def stays(kind):
            src, dst = moved[kind]
            return pltpu.make_async_copy(src.at[0], dst.at[0], s_sh.at[kind, nz])

        moved = ((x_own, x_ref), (g_own, g_out))

        def move(kind, p):
            @pl.when(x == 0)
            def _():
                across(kind, p, at_x).start()
                if p == 0:
                    stays(kind).start()

            @pl.when(x == 1)
            def _():
                across(kind, p, at_cross).start()
                if p == 0:
                    within(kind).start()

        def moved_in(kind):
            for p in range(nz):
                across(kind, p, at_x).wait_recv()

            @pl.when(x == 0)
            def _():
                stays(kind).wait()

            @pl.when(x == 1)
            def _():
                within(kind).wait_recv()

        def moved_out(kind):
            for p in range(nz):
                across(kind, p, at_x).wait_send()

            @pl.when(x == 1)
            def _():
                within(kind).wait_send()

        def tick(i):
            if i < n_slots:
                w, j = divmod(i, nz)
                if j > 0:
                    _, up, down = passes_on(j)

                    @pl.when(jnp.logical_not(up | down))
                    def _():
                        z_arrived(w, j)

                part_copy(w, 0, j).start()
                part_copy(w, 1, j).start()
                if w == 0:
                    vy_copy(j).start()
            if 0 <= i - 1 < n_slots:
                w, j = divmod(i - 1, nz)
                part_copy(w, 0, j).wait_recv()
                part_copy(w, 2, j).start()
                part_copy(w, 1, j).wait_recv()
                part_copy(w, 3, j).start()
            if 0 <= i - 2 < n_slots:
                w, j = divmod(i - 2, nz)
                part_copy(w, 2, j).wait_recv()
                part_copy(w, 3, j).wait_recv()
                part_copy(w, 4, j).start()
            if i + 1 < n_slots and (i + 1) % nz != 0:
                pass_on(i + 1)
            if i % nz == 1 and i + nz - 1 < n_slots:
                pass_on(i + nz - 1)
            if i // nz in (0, 2):
                move(i // nz // 2, i % nz)

        def complete(w):
            for j in range(nz):
                part_copy(w, 4, j).wait_recv()

        barrier = pltpu.get_barrier_semaphore()
        for target in (at_sib, at_x, at_y, at_cross):
            pl.semaphore_signal(barrier, inc=1, device_id=target, device_id_type=MESH)

        @pl.when(has_up)
        def _():
            pl.semaphore_signal(barrier, inc=1, device_id=at_up, device_id_type=MESH)

        @pl.when(has_down)
        def _():
            pl.semaphore_signal(barrier, inc=1, device_id=at_down, device_id_type=MESH)

        sources = (wq_in, wo_in, wf_in, wp_in)
        into = [pltpu.make_async_copy(src, mine[w], s_loc.at[w]) for w, src in enumerate(sources)]
        into.append(pltpu.make_async_copy(vec_in, vbuf.at[z, y], s_loc.at[4]))
        for cp in into:
            cp.start()
        for ref in (q_ref, k_ref, v_ref):
            ref[:, :, wide - LANES :] = jnp.zeros((2, rows, LANES), bf16)
        jrow[...] = jnp.zeros_like(jrow)
        for cp in into:
            cp.wait()
        local = [
            pltpu.make_async_copy(mine[w], piece(w, z, y, x, core), s_loc.at[w]) for w in range(4)
        ]
        for cp in local:
            cp.start()
        for cp in local:
            cp.wait()
        pl.semaphore_wait(barrier, 4 + has_up.astype(jnp.int32) + has_down.astype(jnp.int32))

        pass_on(0)
        for i in range(nz + 1):
            tick(i)
        moved_in(0)
        keep_x = pltpu.make_async_copy(x_ref, x_out, s_loc.at[2])
        keep_x.start()
        for j in range(nz):
            vy_copy(j).wait_recv()

        for part in range(parts):
            line = vbuf[part // grid.ny, part % grid.ny]
            cols = slice(part * n_bias, (part + 1) * n_bias)
            for v in range(8):
                term = line[0:1, n_fc + v * n_bias : n_fc + (v + 1) * n_bias]
                if v < 2:
                    jrow[0:1, 2 * v * width + cols.start : 2 * v * width + cols.stop] = term
                else:
                    rowbuf[v : v + 1, cols] = term
        for s in range(2):
            values = x_ref[s].astype(f32)
            n1_ref[s] = layer_norm(values, rowbuf[4:5, :], rowbuf[5:6, :]).astype(bf16)

        for i in range(nz + 1, nz + 3):
            tick(i)

        def flipped(dst):
            return pltpu.make_async_copy(flip, dst, s_fl.at[0])

        def turn(value, dst, before):
            if before is not None:
                flipped(before).wait()
            flip[...] = value.T
            flipped(dst).start()

        turn(n1_ref[...].reshape(tokens, width), n1t_out, None)
        complete(0)

        def stream(source, buffer, body, hooks):
            def load(part):
                return pltpu.make_async_copy(
                    source.at[part // grid.ny, part % grid.ny], buffer.at[part % 2], s_w.at[part % 2]
                )

            load(0).start()

            def step(part, _):
                load(part).wait()

                @pl.when(part + 1 < parts)
                def _():
                    load(part + 1).start()

                body(part, part % 2)
                for when, todo in hooks.items():

                    @pl.when(part == when)
                    def _():
                        for i in todo:
                            tick(i)

                return 0

            lax.fori_loop(0, parts, step, 0)

        def project(part, slot):
            left = n1_ref[...].reshape(tokens, width)
            product = dot_nn(left, wqkv[slot].reshape(width, n_qkv))
            for p in range(parts):

                @pl.when(part == p)
                def _():
                    first, last = p * n_qkv, (p + 1) * n_qkv
                    out = (product + jrow[0:1, first:last]).astype(bf16).reshape(2, rows, n_qkv)
                    for g, ref in enumerate((q_ref, k_ref, v_ref)):
                        lo, hi = max(first, g * width), min(last, (g + 1) * width)
                        if lo < hi:
                            ref[:, :, lo - g * width : hi - g * width] = out[:, :, lo - first : hi - first]

        stream(gq, wqkv, project, {0: [nz + 3], 4: [nz + 4]})
        swaps = [
            remote(ref, sib.at[kind], s_kv.at[kind], r_kv.at[kind], at_sib)
            for kind, ref in enumerate((k_ref, v_ref))
        ]
        results = (
            (q_ref, q_out), (k_ref, k_out), (v_ref, v_out), (of_ref, of_out), (lse_ref, lse_out), (hid_ref, hid_out)
        )
        saved = [pltpu.make_async_copy(src, dst, s_out.at[i]) for i, (src, dst) in enumerate(results)]
        for cp in (*swaps, *saved[:3]):
            cp.start()
        for cp in swaps:
            cp.wait_recv()
        tick(nz + 5)

        def attend(p, _):
            lanes = pl.ds(pl.multiple_of(p * LANES, LANES), LANES)
            got = pair_forward(
                extra,
                lambda i: q_ref[i, :, lanes],
                lambda i: k_ref[i, :, lanes],
                lambda i: v_ref[i, :, lanes],
                lambda i: sib[0, i, :, lanes],
                lambda i: sib[1, i, :, lanes],
                lambda i: sc_ref[i],
                lambda i: sr_ref[i],
                lambda i: so_ref[i],
                pair_masks(p, width),
            )
            for slot, (out, logs) in enumerate(got):
                att_ref[slot, :, lanes] = out.astype(bf16)
                of_ref[slot, :, lanes] = out
                lse_ref[slot, :, lanes] = logs

            @pl.when(p == pairs // 2)
            def _():
                tick(nz + 6)

            return 0

        lax.fori_loop(0, pairs, attend, 0)
        keep = pltpu.make_async_copy(sib, sib_out, s_loc.at[0])
        for cp in (keep, *saved[3:5]):
            cp.start()
        complete(1)
        turn(att_ref[:, :, :width].reshape(tokens, width), att_out, n1t_out)

        def branch(part, slot):
            product = dot_nn(
                att_ref[:, :, :width].reshape(tokens, width), wout[slot].reshape(width, n_out)
            ).reshape(2, rows, n_out)
            for p in range(parts):

                @pl.when(part == p)
                def _():
                    hid_ref[:, :, p * n_out : (p + 1) * n_out] = product

        stream(go, wout, branch, {0: [nz + 7]})
        for s in range(2):
            hidden = x_ref[s].astype(f32) + hid_ref[s] + rowbuf[2:3, :]
            hid_ref[s] = hidden
            n2_ref[s] = layer_norm(hidden, rowbuf[6:7, :], rowbuf[7:8, :]).astype(bf16)
        saved[5].start()
        tick(nz + 8)
        turn(n2_ref[...].reshape(tokens, width), n2t_out, att_out)
        tick(nz + 9)
        moved_in(1)
        for half in range(2):
            fetch = pltpu.make_async_copy(
                g_out.at[half], stage_a.at[0, pl.ds(half * rows, rows)], s_loc.at[3]
            )
            fetch.start()
            fetch.wait()
        flipped(n2t_out).wait()
        flip[...] = stage_a[0].T
        complete(2)
        band = width // nz

        def save_w(i):
            return pltpu.make_async_copy(
                stage_w.at[i % 2], dw_out.at[i // nz, pl.ds(pl.multiple_of(i % nz * band, 16), band)], s_dw.at[i % 2]
            )

        def proj_terms(group):
            def body(i, _):
                @pl.when(i >= 2)
                def _():
                    save_w(i - 2).wait()

                at = pl.ds(pl.multiple_of(i % nz * band, 16), band)
                stage_w[i % 2] = dot_nn(flip[at, :], stage_a[group % 2]).astype(bf16)
                save_w(i).start()
                return 0

            lax.fori_loop(group * nz, (group + 1) * nz, body, 0)

        ratio = parts // groups

        def saves(group):
            slot = group % 2
            return (
                pltpu.make_async_copy(stage_u.at[slot], slope_out.at[group], s_st.at[0, slot]),
                pltpu.make_async_copy(stage_a.at[slot], act_out.at[group], s_st.at[1, slot]),
            )

        def feed(part, slot):
            group, place = part // ratio, part % ratio

            @pl.when((place == 0) & (group >= 2))
            def _():
                for cp in saves(group - 2):
                    cp.wait()

            left = n2_ref[...].reshape(tokens, width)
            u = dot_nn(left, wbig[slot].reshape(width, n_fc))
            u = u + vbuf[part // grid.ny, part % grid.ny][0:1, :n_fc]
            t = jnp.tanh(GELU_C * (u + GELU_A * u * u * u))
            act = (0.5 * u * (1.0 + t)).astype(bf16)
            slope = 0.5 * (1.0 + t) + 0.5 * u * (1.0 - t * t) * (GELU_C * (1.0 + 3.0 * GELU_A * u * u))
            slope = slope.astype(bf16)
            for r in range(ratio):

                @pl.when(place == r)
                def _():
                    stage_u[group % 2, :, r * n_fc : (r + 1) * n_fc] = slope
                    stage_a[group % 2, :, r * n_fc : (r + 1) * n_fc] = act

            @pl.when(place == ratio - 1)
            def _():
                for cp in saves(group):
                    cp.start()
                proj_terms(group)

        stream(gf, wbig, feed, {0: [nz + 10], 3: [nz + 11], 6: [nz + 12]})
        tick(nz + 13)
        save_vec = pltpu.make_async_copy(vbuf, vec_out, s_loc.at[1])
        save_vec.start()
        for group in range(groups - 2, groups):
            for cp in saves(group):
                cp.wait()
        for i in range(groups * nz - 2, groups * nz):
            save_w(i).wait()
        for cp in (keep, keep_x, *saved):
            cp.wait()
        save_vec.wait()
        complete(3)
        for kind in range(2):
            moved_out(kind)
        for cp in swaps:
            cp.wait_send()

        def finish(j, _):
            zz, up, down = passes_on(j)
            up, down = up | ((j == 0) & has_up), down | ((j == 0) & has_down)
            vy_copy(j).wait_send()
            for w in range(4):
                for kind in range(5):
                    part_copy(w, kind, j).wait_send()
                for way, flag in ((0, up), (1, down)):

                    @pl.when(flag)
                    def _():
                        z_copy(w, zz, way, j).wait_send()
                        if w == 0:
                            vz_copy(zz, way, j).wait_send()

            return 0

        lax.fori_loop(0, nz, finish, 0)

    any_, vm = pl.BlockSpec(memory_space=pl.ANY), pl.BlockSpec(memory_space=pltpu.VMEM)
    dma = pltpu.SemaphoreType.DMA
    columns = [
        jax.ShapeDtypeStruct((nz, grid.ny, grid.nx, 2, *w.shape), bf16) for w in weights[:3]
    ]
    wide_low = jax.ShapeDtypeStruct((2, rows, wide), bf16)
    wide_full = jax.ShapeDtypeStruct((2, rows, wide), f32)
    low = jax.ShapeDtypeStruct((2, rows, width), bf16)
    out_shape = [
        *columns,
        jax.ShapeDtypeStruct((grid.nx, 2, nz, grid.ny, *weights[3].shape), bf16),
        jax.ShapeDtypeStruct((nz, grid.ny, 8, n_vec), f32),
        jax.ShapeDtypeStruct((groups, tokens, ff), bf16),
        jax.ShapeDtypeStruct((groups, tokens, ff), bf16),
        jax.ShapeDtypeStruct((2, 2, rows, wide), bf16),
        low,
        low,
        *[jax.ShapeDtypeStruct((width, tokens), bf16)] * 3,
        jax.ShapeDtypeStruct((groups, width, ff), bf16),
        wide_low,
        wide_low,
        wide_low,
        wide_full,
        wide_full,
        jax.ShapeDtypeStruct((2, rows, width), f32),
    ]
    return pl.pallas_call(
        kernel,
        out_shape=out_shape,
        in_specs=[any_] * 7 + [vm] * 3,
        out_specs=[any_] * 20,
        scratch_shapes=[
            *[pltpu.VMEM((2, rows, wide), bf16)] * 3,
            *[pltpu.VMEM((2, rows, wide), f32)] * 2,
            pltpu.VMEM((2, rows, width), f32),
            pltpu.VMEM((2, rows, width), bf16),
            pltpu.VMEM((2, rows, width), bf16),
            pltpu.VMEM((2, rows, wide), bf16),
            pltpu.VMEM((width, tokens), bf16),
            pltpu.VMEM((2, 2, rows, wide), bf16),
            pltpu.VMEM((nz, grid.ny, 8, n_vec), f32),
            pltpu.VMEM((8, width), f32),
            pltpu.VMEM((8, 3 * width), f32),
            pltpu.VMEM((2, grid.nx, 2, slab, n_qkv), bf16),
            pltpu.VMEM((2, grid.nx, 2, slab, n_fc), bf16),
            pltpu.VMEM((2, grid.nx, 2, slab, n_out), bf16),
            pltpu.VMEM((2, tokens, ff), bf16),
            pltpu.VMEM((2, tokens, ff), bf16),
            pltpu.VMEM((2, width // nz, ff), bf16),
            *(pltpu.VMEM(w.shape, bf16) for w in weights),
            dma((4, 2, nz)),
            dma((4, nz)),
            dma((4, 5, nz)),
            dma((4, 5, nz)),
            dma((2, nz)),
            dma((nz,)),
            dma((nz,)),
            dma((nz,)),
            dma((2,)),
            dma((2,)),
            dma((5,)),
            dma((2,)),
            dma((2, 2)),
            dma((2, nz + 1)),
            dma((2, nz + 1)),
            dma((1,)),
            dma((6,)),
            dma((2,)),
        ],
        compiler_params=pltpu.CompilerParams(
            collective_id=4, has_side_effects=True, vmem_limit_bytes=VMEM_LIMIT
        ),
        cost_estimate=cost(30e9, 150e6),
        name="forward",
    )(x_in, g_in, *weights, vectors, seg_col, seg_row, seg_other)


def backward_sums(
    grid, grad, proj_terms, act, slope, w_proj, hidden, normed_t, w_fc, w_out, queries, keys, values, other,
    att_full, logs, x_in, first_t, att_t, w_qkv, vec_rows, seg_row, seg_col, seg_other,
):
    tokens, width = grad.shape
    rows = tokens // 2
    nz, parts, groups = grid.nz, grid.dp, grid.ctx
    wide = queries.shape[2]
    pairs = wide // LANES
    ff, n_fc, n_out = act.shape[2], w_fc.shape[2], w_out.shape[2]
    n_qkv = 3 * width // parts
    slab = width // groups
    cols = width // parts
    ratio = parts // groups
    h, n = cols * 2 // 5 // 16 * 16, ff
    low_half = slab // 2
    v_rows = 8 + parts
    chunk = min(rows, 64)
    units = 3 * nz

    def kernel(
        g_in, dw_in, act_in, u_in, wp_in, hid_in, nt_in, wf_in, wo_in, q_in, k_in, v_in, s_in, of_in, lse_in,
        x_in, n1t_in, at_in, wq_in, vr_ref, rq_ref, ck_ref, cs_ref,
        gp_out, gf_out, gq_out, sum_ref, y_out, di_out, dx_out, hg_out, bg_out, pg_out, ig_out,
        sa, sb, ga, gb, oa, ob, xa, yb, ta, tb, ya, xb, la, lb, za, zb, ra, rb, swap, v_send, v_got,
        ss, rs, zss, zrs, s_ld, s_st, s_tile, s_kv, s_vec, r_vec, s_back, r_back, s_out, s_dw,
    ):
        d, c = lax.axis_index("dp"), lax.axis_index("ctx")
        z, y = d // grid.ny, d % grid.ny
        x, core = c // 2, c % 2
        extra = 1 - core
        at_sib = (d, c + 1 - 2 * core)
        at_x = (d, (1 - x) * 2 + core)
        at_y = (z * grid.ny + 1 - y, c)
        at_cross = (d, (1 - x) * 2 + 1 - core)
        at_up = ((z + 1) * grid.ny + y, c)
        at_down = ((z - 1) * grid.ny + y, c)
        has_up, has_down = z < nz - 1, z > 0

        def remote(src, dst, send, recv, target):
            return pltpu.make_async_remote_copy(
                src_ref=src, dst_ref=dst, send_sem=send, recv_sem=recv, device_id=target, device_id_type=MESH
            )

        def copy(src, dst, kind, u, target):
            return remote(src, dst, ss.at[kind, u], rs.at[kind, u], target)

        def sib(u):
            return copy(sa, ga.at[u % 2], 0, u, at_sib), copy(sb, gb.at[u % 2], 1, u, at_sib)

        def first(u):
            return copy(oa.at[1 - x], xa.at[u % 2], 2, u, at_x), copy(ob.at[1 - y], yb.at[u % 2], 3, u, at_y)

        def second(u):
            return copy(ta, ya.at[u % 3], 4, u, at_y), copy(tb, xb.at[u % 3], 5, u, at_x)

        def line(u, to, up, place):
            group, k = divmod(u, nz)
            target = at_up if up else at_down
            return [
                remote(
                    (za, zb)[i].at[min(k, nz - 2)],
                    (ra, rb)[i].at[group % 2, place],
                    zss.at[i, u],
                    zrs.at[i, group, place],
                    target,
                )
                for i in range(2)
            ]

        def add_arrived(u, place):
            for cp in line(u, 0, True, place):
                cp.wait_recv()
            la[u % 2] += ra[u // nz % 2, place].astype(f32)
            lb[u % 2] += rb[u // nz % 2, place].astype(f32)

        def target_z(u):
            return far_first(u % nz, z, nz)

        def finish(u):
            at_end = jnp.logical_not(has_up & has_down)

            @pl.when(jnp.logical_not(at_end))
            def _():
                finish_unit(u)

            @pl.when(at_end)
            def _():
                if u % nz == nz - 1:
                    finish_unit(u)
                if (u + 1) % nz != nz - 1:
                    finish_unit(u + 1)

        def finish_unit(u):
            if 0 <= u < units:
                to = target_z(u)
                for cp in second(u):
                    cp.wait_recv()
                la[u % 2] += ya[u % 3].astype(f32)
                lb[u % 2] += xb[u % 3].astype(f32)
                if u % nz == nz - 1:

                    @pl.when(has_down)
                    def _():
                        add_arrived(u, z)

                    @pl.when(has_up)
                    def _():
                        add_arrived(u, nz)

                    out = (gp_out, gf_out, gq_out)[u // nz]
                    done = [
                        pltpu.make_async_copy(src, out.at[at], s_out.at[i])
                        for i, (src, at) in enumerate(
                            ((la.at[u % 2], pl.ds(0, h)), (lb.at[u % 2], pl.ds(h, cols - h)))
                        )
                    ]
                    for cp in done:
                        cp.start()
                    for cp in done:
                        cp.wait()
                else:
                    for up in (True, False):
                        going = (to > z) if up else (to < z)

                        @pl.when(going & (has_down if up else has_up))
                        def _():
                            add_arrived(u, to)

                        @pl.when(going)
                        def _():
                            if u >= nz:
                                for cp in line(u - nz, 0, up, 0):
                                    cp.wait_send()
                            za[u % nz] = la[u % 2].astype(bf16)
                            zb[u % nz] = lb[u % 2].astype(bf16)
                            place = to if up else jnp.where(to == z - 1, nz, to)
                            for cp in line(u, to, up, place):
                                cp.start()

        def second_stage(u):
            if 0 <= u < units:
                if u >= 1:
                    for cp in second(u - 1):
                        cp.wait_send()
                for cp in first(u):
                    cp.wait_recv()
                s = u % 2
                go_a, go_b = second(u)
                ta[...] = oa[x, 1 - y] + xa[s, 1 - y]
                go_a.start()
                tb[...] = ob[y, 1 - x] + yb[s, 1 - x]
                go_b.start()
                la[s] = oa[x, y].astype(f32) + xa[s, y].astype(f32)
                lb[s] = ob[y, x].astype(f32) + yb[s, x].astype(f32)
        def give(u, unit):
            if u >= 1:
                for cp in sib(u - 1):
                    cp.wait_send()

            def store(y_to, x_to, value):
                sa[x_to, y_to] = value[:h].astype(bf16)
                sb[y_to, x_to] = value[h:].astype(bf16)

            if u < nz:
                take_terms(u, 1 - core, sa, sb)
            else:
                unit(target_z(u), 1 - core, store)
            for cp in sib(u):
                cp.start()

        def take_terms(u, plane, to_a, to_b):
            loads = []
            for y_to in range(2):
                first_row = pl.multiple_of((target_z(u) * grid.ny + y_to) * cols, 8)
                for x_to in range(2):
                    src = dw_in.at[2 * x_to + plane]
                    loads += [
                        pltpu.make_async_copy(
                            src.at[pl.ds(first_row, h)], to_a.at[x_to, y_to], s_dw.at[0, y_to, x_to]
                        ),
                        pltpu.make_async_copy(
                            src.at[pl.ds(pl.multiple_of(first_row + h, 8), cols - h)],
                            to_b.at[y_to, x_to],
                            s_dw.at[1, y_to, x_to],
                        ),
                    ]
            for cp in loads:
                cp.start()
            for cp in loads:
                cp.wait()

        def begin_unit(u, unit):
            if u < units:
                s = u % 2
                if u % nz == 0:
                    give(u, unit)
                if u >= 1:
                    for cp in first(u - 1):
                        cp.wait_send()
                if u < nz:
                    take_terms(u, core, oa, ob)
                for cp in sib(u):
                    cp.wait_recv()

                def store(y_to, x_to, value):
                    oa[x_to, y_to] = (value[:h] + ga[s, x_to, y_to].astype(f32)).astype(bf16)
                    ob[y_to, x_to] = (value[h:] + gb[s, y_to, x_to].astype(f32)).astype(bf16)

                if u < nz:
                    oa[...] = oa[...] + ga[s]
                    ob[...] = ob[...] + gb[s]
                else:
                    unit(target_z(u), core, store)
                for cp in first(u):
                    cp.start()
                if (u + 1) % nz != 0:
                    give(u + 1, unit)

        def tick(t, unit=None):
            finish(t - 3)
            second_stage(t - 1)
            begin_unit(t, unit)

        def beside(term):
            return jnp.concatenate([term[:low_half], term[low_half:]], axis=1)

        barrier = pltpu.get_barrier_semaphore()
        for target in (at_sib, at_x, at_y, at_cross):
            pl.semaphore_signal(barrier, inc=1, device_id=target, device_id_type=MESH)

        @pl.when(has_up)
        def _():
            pl.semaphore_signal(barrier, inc=1, device_id=at_up, device_id_type=MESH)

        @pl.when(has_down)
        def _():
            pl.semaphore_signal(barrier, inc=1, device_id=at_down, device_id_type=MESH)

        pl.semaphore_wait(barrier, 4 + has_up.astype(jnp.int32) + has_down.astype(jnp.int32))

        def back_far(kind, src, dst, target):
            return remote(src.at[1 - x], dst.at[x], s_back.at[kind, 0], r_back.at[kind, 0], target)

        def back_near(kind, src, dst):
            return remote(src.at[1], dst.at[1], s_back.at[kind, 1], r_back.at[kind, 1], at_sib)

        def back_stay(kind, src, dst):
            return pltpu.make_async_copy(src.at[0], dst.at[0], s_back.at[kind, 1])

        def give_back(kind, src, dst):
            @pl.when(x == 0)
            def _():
                back_far(kind, src, dst, at_cross).start()
                back_stay(kind, src, dst).start()

            @pl.when(x == 1)
            def _():
                back_far(kind, src, dst, at_x).start()
                back_near(kind, src, dst).start()

        def given_back(kind, src, dst):
            back_far(kind, src, dst, at_x).wait_send()

            @pl.when(x == 0)
            def _():
                back_stay(kind, src, dst).wait()

            @pl.when(x == 1)
            def _():
                back_near(kind, src, dst).wait_send()

        def got_back(kind, src, dst):
            back_far(kind, src, dst, at_x).wait_recv()

            @pl.when(x == 1)
            def _():
                back_near(kind, src, dst).wait_recv()

        def vec_copy(i, target):
            return remote(v_send.at[i], v_got.at[i], s_vec.at[i], r_vec.at[i], target)

        def vec_step(i):
            targets = (at_sib, at_x, at_y)
            if 1 <= i <= 3:
                vec_copy(i - 1, targets[i - 1]).wait()
                sum_ref[...] += v_got[i - 1]
            if i < 3:
                v_send[i] = sum_ref[...]
                vec_copy(i, targets[i]).start()
                return
            if i == 3:
                ways = ((3, has_up, has_down, at_up), (4, has_down, has_up, at_down))
                for slot, going, behind, target in ways:
                    v_send[slot] = sum_ref[...]

                    @pl.when(going & jnp.logical_not(behind))
                    def _():
                        vec_copy(slot, target).start()

                for slot, going, behind, target in ways:

                    @pl.when(behind)
                    def _():
                        vec_copy(slot, target).wait_recv()
                        v_send[slot] += v_got[slot]

                    @pl.when(going & behind)
                    def _():
                        vec_copy(slot, target).start()

                return
            for slot, going, behind, target in ((3, has_up, has_down, at_up), (4, has_down, has_up, at_down)):

                @pl.when(behind)
                def _():
                    sum_ref[...] += v_got[slot]

                @pl.when(going)
                def _():
                    vec_copy(slot, target).wait_send()

        def load(src, dst, sem):
            return pltpu.make_async_copy(src, dst, s_ld.at[sem])

        def first_phase(g, acts, w, u, ig_st, total):
            begin = load(g_in, g, 3)
            begin.start()
            tick(0)

            def fetch(group):
                return load(wp_in.at[group], w, 4), load(u_in.at[group], u, 5)

            for cp in fetch(0):
                cp.start()
            begin.wait()
            sum_ref[0:1, :] = jnp.sum(g[...].astype(f32), axis=0, keepdims=True)
            hid = load(hid_in, total, 6)
            hid.start()
            hid.wait()

            def save(group):
                return pltpu.make_async_copy(ig_st, ig_out.at[pl.ds(group * ratio, ratio)], s_st.at[0])

            def body(group, _):
                for cp in fetch(group):
                    cp.wait()
                act_load = load(act_in.at[group], acts, 0)
                act_load.start()

                @pl.when(group > 0)
                def _():
                    save(group - 1).wait()

                out = (dot_nn(g[...], w[...]) * u[...].astype(f32)).astype(bf16)
                sums = jnp.sum(out.astype(f32), axis=0, keepdims=True)
                for r in range(ratio):
                    ig_st[r] = out[:, r * n_fc : (r + 1) * n_fc]
                    sum_ref[pl.ds(8 + group * ratio + r, 1), :n_fc] = sums[:, r * n_fc : (r + 1) * n_fc]
                save(group).start()
                act_load.wait()
                total[...] += dot_nt(acts[...], w[...])

                @pl.when(group + 1 < groups)
                def _():
                    for cp in fetch(group + 1):
                        cp.start()

                for i in range(nz - 1):

                    @pl.when(group == i)
                    def _():
                        tick(1 + i)

                return 0

            lax.fori_loop(0, groups, body, 0)
            save(groups - 1).wait()
            result = (total[...] + vr_ref[0:1, :]).astype(bf16)
            swap[0, :, :, :width] = result.reshape(2, rows, width)
            give_back(0, swap.at[0], y_out)

        low_rows = pltpu.VMEM((tokens, width), bf16)
        full_rows = pltpu.VMEM((tokens, width), f32)
        pl.run_scoped(
            first_phase,
            low_rows,
            pltpu.VMEM((tokens, ff), bf16),
            pltpu.VMEM((width, ff), bf16),
            pltpu.VMEM((tokens, ff), bf16),
            pltpu.VMEM((ratio, tokens, n_fc), bf16),
            full_rows,
        )

        def second_phase(nt, igs):
            def fc_unit(to, plane, store):
                loads = [load(ig_out.at[to * grid.ny + y_to], igs.at[y_to], y_to) for y_to in range(2)]
                for cp in loads:
                    cp.start()
                for cp in loads:
                    cp.wait()

                def body(i, _):
                    y_to, x_to = i // 2, i % 2
                    at = pl.ds(pl.multiple_of((2 * x_to + plane) * slab, 16), slab)
                    store(y_to, x_to, beside(dot_nn(nt[at, :], igs[y_to])))
                    return 0

                lax.fori_loop(0, 4, body, 0)

            begin = load(nt_in, nt, 2)
            begin.start()
            begin.wait()
            tick(nz, fc_unit)

            def second_norm(dn, hid):
                hid_load = load(hid_in, hid, 7)
                hid_load.start()
                dn[...] = jnp.zeros_like(dn)
                pl.run_scoped(
                    functools.partial(back_feed, dn),
                    pltpu.VMEM((2, width, n_fc), bf16),
                    pltpu.VMEM((2, tokens, n_fc), bf16),
                )
                finish_norm(dn, hid, hid_load)

            def back_feed(dn, w, ig2):
                def fetch(part):
                    s = part % 2
                    return load(wf_in.at[part], w.at[s], 3 + s), load(ig_out.at[part], ig2.at[s], 5 + s)

                for cp in fetch(0):
                    cp.start()

                def body(part, _):
                    for cp in fetch(part):
                        cp.wait()

                    @pl.when(part + 1 < parts)
                    def _():
                        for cp in fetch(part + 1):
                            cp.start()

                    dn[...] += dot_nt(ig2[part % 2], w[part % 2])

                    @pl.when(part == parts // 2)
                    def _():
                        tick(nz + 1, fc_unit)

                    return 0

                lax.fori_loop(0, parts, body, 0)

            def finish_norm(dn, hid, hid_load):
                hid_load.wait()
                for v in (1, 2, 3):
                    sum_ref[v : v + 1, :] = jnp.zeros((1, width), f32)

                def norm(i, _):
                    at = pl.ds(pl.multiple_of(i * chunk, chunk), chunk)
                    values = hid[at, :]
                    grads = dn[at, :]
                    center = values - jnp.mean(values, axis=-1, keepdims=True)
                    factor = lax.rsqrt(jnp.mean(center * center, axis=-1, keepdims=True) + EPS)
                    xhat = center * factor
                    sum_ref[2:3, :] += jnp.sum(grads * xhat, axis=0, keepdims=True)
                    sum_ref[3:4, :] += jnp.sum(grads, axis=0, keepdims=True)
                    scaled = grads * vr_ref[1:2, :]
                    back = factor * (
                        scaled
                        - jnp.mean(scaled, axis=-1, keepdims=True)
                        - xhat * jnp.mean(scaled * xhat, axis=-1, keepdims=True)
                    )
                    hid[at, :] = back
                    return 0

                lax.fori_loop(0, tokens // chunk, norm, 0)

                def branch(bg, gl):
                    grad_load = load(g_in, gl, 3)
                    grad_load.start()
                    grad_load.wait()
                    hid[...] += gl[...].astype(f32)
                    low_grad = hid[...].astype(bf16)
                    sum_ref[1:2, :] = jnp.sum(low_grad.astype(f32), axis=0, keepdims=True)
                    for part in range(parts):
                        bg[part] = low_grad[:, part * n_out : (part + 1) * n_out]
                    outs = [
                        pltpu.make_async_copy(hid, hg_out, s_st.at[0]),
                        pltpu.make_async_copy(bg, bg_out, s_st.at[1]),
                    ]
                    for cp in outs:
                        cp.start()
                    for cp in outs:
                        cp.wait()

                pl.run_scoped(branch, pltpu.VMEM((parts, tokens, n_out), bf16), low_rows)

            pl.run_scoped(second_norm, full_rows, full_rows)
            given_back(0, swap.at[0], y_out)
            tick(nz + 2, fc_unit)

            def attention(ag):
                def back_out(acc, w, bgs):
                    def fetch(part):
                        s = part % 2
                        return load(wo_in.at[part], w.at[s], 3 + s), load(bg_out.at[part], bgs.at[s], 5 + s)

                    for cp in fetch(0):
                        cp.start()
                    acc[...] = jnp.zeros_like(acc)

                    def body(part, _):
                        for cp in fetch(part):
                            cp.wait()

                        @pl.when(part + 1 < parts)
                        def _():
                            for cp in fetch(part + 1):
                                cp.start()

                        acc[...] += dot_nt(bgs[part % 2], w[part % 2])
                        return 0

                    lax.fori_loop(0, parts, body, 0)
                    ag[:, :, wide - LANES :] = jnp.zeros((2, rows, LANES), bf16)
                    ag[:, :, :width] = acc[...].astype(bf16).reshape(2, rows, width)

                pl.run_scoped(
                    back_out,
                    full_rows,
                    pltpu.VMEM((2, width, n_out), bf16),
                    pltpu.VMEM((2, tokens, n_out), bf16),
                )

                pl.run_scoped(
                    functools.partial(attend_back, ag),
                    wide_low,
                    pltpu.VMEM((2, 2, rows, wide), f32),
                    pltpu.VMEM((2, 2, rows, wide), bf16),
                )

            def attend_back(ag, dq, own, oth):
                def heads(tq, tk, tv, ts, tof, tls):
                    def tiles(p):
                        s = p % 2
                        lanes = pl.ds(pl.multiple_of(p * LANES, LANES), LANES)
                        return [
                            pltpu.make_async_copy(src.at[:, :, lanes], dst.at[s], s_tile.at[i, s])
                            for i, (src, dst) in enumerate(
                                ((q_in, tq), (k_in, tk), (v_in, tv), (of_in, tof), (lse_in, tls))
                            )
                        ] + [pltpu.make_async_copy(s_in.at[:, :, :, lanes], ts.at[s], s_tile.at[5, s])]

                    for cp in tiles(0):
                        cp.start()

                    def body(p, _):
                        s = p % 2
                        for cp in tiles(p):
                            cp.wait()

                        @pl.when(p + 1 < pairs)
                        def _():
                            for cp in tiles(p + 1):
                                cp.start()

                        lanes = pl.ds(pl.multiple_of(p * LANES, LANES), LANES)
                        got_q, got_own, got_oth = pair_backward(
                            extra,
                            lambda i: tq[s, i],
                            lambda i: tk[s, i],
                            lambda i: tv[s, i],
                            lambda i: ts[s, 0, i],
                            lambda i: ts[s, 1, i],
                            lambda i: ag[i, :, lanes],
                            lambda i: tof[s, i],
                            lambda i: tls[s, i],
                            lambda i: rq_ref[i],
                            lambda i: ck_ref[i],
                            lambda i: cs_ref[i],
                            pair_masks(p, width),
                        )
                        for slot in range(2):
                            dq[slot, :, lanes] = got_q[slot].astype(bf16)
                            for kind in range(2):
                                own[kind, slot, :, lanes] = got_own[slot][kind]
                                oth[kind, slot, :, lanes] = got_oth[slot][kind].astype(bf16)
                        @pl.when(p == 3)
                        def _():
                            tick(nz + 3, fc_unit)

                        @pl.when(p == 8)
                        def _():
                            finish(2 * nz - 3)
                            second_stage(2 * nz - 1)

                        return 0

                    lax.fori_loop(0, pairs, body, 0)

                low_tile, full_tile = pltpu.VMEM((2, 2, rows, LANES), bf16), pltpu.VMEM((2, 2, rows, LANES), f32)
                pl.run_scoped(
                    heads, low_tile, low_tile, low_tile, pltpu.VMEM((2, 2, 2, rows, LANES), bf16), full_tile, full_tile
                )
                give = remote(oth, swap, s_kv.at[0], s_kv.at[1], at_sib)
                give.start()
                give.wait_recv()
                give.wait_send()
                for kind in range(2):
                    oth[kind] = (own[kind] + swap[kind].astype(f32)).astype(bf16)
                sum_ref[4:5, :] = jnp.sum(dq[...].astype(f32), axis=(0, 1))[None, :width]
                sum_ref[5:6, :] = jnp.sum(oth[1].astype(f32), axis=(0, 1))[None, :width]

                def spread(st):
                    def save(part):
                        return pltpu.make_async_copy(st.at[part % 2], pg_out.at[part], s_st.at[part % 2])

                    for part in range(parts):
                        if part >= 2:
                            save(part - 2).wait()
                        lo_part, hi_part = part * n_qkv, (part + 1) * n_qkv
                        for g in range(3):
                            lo, hi = max(lo_part, g * width), min(hi_part, (g + 1) * width)
                            if lo < hi:
                                a, b = lo - g * width, hi - g * width
                                piece = dq[:, :, a:b] if g == 0 else oth[g - 1, :, :, a:b]
                                st[part % 2, :, lo - lo_part : hi - lo_part] = piece.reshape(tokens, b - a)
                        save(part).start()
                    for part in range(parts - 2, parts):
                        save(part).wait()

                pl.run_scoped(spread, pltpu.VMEM((2, tokens, n_qkv), bf16))

            wide_low = pltpu.VMEM((2, rows, wide), bf16)
            pl.run_scoped(attention, wide_low)

        pl.run_scoped(
            second_phase,
            pltpu.VMEM((width, tokens), bf16),
            pltpu.VMEM((2, tokens, n_fc), bf16),
        )

        def third_phase(nt, at_t, pgs, bgs, dn, w, pg2, xs, hg):
            def qkv_unit(to, plane, store):
                loads = [
                    load(src.at[to * grid.ny + y_to], dst.at[y_to], sem + y_to)
                    for src, dst, sem in ((pg_out, pgs, 0), (bg_out, bgs, 6))
                    for y_to in range(2)
                ]
                for cp in loads:
                    cp.start()
                for cp in loads:
                    cp.wait()

                def body(i, _):
                    y_to, x_to = i // 2, i % 2
                    at = pl.ds(pl.multiple_of((2 * x_to + plane) * slab, 16), slab)
                    term = jnp.concatenate(
                        [dot_nn(nt[at, :], pgs[y_to]), dot_nn(at_t[at, :], bgs[y_to])], axis=1
                    )
                    store(y_to, x_to, beside(term))
                    return 0

                lax.fori_loop(0, 4, body, 0)

            begin = [load(n1t_in, nt, 2), load(at_in, at_t, 3)]
            for cp in begin:
                cp.start()
            for cp in begin:
                cp.wait()
            finish(2 * nz - 2)
            begin_unit(2 * nz, qkv_unit)

            def fetch(part):
                s = part % 2
                return load(wq_in.at[part], w.at[s], 2 + s), load(pg_out.at[part], pg2.at[s], 4 + s)

            late = [pltpu.make_async_copy(x_in, xs, s_st.at[0]), pltpu.make_async_copy(hg_out, hg, s_st.at[1])]
            for cp in (*late, *fetch(0)):
                cp.start()
            dn[...] = jnp.zeros_like(dn)

            def body(part, _):
                for cp in fetch(part):
                    cp.wait()

                @pl.when(part + 1 < parts)
                def _():
                    for cp in fetch(part + 1):
                        cp.start()

                dn[...] += dot_nt(pg2[part % 2], w[part % 2])

                @pl.when(part == parts // 2)
                def _():
                    second_stage(2 * nz)
                    begin_unit(2 * nz + 1, qkv_unit)

                return 0

            lax.fori_loop(0, parts, body, 0)
            for cp in late:
                cp.wait()
            sum_ref[6:8, :] = jnp.zeros((2, width), f32)

            def norm(i, _):
                at = pl.ds(pl.multiple_of(i * chunk, chunk), chunk)
                values = xs[at, :].astype(f32)
                grads = dn[at, :]
                center = values - jnp.mean(values, axis=-1, keepdims=True)
                factor = lax.rsqrt(jnp.mean(center * center, axis=-1, keepdims=True) + EPS)
                xhat = center * factor
                sum_ref[6:7, :] += jnp.sum(grads * xhat, axis=0, keepdims=True)
                sum_ref[7:8, :] += jnp.sum(grads, axis=0, keepdims=True)
                scaled = grads * vr_ref[2:3, :]
                back = factor * (
                    scaled
                    - jnp.mean(scaled, axis=-1, keepdims=True)
                    - xhat * jnp.mean(scaled * xhat, axis=-1, keepdims=True)
                )
                total = hg[at, :] + back
                hg[at, :] = total
                per = rows // chunk
                inside = pl.ds(pl.multiple_of(i % per * chunk, chunk), chunk)
                swap[1, i // per, inside, :width] = total.astype(bf16)
                return 0

            lax.fori_loop(0, tokens // chunk, norm, 0)
            give_back(1, swap.at[1], di_out)
            keep = pltpu.make_async_copy(hg, dx_out, s_st.at[1])
            keep.start()
            vec_step(0)
            tick(2 * nz + 2, qkv_unit)
            vec_step(1)
            tick(2 * nz + 3, qkv_unit)
            vec_step(2)
            finish(units - 3)
            finish(units - 2)
            vec_step(3)
            keep.wait()

        pl.run_scoped(
            third_phase,
            pltpu.VMEM((width, tokens), bf16),
            pltpu.VMEM((width, tokens), bf16),
            pltpu.VMEM((2, tokens, n_qkv), bf16),
            pltpu.VMEM((2, tokens, n_out), bf16),
            full_rows,
            pltpu.VMEM((2, width, n_qkv), bf16),
            pltpu.VMEM((2, tokens, n_qkv), bf16),
            low_rows,
            full_rows,
        )
        second_stage(units - 1)
        vec_step(4)
        finish(units - 1)
        given_back(1, swap.at[1], di_out)
        for kind, out in ((0, y_out), (1, di_out)):
            got_back(kind, swap.at[kind], out)
        for cp in (*sib(units - 1), *first(units - 1), *second(units - 1)):
            cp.wait_send()
        for u in range(units - nz, units - 1):
            for cp in line(u, 0, True, 0):
                cp.wait_send()

    any_, vm = pl.BlockSpec(memory_space=pl.ANY), pl.BlockSpec(memory_space=pltpu.VMEM)
    dma = pltpu.SemaphoreType.DMA
    halves = (h, n), (cols - h, n)
    scratch = []
    for dims in ((2, 2), (2, 2, 2), (2, 2), (2, 2), (), (3,)):
        scratch += [pltpu.VMEM((*dims, *half), bf16) for half in halves]
    scratch += [pltpu.VMEM((2, *half), f32) for half in halves]
    scratch += [pltpu.VMEM((nz - 1, *half), bf16) for half in halves]
    scratch += [pltpu.VMEM((2, nz + 1, *half), bf16) for half in halves]
    scratch += [
        pltpu.VMEM((2, 2, rows, wide), bf16),
        pltpu.VMEM((5, v_rows, width), f32),
        pltpu.VMEM((5, v_rows, width), f32),
        dma((6, units)),
        dma((6, units)),
        dma((2, units)),
        dma((2, 3, nz + 1)),
        dma((8,)),
        dma((2,)),
        dma((6, 2)),
        dma((2,)),
        dma((5,)),
        dma((5,)),
        dma((2, 2)),
        dma((2, 2)),
        dma((2,)),
        dma((2, 2, 2)),
    ]
    shape = jax.ShapeDtypeStruct
    return pl.pallas_call(
        kernel,
        out_shape=[
            *[shape((cols, n), f32)] * 3,
            shape((v_rows, width), f32),
            shape((2, rows, wide), bf16),
            shape((2, rows, wide), bf16),
            shape((tokens, width), f32),
            shape((tokens, width), f32),
            shape((parts, tokens, n_out), bf16),
            shape((parts, tokens, n_qkv), bf16),
            shape((parts, tokens, n_fc), bf16),
        ],
        in_specs=[any_] * 19 + [vm] * 4,
        out_specs=[any_] * 3 + [vm] + [any_] * 7,
        scratch_shapes=scratch,
        compiler_params=pltpu.CompilerParams(
            collective_id=5, has_side_effects=True, vmem_limit_bytes=60 * 1024 * 1024
        ),
        cost_estimate=cost(60e9, 200e6),
        name="backward",
    )(
        grad, proj_terms, act, slope, w_proj, hidden, normed_t, w_fc, w_out, queries, keys, values, other,
        att_full, logs, x_in, first_t, att_t, w_qkv, vec_rows, seg_row, seg_col, seg_other,
    )


def pick(array, index, axis):
    return lax.dynamic_index_in_dim(array, index, axis, keepdims=False)


def add_low(first, second):
    return (first.astype(f32) + second.astype(f32)).astype(bf16)


class Grid:
    def __init__(self, dp, ctx):
        self.dp, self.ctx = dp, ctx
        self.nx = max(ctx // 2, 1)
        self.ny = self.nx
        self.nz = dp // self.ny
        self.paired = self.nx == 2 and ctx == 4 and dp % 2 == 0

    def place(self):
        d, c = lax.axis_index("dp"), lax.axis_index("ctx")
        self.d, self.c = d, c
        self.z, self.y = d // self.ny, d % self.ny
        self.x, self.core = c // 2, c % 2

    def swap_core(self, v):
        return lax.ppermute(v, "ctx", [(i, i ^ 1) for i in range(self.ctx)])

    ACROSS = ((0, 2), (1, 3), (2, 1), (3, 0))
    WITHIN = ((2, 3), (3, 2))

    def by_sequence(self, v):
        first = self.x == 0
        across = lax.ppermute(pick(v, 1 - self.x, 0), "ctx", self.ACROSS)
        within = lax.ppermute(v[1], "ctx", self.WITHIN)
        return jnp.stack([jnp.where(first, v[0], across), jnp.where(first, across, within)])

    def by_position(self, v):
        first = self.x == 0
        across = lax.ppermute(pick(v, 1 - self.x, 0), "ctx", [(b, a) for a, b in self.ACROSS])
        within = lax.ppermute(v[1], "ctx", self.WITHIN)
        return jnp.stack([jnp.where(first, v[0], across), jnp.where(first, across, within)])


def on_device(grid, *args):
    (
        layer_input,
        grad_out,
        segment_ids,
        qkv_weight,
        q_bias,
        v_bias,
        out_weight,
        out_bias,
        fc_weight,
        fc_bias,
        proj_weight,
        proj_bias,
        ln1_gain,
        ln1_bias,
        ln2_gain,
        ln2_bias,
    ) = args
    seqs, rows, width = layer_input.shape
    tokens = seqs * rows
    parts, groups = grid.dp, grid.ctx
    both = ("dp", "ctx")
    grid.place()

    n_qkv, n_out, n_fc = qkv_weight.shape[1], out_weight.shape[1], fc_weight.shape[1]
    slab, hidden_slab = qkv_weight.shape[0], proj_weight.shape[0]
    paired = grid.paired and seqs == 2
    seg_blocks = segment_ids.reshape(seqs, groups, rows)
    vectors = (fc_bias, q_bias, v_bias, out_bias, proj_bias, ln1_gain, ln1_bias, ln2_gain, ln2_bias)
    sizes = [v.shape[0] for v in vectors]

    def unpack(packed):
        spread, at = [], 0
        for size in sizes:
            spread.append(packed[:, at : at + size].astype(f32))
            at += size
        return [v.reshape(-1) for v in spread]

    if paired:
        extra = 1 - grid.core
        chip_seg = pick(seg_blocks, grid.x, 0)
        seg_own = jnp.stack([pick(chip_seg, grid.core, 0), pick(chip_seg, 3 - grid.core, 0)])
        seg_other = jnp.stack([pick(chip_seg, extra, 0), pick(chip_seg, 3 - extra, 0)])
        packed = jnp.concatenate(vectors).astype(f32)[None]
        (
            w_qkv, w_out, w_fc, w_proj, packed, slope, activated, other, x_seq, grad_seq, normed1_t, normed2_t, attended_t,
            proj_terms, queries, keys, vals, attended_f32, log_total, hidden,
        ) = forward_gather(
            grid,
            layer_input,
            grad_out,
            (qkv_weight, out_weight, fc_weight, proj_weight.T),
            jnp.broadcast_to(packed, (8, packed.shape[1])),
            seg_own[:, :, None],
            seg_own[:, None, :],
            seg_other[:, None, :],
        )
        _, _, _, _, pb_all, g1, b1, g2, b2 = unpack(packed[:, :, 0].reshape(parts, -1))
        w_qkv = w_qkv.reshape(parts, width, n_qkv)
        w_fc = w_fc.reshape(parts, width, n_fc)
        w_proj = w_proj.reshape(groups, width, hidden_slab)
    else:
        packed = lax.all_gather(jnp.concatenate(vectors), "dp", axis=0)
        fcb, q_all, v_all, ob_all, pb_all, g1, b1, g2, b2 = unpack(packed)

        def gather(block, axes):
            return lax.all_gather(block, axes, axis=0)

        w_qkv = gather(qkv_weight, both).reshape(parts, width, n_qkv)
        w_out = gather(out_weight, both).reshape(parts, width, n_out)
        w_fc = gather(fc_weight, both).reshape(parts, width, n_fc)
        w_proj = gather(proj_weight.T, ("ctx", "dp")).reshape(groups, width, hidden_slab)
        out_full = w_out.transpose(1, 0, 2).reshape(width, width)
        values = layer_input.reshape(tokens, width).astype(f32)
        normed1 = layer_norm(values, g1, b1).astype(bf16)
        joined = jnp.concatenate([q_all, jnp.zeros((width,), f32), v_all])
        queries, key_rows, value_rows = qkv_project(normed1, w_qkv, joined.reshape(parts, 1, n_qkv))
        queries = queries.reshape(seqs, rows, width)
        own = jnp.stack([key_rows, value_rows]).reshape(2, seqs, rows, width)
        pairs_full = lax.all_gather(own, "ctx", axis=0)
        seg_mine = pick(seg_blocks, grid.c, 1)
        needed = seg_blocks[:, :, -1] >= seg_mine[:, :1]
        start = jnp.minimum(jnp.argmax(needed, axis=1).astype(jnp.int32), grid.c)
        bounds = jnp.concatenate([grid.c[None].astype(jnp.int32), start])
        attended, attended_f32, log_total = attention_forward(
            bounds, queries, pairs_full, seg_mine[:, :, None], seg_blocks[:, :, None, :]
        )
        attended = attended.reshape(tokens, width)
        hidden = values + jnp.dot(attended, out_full, preferred_element_type=f32) + ob_all
        normed2 = layer_norm(hidden, g2, b2).astype(bf16)
        inner, activated = feed_in(normed2, w_fc, fcb.reshape(parts, 1, n_fc), groups)

    def tall_cut(size):
        return (size // 2 + 15) // 16 * 16

    def by_columns(refs, core, z, store):
        for y_to in range(2):
            for x_to in range(2):
                at = pl.ds(pl.multiple_of((2 * x_to + core) * slab, 16), slab)
                terms = [
                    dot_nn(left[at, :], right[z * grid.ny + y_to])
                    for left, right in zip(refs[::2], refs[1::2])
                ]
                store(y_to, x_to, jnp.concatenate(terms, axis=1) if len(terms) > 1 else terms[0])

    def by_rows(refs, core, z, store):
        left, right = refs
        cols = width // parts
        at = pl.ds(pl.multiple_of(z * (grid.ny * cols), 16), grid.ny * cols)
        for x_to in range(2):
            term = dot_nn(left[at, :], right[2 * x_to + core])
            for y_to in range(2):
                store(y_to, x_to, term[y_to * cols : (y_to + 1) * cols])

    def reduced(pairs, collective_id, name):
        if not paired:
            everything = jnp.arange(parts, dtype=jnp.int32)
            results = []
            for left, right in pairs:
                whole = weight_grad(left.T, right, everything)
                whole = whole.reshape(parts * groups, slab, right.shape[2])
                results.append(lax.psum_scatter(whole, both, scatter_dimension=0).astype(f32))
            return results
        operands, ends = [], [0]
        for left, right in pairs:
            n = right.shape[2]
            full = n if len(ends) == len(pairs) else pl.cdiv(n, LANES) * LANES
            operands += [left.T, jnp.pad(right, ((0, 0), (0, 0), (0, full - n)))]
            ends.append(ends[-1] + full)
        total = summed_grads(
            grid, collective_id, operands, by_columns, (slab, ends[-1]), tall_cut(slab), name
        )
        return [total[:, at : at + pair[1].shape[2]] for at, pair in zip(ends, pairs)]

    def reduced_proj(left, right):
        f = right.shape[2]
        cols = width // parts
        if not paired:
            whole = weight_grad(left.T, right, jnp.arange(groups, dtype=jnp.int32))
            whole = whole.reshape(groups * parts, cols, f)
            return lax.psum_scatter(whole, ("ctx", "dp"), scatter_dimension=0).astype(f32)
        return summed_grads(grid, 1, [left.T, right], by_rows, (cols, f), tall_cut(cols), "rs_proj")

    if paired:
        proj_halves, fc_halves, last_halves, sums, output, far, near, *_ = backward_sums(
            grid,
            grad_seq.reshape(tokens, width),
            proj_terms,
            activated,
            slope,
            w_proj,
            hidden.reshape(tokens, width),
            normed2_t,
            w_fc,
            w_out.reshape(parts, width, n_out),
            queries,
            keys,
            vals,
            other,
            attended_f32,
            log_total,
            x_seq.reshape(tokens, width),
            normed1_t,
            attended_t,
            w_qkv,
            jnp.stack([pb_all, g2, g1] + [jnp.zeros_like(g1)] * 5),
            seg_own[:, None, :],
            seg_own[:, :, None],
            seg_other[:, :, None],
        )
        proj_weight_grad = proj_halves.T
        fc_weight_grad = jnp.concatenate([fc_halves[:, :n_fc], fc_halves[:, n_fc:]], axis=0)
        last = jnp.concatenate([last_halves[:, :n_fc], last_halves[:, n_fc:]], axis=0)
        qkv_weight_grad, out_weight_grad = last[:, :n_qkv], last[:, n_qkv:]
        far = far[:, :, :width].astype(f32)
        near = near.reshape(2, rows, width)
        stays = (grid.x == 0) & (jnp.arange(2) == 0)
        input_grad = jnp.where(stays[:, None, None], near, far)
        own = pick(sums[:8].reshape(8, parts, n_out), grid.d, 1)
        fc_own = pick(sums[8:, :n_fc], grid.d, 0)
        return (
            output[:, :, :width],
            input_grad,
            qkv_weight_grad,
            own[4],
            own[5],
            out_weight_grad,
            own[1],
            fc_weight_grad,
            fc_own,
            proj_weight_grad,
            own[0],
            own[6],
            own[7],
            own[2],
            own[3],
        )
    else:
        mlp_grad = grad_out.reshape(tokens, width)
        cotangent = mlp_grad.astype(f32)
        output = feed_out(activated, w_proj, hidden, pb_all[None])
        proj_bias_grad = jnp.sum(cotangent, axis=0)
        inner_grad, fc_bias_grad = feed_back(mlp_grad, w_proj, inner, parts)
        proj_weight_grad = reduced_proj(mlp_grad, activated).T
        (fc_weight_grad,) = reduced([(normed2, inner_grad)], 2, "rs_fc")
        normed2_grad = back_project(inner_grad, w_fc)
        norm2_out, norm2_pull = jax.vjp(layer_norm, hidden, g2, b2)
        hidden_ln, g2_grad, b2_grad = norm2_pull(normed2_grad)
        hidden_grad = cotangent + hidden_ln
        branch_grad = hidden_grad.astype(bf16)
        out_bias_grad = jnp.sum(branch_grad, axis=0, dtype=f32)
        attended_grad = jnp.einsum(
            "nd,ed->ne", branch_grad, out_full, preferred_element_type=f32
        ).astype(bf16)
        branch_parts = branch_grad.reshape(tokens, parts, n_out).transpose(1, 0, 2)
        query_grad, pairs_grad = attention_backward(
            bounds,
            queries,
            pairs_full,
            seg_blocks[:, :, :, None],
            seg_mine[:, None, :],
            attended_grad.reshape(seqs, rows, width),
            attended_f32,
            log_total,
        )
        pair_grad = lax.psum_scatter(pairs_grad, "ctx", scatter_dimension=0)
        pair_grad = pair_grad.reshape(2, tokens, width)
        projected_grad = jnp.concatenate(
            [query_grad.reshape(tokens, width), pair_grad[0], pair_grad[1]], axis=1
        )
        q_bias_grad = jnp.sum(query_grad.reshape(tokens, width), axis=0, dtype=f32)
        v_bias_grad = jnp.sum(pair_grad[1], axis=0, dtype=f32)
        by_part = projected_grad.reshape(tokens, parts, n_qkv).transpose(1, 0, 2)
    out_weight_grad, qkv_weight_grad = reduced(
        [(attended, branch_parts), (normed1, by_part)], 3, "rs_qkv"
    )
    normed1_grad = back_project(by_part, w_qkv)
    norm1_out, norm1_pull = jax.vjp(layer_norm, values, g1, b1)
    values_ln, g1_grad, b1_grad = norm1_pull(normed1_grad)
    input_grad = hidden_grad + values_ln

    output, input_grad = (v.reshape(seqs, rows, width) for v in (output, input_grad))
    sums = [
        fc_bias_grad,
        q_bias_grad,
        v_bias_grad,
        out_bias_grad,
        proj_bias_grad,
        g1_grad,
        b1_grad,
        g2_grad,
        b2_grad,
    ]
    stacked = jnp.concatenate([v.reshape(parts, -1) for v in sums], axis=1)
    total = pick(lax.psum(stacked, both), grid.d, 0)
    vec, at = [], 0
    for size in sizes:
        vec.append(total[at : at + size])
        at += size
    return (
        output,
        input_grad,
        qkv_weight_grad,
        vec[1],
        vec[2],
        out_weight_grad,
        vec[3],
        fc_weight_grad,
        vec[0],
        proj_weight_grad,
        vec[4],
        vec[5],
        vec[6],
        vec[7],
        vec[8],
    )


def solution(mesh):
    rows3, mat, vec = P("dp", "ctx", None), P("ctx", "dp"), P("dp")
    grid = Grid(mesh.shape["dp"], mesh.shape["ctx"])
    return jax.shard_map(
        functools.partial(on_device, grid),
        mesh=mesh,
        in_specs=(
            rows3,
            rows3,
            P("dp", None),
            mat,
            vec,
            vec,
            mat,
            vec,
            mat,
            vec,
            mat,
            vec,
            vec,
            vec,
            vec,
            vec,
        ),
        out_specs=(
            rows3,
            rows3,
            mat,
            vec,
            vec,
            mat,
            vec,
            mat,
            vec,
            mat,
            vec,
            vec,
            vec,
            vec,
            vec,
        ),
        check_vma=False,
    )
```

```python
import functools

import jax
import jax.numpy as jnp
from jax import lax
from jax.experimental import pallas as pl
from jax.experimental.pallas import tpu as pltpu
from jax.sharding import PartitionSpec as P

HEADS = 25
HEAD_DIM = 64
LANES = 128
EPS = 1e-05
NEG_FILL = -1e30
GELU_C = 0.7978845608028654
GELU_A = 0.044715

bf16 = jnp.bfloat16
f32 = jnp.float32
VMEM_LIMIT = 58 * 1024 * 1024


def layer_norm(values, gain, shift):
    center = values - jnp.mean(values, axis=-1, keepdims=True)
    factor = lax.rsqrt(jnp.mean(center * center, axis=-1, keepdims=True) + EPS)
    return center * factor * gain + shift


def dot_nn(a, b):
    return lax.dot_general(a, b, (((1,), (0,)), ((), ())), preferred_element_type=f32)


def dot_nt(a, b):
    return lax.dot_general(a, b, (((1,), (1,)), ((), ())), preferred_element_type=f32)


def dot_tn(a, b):
    return lax.dot_general(a, b, (((0,), (0,)), ((), ())), preferred_element_type=f32)


def params(n_axes=1):
    return pltpu.CompilerParams(
        dimension_semantics=("arbitrary",) * n_axes, vmem_limit_bytes=VMEM_LIMIT
    )


def cost(flops, read, transcendentals=0):
    return pl.CostEstimate(
        flops=int(flops), bytes_accessed=int(read), transcendentals=int(transcendentals)
    )


def qkv_project(normed, weight, bias):
    tokens, width = normed.shape
    parts, _, n = weight.shape

    def kernel(x_ref, w_ref, b_ref, *out_refs):
        part = pl.program_id(0)
        y = (dot_nn(x_ref[...], w_ref[0]) + b_ref[0]).astype(bf16)
        for d in range(parts):

            @pl.when(part == d)
            def _():
                first, last = d * n, (d + 1) * n
                for g in range(3):
                    lo, hi = max(first, g * width), min(last, (g + 1) * width)
                    if lo < hi:
                        out_refs[g][:, lo - g * width : hi - g * width] = y[
                            :, lo - first : hi - first
                        ]

    whole = pl.BlockSpec((tokens, width), lambda d: (0, 0))
    return pl.pallas_call(
        kernel,
        grid=(parts,),
        in_specs=[
            whole,
            pl.BlockSpec((1, width, n), lambda d: (d, 0, 0)),
            pl.BlockSpec((1, 1, n), lambda d: (d, 0, 0)),
        ],
        out_specs=[whole] * 3,
        out_shape=[jax.ShapeDtypeStruct((tokens, width), bf16)] * 3,
        compiler_params=params(),
        cost_estimate=cost(2 * tokens * width * parts * n, 2 * width * parts * n),
        name="qkv",
    )(normed, weight, bias)


def pair_masks(pair, width):
    lane = lax.broadcasted_iota(jnp.int32, (1, LANES), 1)
    inside = lane + pair * LANES < width
    return inside & (lane < HEAD_DIM), inside & (lane >= HEAD_DIM), inside


def attention_forward(bounds, queries, pairs_full, seg_col, seg_row):
    seqs, rows, width = queries.shape
    blocks = pairs_full.shape[0]
    pairs = pl.cdiv(width, LANES)

    def kernel(bounds_ref, q_ref, kv_ref, sc_ref, sr_ref, o_ref, of_ref, lse_ref):
        seq, pair = pl.program_id(0), pl.program_id(1)
        mine, start = bounds_ref[0], bounds_ref[1 + seq]
        low, high, inside = pair_masks(pair, width)
        scaled = q_ref[0] * jnp.asarray(0.125, bf16)
        q_heads = (
            jnp.where(low, scaled, jnp.zeros_like(scaled)),
            jnp.where(high, scaled, jnp.zeros_like(scaled)),
        )
        seg_q = sc_ref[0]

        def block(j, diagonal, carry):
            k = jnp.where(inside, kv_ref[j, 0, 0], jnp.zeros((rows, LANES), bf16))
            v = jnp.where(inside, kv_ref[j, 1, 0], jnp.zeros((rows, LANES), bf16))
            allowed = sr_ref[0, j] == seg_q
            if diagonal:
                at_row = lax.broadcasted_iota(jnp.int32, (rows, rows), 0)
                at_col = lax.broadcasted_iota(jnp.int32, (rows, rows), 1)
                allowed = allowed & (at_col <= at_row)
            out = []
            for head in range(2):
                s = jnp.where(allowed, dot_nt(q_heads[head], k), NEG_FILL)
                top = jnp.max(s, axis=1, keepdims=True)
                if carry is None:
                    p = jnp.exp(s - top)
                    out += [top, jnp.sum(p, axis=1, keepdims=True), dot_nn(p.astype(bf16), v)]
                else:
                    m, l, acc = carry[3 * head : 3 * head + 3]
                    new = jnp.maximum(m, top)
                    scale = jnp.exp(m - new)
                    p = jnp.exp(s - new)
                    out += [
                        new,
                        l * scale + jnp.sum(p, axis=1, keepdims=True),
                        acc * scale + dot_nn(p.astype(bf16), v),
                    ]
            return tuple(out)

        carry = block(mine, True, None)
        carry = lax.fori_loop(start, mine, lambda j, c: block(j, False, c), carry)
        m0, l0, a0, m1, l1, a1 = carry
        result = jnp.where(low, a0 / l0, a1 / l1)
        o_ref[0] = result.astype(bf16)
        of_ref[0] = result
        lse_ref[0] = jnp.where(low, m0 + jnp.log(l0), m1 + jnp.log(l1))

    tile = pl.BlockSpec((1, rows, LANES), lambda s, p, b: (s, 0, p))
    return pl.pallas_call(
        kernel,
        grid_spec=pltpu.PrefetchScalarGridSpec(
            num_scalar_prefetch=1,
            grid=(seqs, pairs),
            in_specs=[
                tile,
                pl.BlockSpec((blocks, 2, 1, rows, LANES), lambda s, p, b: (0, 0, s, 0, p)),
                pl.BlockSpec((1, rows, 1), lambda s, p, b: (s, 0, 0)),
                pl.BlockSpec((1, blocks, 1, rows), lambda s, p, b: (s, 0, 0, 0)),
            ],
            out_specs=[tile, tile, tile],
        ),
        out_shape=[
            jax.ShapeDtypeStruct((seqs, rows, width), bf16),
            jax.ShapeDtypeStruct((seqs, rows, width), f32),
            jax.ShapeDtypeStruct((seqs, rows, width), f32),
        ],
        compiler_params=params(2),
        cost_estimate=cost(
            4 * seqs * rows * rows * blocks * width, 4 * seqs * rows * blocks * width
        ),
        name="attn_fwd",
    )(bounds, queries, pairs_full, seg_col, seg_row)


def attention_backward(
    bounds, queries, pairs_full, seg_col, seg_row, out_grad, out_full, log_total
):
    seqs, rows, width = queries.shape
    blocks = pairs_full.shape[0]
    pairs = pl.cdiv(width, LANES)

    def kernel(bounds_ref, q_ref, kv_ref, sc_ref, sr_ref, g_ref, of_ref, lse_ref, dq_ref, dkv_ref):
        seq, pair = pl.program_id(0), pl.program_id(1)
        mine, start = bounds_ref[0], bounds_ref[1 + seq]
        low, high, inside = pair_masks(pair, width)
        zero = jnp.zeros((rows, LANES), bf16)
        scaled = q_ref[0] * jnp.asarray(0.125, bf16)
        grad = g_ref[0]
        q_heads = (jnp.where(low, scaled, zero), jnp.where(high, scaled, zero))
        g_heads = (jnp.where(low, grad, zero), jnp.where(high, grad, zero))
        product = jnp.where(inside, grad.astype(f32) * of_ref[0], 0.0)
        lse = jnp.where(inside, lse_ref[0], 0.0)
        product_t = product.T
        lse_t = lse.T
        delta = (
            jnp.sum(product_t[:HEAD_DIM], axis=0, keepdims=True),
            jnp.sum(product_t[HEAD_DIM:], axis=0, keepdims=True),
        )
        log_row = (lse_t[0:1], lse_t[HEAD_DIM : HEAD_DIM + 1])
        seg_q = sr_ref[0]
        dkv_ref[...] = jnp.zeros_like(dkv_ref)

        def block(j, diagonal, total):
            k = jnp.where(inside, kv_ref[j, 0, 0], zero)
            v = jnp.where(inside, kv_ref[j, 1, 0], zero)
            allowed = sc_ref[0, j] == seg_q
            if diagonal:
                at_key = lax.broadcasted_iota(jnp.int32, (rows, rows), 0)
                at_query = lax.broadcasted_iota(jnp.int32, (rows, rows), 1)
                allowed = allowed & (at_key <= at_query)
            key_grad, value_grad = None, None
            for head in range(2):
                k_head = jnp.where((low, high)[head], k, zero)
                s = jnp.where(allowed, dot_nt(k, q_heads[head]), NEG_FILL)
                p = jnp.exp(s - log_row[head])
                pushed = dot_nt(v, g_heads[head])
                ds = (p * (pushed - delta[head])).astype(bf16)
                dv = dot_nn(p.astype(bf16), g_heads[head])
                dk = dot_nn(ds, q_heads[head])
                dq = dot_tn(ds, k_head)
                key_grad = dk if key_grad is None else key_grad + dk
                value_grad = dv if value_grad is None else value_grad + dv
                total = dq if total is None else total + dq
            dkv_ref[j, 0, 0] = key_grad.astype(bf16)
            dkv_ref[j, 1, 0] = value_grad.astype(bf16)
            return total

        total = block(mine, True, None)
        total = lax.fori_loop(start, mine, lambda j, c: block(j, False, c), total)
        dq_ref[0] = (total * 0.125).astype(bf16)

    tile = pl.BlockSpec((1, rows, LANES), lambda s, p, b: (s, 0, p))
    many = pl.BlockSpec((blocks, 2, 1, rows, LANES), lambda s, p, b: (0, 0, s, 0, p))
    return pl.pallas_call(
        kernel,
        grid_spec=pltpu.PrefetchScalarGridSpec(
            num_scalar_prefetch=1,
            grid=(seqs, pairs),
            in_specs=[
                tile,
                many,
                pl.BlockSpec((1, blocks, rows, 1), lambda s, p, b: (s, 0, 0, 0)),
                pl.BlockSpec((1, 1, rows), lambda s, p, b: (s, 0, 0)),
                tile,
                tile,
                tile,
            ],
            out_specs=[tile, many],
        ),
        out_shape=[
            jax.ShapeDtypeStruct((seqs, rows, width), bf16),
            jax.ShapeDtypeStruct(pairs_full.shape, bf16),
        ],
        compiler_params=params(2),
        cost_estimate=cost(
            10 * seqs * rows * rows * blocks * width, 8 * seqs * rows * blocks * width
        ),
        name="attn_bwd",
    )(bounds, queries, pairs_full, seg_col, seg_row, out_grad, out_full, log_total)


def causal(rows, transposed=False):
    first = lax.broadcasted_iota(jnp.int32, (rows, rows), 0)
    second = lax.broadcasted_iota(jnp.int32, (rows, rows), 1)
    return first <= second if transposed else second <= first


def pair_forward(extra, q, k, v, sk, sv, seg_q, seg_k, seg_sk, masks):
    low, high, inside = masks
    rows = q(0).shape[0]
    zero = jnp.zeros((rows, LANES), bf16)
    tri = causal(rows)

    def heads_of(value):
        scaled = value * jnp.asarray(0.125, bf16)
        return jnp.where(low, scaled, zero), jnp.where(high, scaled, zero)

    def clean(value):
        return jnp.where(inside, value, zero)

    def unit(q_heads, keys, values, allowed, state):
        out = []
        for head in range(2):
            s = jnp.where(allowed, dot_nt(q_heads[head], keys), NEG_FILL)
            top = jnp.max(s, axis=1, keepdims=True)
            if state is None:
                p = jnp.exp(s - top)
                out.append((top, jnp.sum(p, axis=1, keepdims=True), dot_nn(p.astype(bf16), values)))
            else:
                m, l, acc = state[head]
                new = jnp.maximum(m, top)
                scale = jnp.exp(m - new)
                p = jnp.exp(s - new)
                out.append(
                    (
                        new,
                        l * scale + jnp.sum(p, axis=1, keepdims=True),
                        acc * scale + dot_nn(p.astype(bf16), values),
                    )
                )
        return out

    more = unit(
        heads_of(q(extra)), clean(sk(extra)), clean(sv(extra)), seg_sk(extra) == seg_q(extra), None
    )
    results = []
    for slot in range(2):
        here = extra == slot
        state = [
            (jnp.where(here, m, NEG_FILL), jnp.where(here, l, 0.0), jnp.where(here, acc, 0.0))
            for m, l, acc in more
        ]
        q_heads = heads_of(q(slot))
        state = unit(
            q_heads, clean(k(slot)), clean(v(slot)), (seg_k(slot) == seg_q(slot)) & tri, state
        )
        if slot == 1:
            state = unit(q_heads, clean(k(0)), clean(v(0)), seg_k(0) == seg_q(1), state)
            state = unit(q_heads, clean(sk(0)), clean(sv(0)), seg_sk(0) == seg_q(1), state)
        (m0, l0, a0), (m1, l1, a1) = state
        results.append(
            (jnp.where(low, a0 / l0, a1 / l1), jnp.where(low, m0 + jnp.log(l0), m1 + jnp.log(l1)))
        )
    return results


def pair_backward(extra, q, k, v, sk, sv, g, o, lse, seg_q, seg_k, seg_sk, masks):
    low, high, inside = masks
    rows = q(0).shape[0]
    zero = jnp.zeros((rows, LANES), bf16)
    tri = causal(rows, transposed=True)

    def halves(value):
        return jnp.where(low, value, zero), jnp.where(high, value, zero)

    def queries(slot):
        grad = g(slot)
        product = jnp.where(inside, grad.astype(f32) * o(slot), 0.0).T
        sums = jnp.where(inside, lse(slot), 0.0).T
        return (
            halves(q(slot) * jnp.asarray(0.125, bf16)),
            halves(grad),
            (
                jnp.sum(product[:HEAD_DIM], axis=0, keepdims=True),
                jnp.sum(product[HEAD_DIM:], axis=0, keepdims=True),
            ),
            (sums[0:1], sums[HEAD_DIM : HEAD_DIM + 1]),
        )

    def unit(side, keys, values, allowed):
        q_heads, g_heads, delta, logs = side
        keys, values = jnp.where(inside, keys, zero), jnp.where(inside, values, zero)
        k_heads = halves(keys)
        dq = dk = dv = None
        for head in range(2):
            s = jnp.where(allowed, dot_nt(keys, q_heads[head]), NEG_FILL)
            p = jnp.exp(s - logs[head])
            ds = (p * (dot_nt(values, g_heads[head]) - delta[head])).astype(bf16)
            terms = (
                dot_tn(ds, k_heads[head]),
                dot_nn(ds, q_heads[head]),
                dot_nn(p.astype(bf16), g_heads[head]),
            )
            dq, dk, dv = terms if dq is None else (dq + terms[0], dk + terms[1], dv + terms[2])
        return dq, dk, dv

    sides = [queries(0), queries(1)]
    first = unit(sides[0], k(0), v(0), (seg_k(0) == seg_q(0)) & tri)
    second = unit(sides[1], k(1), v(1), (seg_k(1) == seg_q(1)) & tri)
    third = unit(sides[1], k(0), v(0), seg_k(0) == seg_q(1))
    fourth = unit(sides[1], sk(0), sv(0), seg_sk(0) == seg_q(1))
    fifth = unit(queries(extra), sk(extra), sv(extra), seg_sk(extra) == seg_q(extra))
    at_one = extra == 1

    def when(flag, value):
        return jnp.where(flag, value, 0.0)

    dq0 = first[0] + when(~at_one, fifth[0])
    dq1 = second[0] + third[0] + fourth[0] + when(at_one, fifth[0])
    own = [(first[1] + third[1], first[2] + third[2]), second[1:]]
    other = [
        tuple(fourth[i] + when(~at_one, fifth[i]) for i in (1, 2)),
        tuple(when(at_one, fifth[i]) for i in (1, 2)),
    ]
    return (dq0 * 0.125, dq1 * 0.125), own, other


def feed_in(normed, weight, bias, groups):
    tokens, width = normed.shape
    parts, _, n = weight.shape
    ratio = parts // groups

    def kernel(x_ref, w_ref, b_ref, inner_ref, act_ref):
        place = lax.rem(pl.program_id(0), ratio)
        u = dot_nn(x_ref[...], w_ref[0]) + b_ref[0]
        act = (0.5 * u * (1.0 + jnp.tanh(GELU_C * (u + GELU_A * u * u * u)))).astype(bf16)
        for r in range(ratio):

            @pl.when(place == r)
            def _():
                inner_ref[0, :, r * n : (r + 1) * n] = u
                act_ref[0, :, r * n : (r + 1) * n] = act

    out = pl.BlockSpec((1, tokens, ratio * n), lambda d: (d // ratio, 0, 0))
    return pl.pallas_call(
        kernel,
        grid=(parts,),
        in_specs=[
            pl.BlockSpec((tokens, width), lambda d: (0, 0)),
            pl.BlockSpec((1, width, n), lambda d: (d, 0, 0)),
            pl.BlockSpec((1, 1, n), lambda d: (d, 0, 0)),
        ],
        out_specs=[out, out],
        out_shape=[
            jax.ShapeDtypeStruct((groups, tokens, ratio * n), f32),
            jax.ShapeDtypeStruct((groups, tokens, ratio * n), bf16),
        ],
        compiler_params=params(),
        cost_estimate=cost(2 * tokens * width * parts * n, 2 * width * parts * n),
        name="fc",
    )(normed, weight, bias)


def feed_out(act, weight, hidden, bias):
    groups, tokens, f = act.shape
    width = weight.shape[1]

    def kernel(a_ref, w_ref, h_ref, b_ref, o_ref, acc_ref):
        step = pl.program_id(0)

        @pl.when(step == 0)
        def _():
            acc_ref[...] = h_ref[...] + b_ref[...]

        acc_ref[...] += dot_nt(a_ref[0], w_ref[0])

        @pl.when(step == groups - 1)
        def _():
            o_ref[...] = acc_ref[...].astype(bf16)

    return pl.pallas_call(
        kernel,
        grid=(groups,),
        in_specs=[
            pl.BlockSpec((1, tokens, f), lambda c: (c, 0, 0)),
            pl.BlockSpec((1, width, f), lambda c: (c, 0, 0)),
            pl.BlockSpec((tokens, width), lambda c: (0, 0)),
            pl.BlockSpec((1, width), lambda c: (0, 0)),
        ],
        out_specs=pl.BlockSpec((tokens, width), lambda c: (0, 0)),
        out_shape=jax.ShapeDtypeStruct((tokens, width), bf16),
        scratch_shapes=[pltpu.VMEM((tokens, width), f32)],
        compiler_params=params(),
        cost_estimate=cost(2 * groups * tokens * width * f, 2 * groups * width * f),
        name="proj",
    )(act, weight, hidden, bias)


def feed_back(grad, weight, inner, parts):
    groups, tokens, f = inner.shape
    width = weight.shape[1]
    ratio = parts // groups
    n = f // ratio

    def kernel(g_ref, w_ref, u_ref, o_ref, s_ref):
        u = u_ref[0]
        t = jnp.tanh(GELU_C * (u + GELU_A * u * u * u))
        slope = 0.5 * (1.0 + t) + 0.5 * u * (1.0 - t * t) * (
            GELU_C * (1.0 + 3.0 * GELU_A * u * u)
        )
        out = (dot_nn(g_ref[...], w_ref[0]) * slope).astype(bf16)
        total = jnp.sum(out.astype(f32), axis=0, keepdims=True)
        for r in range(ratio):
            o_ref[r] = out[:, r * n : (r + 1) * n]
            s_ref[r] = total[:, r * n : (r + 1) * n]

    return pl.pallas_call(
        kernel,
        grid=(groups,),
        in_specs=[
            pl.BlockSpec((tokens, width), lambda c: (0, 0)),
            pl.BlockSpec((1, width, f), lambda c: (c, 0, 0)),
            pl.BlockSpec((1, tokens, f), lambda c: (c, 0, 0)),
        ],
        out_specs=[
            pl.BlockSpec((ratio, tokens, n), lambda c: (c, 0, 0)),
            pl.BlockSpec((ratio, 1, n), lambda c: (c, 0, 0)),
        ],
        out_shape=[
            jax.ShapeDtypeStruct((parts, tokens, n), bf16),
            jax.ShapeDtypeStruct((parts, 1, n), f32),
        ],
        compiler_params=params(),
        cost_estimate=cost(2 * groups * tokens * width * f, 6 * groups * width * f),
        name="act_bwd",
    )(grad, weight, inner)


def back_project(grads, weight):
    parts, tokens, n = grads.shape
    width = weight.shape[1]

    def kernel(g_ref, w_ref, o_ref):
        @pl.when(pl.program_id(0) == 0)
        def _():
            o_ref[...] = dot_nt(g_ref[0], w_ref[0])

        @pl.when(pl.program_id(0) > 0)
        def _():
            o_ref[...] += dot_nt(g_ref[0], w_ref[0])

    return pl.pallas_call(
        kernel,
        grid=(parts,),
        in_specs=[
            pl.BlockSpec((1, tokens, n), lambda d: (d, 0, 0)),
            pl.BlockSpec((1, width, n), lambda d: (d, 0, 0)),
        ],
        out_specs=pl.BlockSpec((tokens, width), lambda d: (0, 0)),
        out_shape=jax.ShapeDtypeStruct((tokens, width), f32),
        compiler_params=params(),
        cost_estimate=cost(2 * parts * tokens * width * n, 2 * parts * width * n),
        name="back",
    )(grads, weight)


def weight_grad(left, right, picks, arrived=None):
    rows, tokens = left.shape
    n = right.shape[2]
    count = picks.shape[0]

    def kernel(picks_ref, a_ref, b_ref, *refs):
        y = dot_nn(a_ref[...], b_ref[0])
        if arrived is not None:
            y = y + refs[0][0].astype(f32)
        refs[-1][0] = y.astype(bf16)

    block = pl.BlockSpec((1, rows, n), lambda j, picks: (j, 0, 0))
    return pl.pallas_call(
        kernel,
        grid_spec=pltpu.PrefetchScalarGridSpec(
            num_scalar_prefetch=1,
            grid=(count,),
            in_specs=[
                pl.BlockSpec((rows, tokens), lambda j, picks: (0, 0)),
                pl.BlockSpec((1, tokens, n), lambda j, picks: (picks[j], 0, 0)),
            ]
            + ([block] if arrived is not None else []),
            out_specs=block,
        ),
        out_shape=jax.ShapeDtypeStruct((count, rows, n), bf16),
        compiler_params=params(),
        cost_estimate=cost(2 * count * rows * tokens * n, 2 * count * rows * n),
        name="wgrad",
    )(picks, left, right, *(() if arrived is None else (arrived,)))


MESH = pl.DeviceIdType.MESH


def far_first(k, z, nz):
    low = z < nz // 2
    me = jnp.where(low, z, nz - 1 - z)
    got = jnp.where(k < nz - 1 - me, nz - 1 - k, jnp.where(k == nz - 1, me, nz - 2 - k))
    return jnp.where(low, got, nz - 1 - got)


def summed_grads(grid, collective_id, operands, unit, shape, cut, name):
    rows, n = shape
    ra, rb = cut, rows - cut
    nz = grid.nz
    count = len(operands)

    def kernel(*refs):
        ins, out = refs[:count], refs[count]
        (sa, sb, ga, gb, oa, ob, xa, yb, ta, tb, ya, xb, la, lb, za, zb, ua, ub, da, db, ss, rs, zr) = refs[count + 1 :]
        d, c = lax.axis_index("dp"), lax.axis_index("ctx")
        z, y = d // grid.ny, d % grid.ny
        x, core = c // 2, c % 2
        at_sib = (d, c + 1 - 2 * core)
        at_x = (d, (1 - x) * 2 + core)
        at_y = (z * grid.ny + 1 - y, c)
        at_up = ((z + 1) * grid.ny + y, c)
        at_down = ((z - 1) * grid.ny + y, c)
        has_up, has_down = z < nz - 1, z > 0

        barrier = pltpu.get_barrier_semaphore()
        for target in (at_sib, at_x, at_y):
            pl.semaphore_signal(barrier, inc=1, device_id=target, device_id_type=MESH)

        @pl.when(has_up)
        def _():
            pl.semaphore_signal(barrier, inc=1, device_id=at_up, device_id_type=MESH)

        @pl.when(has_down)
        def _():
            pl.semaphore_signal(barrier, inc=1, device_id=at_down, device_id_type=MESH)

        pl.semaphore_wait(barrier, 3 + has_up.astype(jnp.int32) + has_down.astype(jnp.int32))

        def copy(src, dst, kind, k, target):
            return pltpu.make_async_remote_copy(
                src_ref=src,
                dst_ref=dst,
                send_sem=ss.at[kind, k],
                recv_sem=rs.at[kind, k],
                device_id=target,
                device_id_type=MESH,
            )

        def sib(k):
            s = k % 2
            return copy(sa.at[s], ga.at[k], 0, k, at_sib), copy(sb.at[s], gb.at[k], 1, k, at_sib)

        def first(k):
            s = k % 2
            return (
                copy(oa.at[s, 1 - x], xa.at[k], 2, k, at_x),
                copy(ob.at[s, 1 - y], yb.at[k], 3, k, at_y),
            )

        def second(k):
            s = k % 2
            return copy(ta.at[s], ya.at[k], 4, k, at_y), copy(tb.at[s], xb.at[k], 5, k, at_x)

        def line(k, to, up):
            dst = (ua, ub) if up else (da, db)
            target = at_up if up else at_down
            way = 0 if up else 1
            return [
                pltpu.make_async_remote_copy(
                    src_ref=(za, zb)[h].at[k],
                    dst_ref=dst[h].at[to],
                    send_sem=ss.at[6 + h, k],
                    recv_sem=zr.at[way, h, to],
                    device_id=target,
                    device_id_type=MESH,
                )
                for h in range(2)
            ]

        def step(t, _):
            @pl.when(t < nz)
            def _():
                k, s = t, t % 2
                to = far_first(k, z, nz)

                @pl.when(k >= 2)
                def _():
                    for cp in sib(k - 2):
                        cp.wait_send()
                    for cp in first(k - 2):
                        cp.wait_send()

                def store_sib(y_to, x_to, value):
                    sa[s, x_to, y_to] = value[:ra].astype(bf16)
                    sb[s, y_to, x_to] = value[ra:].astype(bf16)

                unit(ins, 1 - core, to, store_sib)
                for cp in sib(k):
                    cp.start()
                waits = sib(k)
                done = []

                def store_own(y_to, x_to, value):
                    if not done:
                        done.append(True)
                        for cp in waits:
                            cp.wait_recv()
                    oa[s, x_to, y_to] = (value[:ra] + ga[k, x_to, y_to].astype(f32)).astype(bf16)
                    ob[s, y_to, x_to] = (value[ra:] + gb[k, y_to, x_to].astype(f32)).astype(bf16)

                unit(ins, core, to, store_own)
                for cp in first(k):
                    cp.start()

            @pl.when((t >= 1) & (t <= nz))
            def _():
                k, s = t - 1, (t - 1) % 2

                @pl.when(k >= 2)
                def _():
                    for cp in second(k - 2):
                        cp.wait_send()

                one, two = first(k)
                one.wait_recv()
                ta[s] = (oa[s, x, 1 - y].astype(f32) + xa[k, 1 - y].astype(f32)).astype(bf16)
                go_a, go_b = second(k)
                go_a.start()
                la[s] = oa[s, x, y].astype(f32) + xa[k, y].astype(f32)
                two.wait_recv()
                tb[s] = (ob[s, y, 1 - x].astype(f32) + yb[k, 1 - x].astype(f32)).astype(bf16)
                go_b.start()
                lb[s] = ob[s, y, x].astype(f32) + yb[k, x].astype(f32)

            @pl.when(t >= 2)
            def _():
                k, s = t - 2, t % 2
                to = far_first(k, z, nz)
                one, two = second(k)
                one.wait_recv()
                two.wait_recv()
                la[s] = la[s] + ya[k].astype(f32)
                lb[s] = lb[s] + xb[k].astype(f32)
                for up in (True, False):
                    behind = has_down if up else has_up

                    @pl.when(((to > z) if up else (to < z)) & behind)
                    def _():
                        for cp in line(k, to, up):
                            cp.wait_recv()
                        la[s] = la[s] + (ua, da)[0 if up else 1][to].astype(f32)
                        lb[s] = lb[s] + (ub, db)[0 if up else 1][to].astype(f32)

                    @pl.when((to > z) if up else (to < z))
                    def _():
                        za[k] = la[s].astype(bf16)
                        zb[k] = lb[s].astype(bf16)
                        for cp in line(k, to, up):
                            cp.start()

            return 0

        lax.fori_loop(0, nz + 2, step, 0)
        last = (nz - 1) % 2
        for up in (True, False):

            @pl.when(has_down if up else has_up)
            def _():
                for cp in line(nz - 1, z, up):
                    cp.wait_recv()
                la[last] = la[last] + (ua, da)[0 if up else 1][z].astype(f32)
                lb[last] = lb[last] + (ub, db)[0 if up else 1][z].astype(f32)

        out[:ra] = la[last]
        out[ra:] = lb[last]
        for k in range(nz - 2, nz):
            for cp in (*sib(k), *first(k), *second(k)):
                cp.wait_send()
        for k in range(nz - 1):
            for cp in line(k, 0, True):
                cp.wait_send()

    def vm(*dims, dtype=bf16):
        return pltpu.VMEM(dims, dtype)

    halves = [
        *(vm(2, 2, 2, h, n) for h in (ra, rb)),
        *(vm(nz, 2, 2, h, n) for h in (ra, rb)),
        *(vm(2, 2, 2, h, n) for h in (ra, rb)),
        *(vm(nz, 2, h, n) for h in (ra, rb)),
        *(vm(2, h, n) for h in (ra, rb)),
        *(vm(nz, h, n) for h in (ra, rb)),
        *(vm(2, h, n, dtype=f32) for h in (ra, rb)),
        *(vm(nz, h, n) for h in (ra, rb)),
        *(vm(nz, h, n) for h in (ra, rb)),
        *(vm(nz, h, n) for h in (ra, rb)),
    ]
    flops = sum(2 * 2 * 2 * nz * grid.ny * rows * n * 512 for _ in range(1))
    return pl.pallas_call(
        kernel,
        out_shape=jax.ShapeDtypeStruct((rows, n), f32),
        in_specs=[pl.BlockSpec(memory_space=pltpu.VMEM)] * count,
        out_specs=pl.BlockSpec(memory_space=pltpu.VMEM),
        scratch_shapes=[
            *halves,
            pltpu.SemaphoreType.DMA((8, nz)),
            pltpu.SemaphoreType.DMA((6, nz)),
            pltpu.SemaphoreType.DMA((2, 2, nz)),
        ],
        compiler_params=pltpu.CompilerParams(
            collective_id=collective_id, has_side_effects=True, vmem_limit_bytes=VMEM_LIMIT
        ),
        cost_estimate=cost(flops, 100_000_000),
        name=name,
    )(*operands)


def near_first(k, z, nz):
    return far_first(nz - 1 - k, z, nz)


def forward_gather(grid, x_in, g_in, weights, vectors, seg_col, seg_row, seg_other):
    _, rows, width = x_in.shape
    tokens = 2 * rows
    nz = grid.nz
    parts, groups = grid.dp, grid.ctx
    wide = pl.cdiv(width, LANES) * LANES
    pairs = wide // LANES
    n_qkv, n_out, n_fc = (w.shape[1] for w in weights[:3])
    slab = weights[0].shape[0]
    ff = weights[3].shape[1]
    n_vec = vectors.shape[1]
    n_bias = n_out
    n_slots = 4 * nz

    def kernel(
        x_own, g_own, wq_in, wo_in, wf_in, wp_in, vec_in, sc_ref, sr_ref, so_ref,
        gq, go, gf, gp, vec_out, slope_out, act_out, sib_out, x_out, g_out, n1t_out, n2t_out, att_out, dw_out,
        q_out, k_out, v_out, of_out, lse_out, hid_out,
        q_ref, k_ref, v_ref, of_ref, lse_ref, hid_ref, x_ref, n1_ref, att_ref, flip, sib, vbuf, rowbuf, jrow, wqkv, wbig, wout, stage_u, stage_a, stage_w, mq, mo, mf, mp,
        s_z, r_z, s_p, r_p, s_vz, r_vz, s_vy, r_vy, s_kv, r_kv, s_loc, s_w, s_st, s_sh, r_sh, s_fl, s_out, s_dw,
    ):
        d, c = lax.axis_index("dp"), lax.axis_index("ctx")
        z, y = d // grid.ny, d % grid.ny
        x, core = c // 2, c % 2
        extra = 1 - core
        at_sib = (d, c + 1 - 2 * core)
        at_x = (d, (1 - x) * 2 + core)
        at_y = (z * grid.ny + 1 - y, c)
        at_up = ((z + 1) * grid.ny + y, c)
        at_down = ((z - 1) * grid.ny + y, c)
        has_up, has_down = z < nz - 1, z > 0
        gathered = (gq, go, gf, gp)
        mine = (mq, mo, mf, mp)
        cuts = [(w.shape[0] * 2 // 5 + 7) // 8 * 8 for w in weights]
        at_cross = (d, (1 - x) * 2 + 1 - core)
        n2_ref = n1_ref

        def piece(w, zz, yy, xx, cc, half=None):
            h = weights[w].shape[0]
            tail = () if half is None else ((pl.ds(0, cuts[w]) if half == 0 else pl.ds(cuts[w], h - cuts[w])),)
            index = (zz, yy, xx, cc) if w < 3 else (xx, cc, zz, yy)
            return gathered[w].at[(*index, *tail)]

        def remote(src, dst, send, recv, target):
            return pltpu.make_async_remote_copy(
                src_ref=src, dst_ref=dst, send_sem=send, recv_sem=recv, device_id=target, device_id_type=MESH
            )

        every = slice(None)

        def part_copy(w, kind, j):
            zz = near_first(j, z, nz)
            src, target = (
                (piece(w, zz, y, x, core, 0), at_y),
                (piece(w, zz, y, x, core, 1), at_x),
                (piece(w, zz, every, x, core, 0), at_x),
                (piece(w, zz, y, every, core, 1), at_y),
                (piece(w, zz, every, every, core), at_sib),
            )[kind]
            return remote(src, src, s_p.at[w, kind, j], r_p.at[w, kind, j], target)

        def z_copy(w, zz, way, j):
            src = piece(w, zz, y, x, core)
            return remote(src, src, s_z.at[w, way, j], r_z.at[w, zz], (at_up, at_down)[way])

        def vz_copy(zz, way, j):
            src = vbuf.at[zz, y]
            return remote(src, src, s_vz.at[way, j], r_vz.at[zz], (at_up, at_down)[way])

        def vy_copy(j):
            src = vbuf.at[near_first(j, z, nz), y]
            return remote(src, src, s_vy.at[j], r_vy.at[j], at_y)

        def passes_on(j):
            zz = near_first(j, z, nz)
            return zz, (zz < z) & has_up, (zz > z) & has_down

        def z_arrived(w, j):
            zz = near_first(j, z, nz)
            z_copy(w, zz, 0, j).wait_recv()
            if w == 0:
                vz_copy(zz, 0, j).wait_recv()

        def z_send(w, zz, way, j):
            z_copy(w, zz, way, j).start()
            if w == 0:
                vz_copy(zz, way, j).start()

        def pass_on(i):
            w, j = divmod(i, nz)
            if j == 0:

                @pl.when(has_up)
                def _():
                    z_send(w, z, 0, 0)

                @pl.when(has_down)
                def _():
                    z_send(w, z, 1, 0)

                return
            zz, up, down = passes_on(j)
            for way, flag in ((0, up), (1, down)):

                @pl.when(flag)
                def _():
                    z_arrived(w, j)
                    z_send(w, zz, way, j)

        def across(kind, p, target):
            src, dst = moved[kind]
            at = pl.ds(p * (rows // nz), rows // nz)
            return remote(src.at[1 - x, at], dst.at[x, at], s_sh.at[kind, p], r_sh.at[kind, p], target)

        def within(kind):
            src, dst = moved[kind]
            return remote(src.at[1], dst.at[1], s_sh.at[kind, nz], r_sh.at[kind, nz], at_sib)

        def stays(kind):
            src, dst = moved[kind]
            return pltpu.make_async_copy(src.at[0], dst.at[0], s_sh.at[kind, nz])

        moved = ((x_own, x_ref), (g_own, g_out))

        def move(kind, p):
            @pl.when(x == 0)
            def _():
                across(kind, p, at_x).start()
                if p == 0:
                    stays(kind).start()

            @pl.when(x == 1)
            def _():
                across(kind, p, at_cross).start()
                if p == 0:
                    within(kind).start()

        def moved_in(kind):
            for p in range(nz):
                across(kind, p, at_x).wait_recv()

            @pl.when(x == 0)
            def _():
                stays(kind).wait()

            @pl.when(x == 1)
            def _():
                within(kind).wait_recv()

        def moved_out(kind):
            for p in range(nz):
                across(kind, p, at_x).wait_send()

            @pl.when(x == 1)
            def _():
                within(kind).wait_send()

        def tick(i):
            if i < n_slots:
                w, j = divmod(i, nz)
                if j > 0:
                    _, up, down = passes_on(j)

                    @pl.when(jnp.logical_not(up | down))
                    def _():
                        z_arrived(w, j)

                part_copy(w, 0, j).start()
                part_copy(w, 1, j).start()
                if w == 0:
                    vy_copy(j).start()
            if 0 <= i - 1 < n_slots:
                w, j = divmod(i - 1, nz)
                part_copy(w, 0, j).wait_recv()
                part_copy(w, 2, j).start()
                part_copy(w, 1, j).wait_recv()
                part_copy(w, 3, j).start()
            if 0 <= i - 2 < n_slots:
                w, j = divmod(i - 2, nz)
                part_copy(w, 2, j).wait_recv()
                part_copy(w, 3, j).wait_recv()
                part_copy(w, 4, j).start()
            if i + 1 < n_slots and (i + 1) % nz != 0:
                pass_on(i + 1)
            if i % nz == 1 and i + nz - 1 < n_slots:
                pass_on(i + nz - 1)
            if i // nz in (0, 2):
                move(i // nz // 2, i % nz)

        def complete(w):
            for j in range(nz):
                part_copy(w, 4, j).wait_recv()

        barrier = pltpu.get_barrier_semaphore()
        for target in (at_sib, at_x, at_y, at_cross):
            pl.semaphore_signal(barrier, inc=1, device_id=target, device_id_type=MESH)

        @pl.when(has_up)
        def _():
            pl.semaphore_signal(barrier, inc=1, device_id=at_up, device_id_type=MESH)

        @pl.when(has_down)
        def _():
            pl.semaphore_signal(barrier, inc=1, device_id=at_down, device_id_type=MESH)

        sources = (wq_in, wo_in, wf_in, wp_in)
        into = [pltpu.make_async_copy(src, mine[w], s_loc.at[w]) for w, src in enumerate(sources)]
        into.append(pltpu.make_async_copy(vec_in, vbuf.at[z, y], s_loc.at[4]))
        for cp in into:
            cp.start()
        for ref in (q_ref, k_ref, v_ref):
            ref[:, :, wide - LANES :] = jnp.zeros((2, rows, LANES), bf16)
        jrow[...] = jnp.zeros_like(jrow)
        for cp in into:
            cp.wait()
        local = [
            pltpu.make_async_copy(mine[w], piece(w, z, y, x, core), s_loc.at[w]) for w in range(4)
        ]
        for cp in local:
            cp.start()
        for cp in local:
            cp.wait()
        pl.semaphore_wait(barrier, 4 + has_up.astype(jnp.int32) + has_down.astype(jnp.int32))

        pass_on(0)
        for i in range(nz + 1):
            tick(i)
        moved_in(0)
        keep_x = pltpu.make_async_copy(x_ref, x_out, s_loc.at[2])
        keep_x.start()
        for j in range(nz):
            vy_copy(j).wait_recv()

        for part in range(parts):
            line = vbuf[part // grid.ny, part % grid.ny]
            cols = slice(part * n_bias, (part + 1) * n_bias)
            for v in range(8):
                term = line[0:1, n_fc + v * n_bias : n_fc + (v + 1) * n_bias]
                if v < 2:
                    jrow[0:1, 2 * v * width + cols.start : 2 * v * width + cols.stop] = term
                else:
                    rowbuf[v : v + 1, cols] = term
        for s in range(2):
            values = x_ref[s].astype(f32)
            n1_ref[s] = layer_norm(values, rowbuf[4:5, :], rowbuf[5:6, :]).astype(bf16)

        for i in range(nz + 1, nz + 3):
            tick(i)

        def flipped(dst):
            return pltpu.make_async_copy(flip, dst, s_fl.at[0])

        def turn(value, dst, before):
            if before is not None:
                flipped(before).wait()
            flip[...] = value.T
            flipped(dst).start()

        turn(n1_ref[...].reshape(tokens, width), n1t_out, None)
        complete(0)

        def stream(source, buffer, body, hooks):
            def load(part):
                return pltpu.make_async_copy(
                    source.at[part // grid.ny, part % grid.ny], buffer.at[part % 2], s_w.at[part % 2]
                )

            load(0).start()

            def step(part, _):
                load(part).wait()

                @pl.when(part + 1 < parts)
                def _():
                    load(part + 1).start()

                body(part, part % 2)
                for when, todo in hooks.items():

                    @pl.when(part == when)
                    def _():
                        for i in todo:
                            tick(i)

                return 0

            lax.fori_loop(0, parts, step, 0)

        def project(part, slot):
            left = n1_ref[...].reshape(tokens, width)
            product = dot_nn(left, wqkv[slot].reshape(width, n_qkv))
            for p in range(parts):

                @pl.when(part == p)
                def _():
                    first, last = p * n_qkv, (p + 1) * n_qkv
                    out = (product + jrow[0:1, first:last]).astype(bf16).reshape(2, rows, n_qkv)
                    for g, ref in enumerate((q_ref, k_ref, v_ref)):
                        lo, hi = max(first, g * width), min(last, (g + 1) * width)
                        if lo < hi:
                            ref[:, :, lo - g * width : hi - g * width] = out[:, :, lo - first : hi - first]

        stream(gq, wqkv, project, {0: [nz + 3], 4: [nz + 4]})
        swaps = [
            remote(ref, sib.at[kind], s_kv.at[kind], r_kv.at[kind], at_sib)
            for kind, ref in enumerate((k_ref, v_ref))
        ]
        results = (
            (q_ref, q_out), (k_ref, k_out), (v_ref, v_out), (of_ref, of_out), (lse_ref, lse_out), (hid_ref, hid_out)
        )
        saved = [pltpu.make_async_copy(src, dst, s_out.at[i]) for i, (src, dst) in enumerate(results)]
        for cp in (*swaps, *saved[:3]):
            cp.start()
        for cp in swaps:
            cp.wait_recv()
        tick(nz + 5)

        def attend(p, _):
            lanes = pl.ds(pl.multiple_of(p * LANES, LANES), LANES)
            got = pair_forward(
                extra,
                lambda i: q_ref[i, :, lanes],
                lambda i: k_ref[i, :, lanes],
                lambda i: v_ref[i, :, lanes],
                lambda i: sib[0, i, :, lanes],
                lambda i: sib[1, i, :, lanes],
                lambda i: sc_ref[i],
                lambda i: sr_ref[i],
                lambda i: so_ref[i],
                pair_masks(p, width),
            )
            for slot, (out, logs) in enumerate(got):
                att_ref[slot, :, lanes] = out.astype(bf16)
                of_ref[slot, :, lanes] = out
                lse_ref[slot, :, lanes] = logs

            @pl.when(p == pairs // 2)
            def _():
                tick(nz + 6)

            return 0

        lax.fori_loop(0, pairs, attend, 0)
        keep = pltpu.make_async_copy(sib, sib_out, s_loc.at[0])
        for cp in (keep, *saved[3:5]):
            cp.start()
        complete(1)
        turn(att_ref[:, :, :width].reshape(tokens, width), att_out, n1t_out)

        def branch(part, slot):
            product = dot_nn(
                att_ref[:, :, :width].reshape(tokens, width), wout[slot].reshape(width, n_out)
            ).reshape(2, rows, n_out)
            for p in range(parts):

                @pl.when(part == p)
                def _():
                    hid_ref[:, :, p * n_out : (p + 1) * n_out] = product

        stream(go, wout, branch, {0: [nz + 7]})
        for s in range(2):
            hidden = x_ref[s].astype(f32) + hid_ref[s] + rowbuf[2:3, :]
            hid_ref[s] = hidden
            n2_ref[s] = layer_norm(hidden, rowbuf[6:7, :], rowbuf[7:8, :]).astype(bf16)
        saved[5].start()
        tick(nz + 8)
        turn(n2_ref[...].reshape(tokens, width), n2t_out, att_out)
        tick(nz + 9)
        moved_in(1)
        for half in range(2):
            fetch = pltpu.make_async_copy(
                g_out.at[half], stage_a.at[0, pl.ds(half * rows, rows)], s_loc.at[3]
            )
            fetch.start()
            fetch.wait()
        flipped(n2t_out).wait()
        flip[...] = stage_a[0].T
        complete(2)
        band = width // nz

        def save_w(i):
            return pltpu.make_async_copy(
                stage_w.at[i % 2], dw_out.at[i // nz, pl.ds(pl.multiple_of(i % nz * band, 16), band)], s_dw.at[i % 2]
            )

        def proj_terms(group):
            def body(i, _):
                @pl.when(i >= 2)
                def _():
                    save_w(i - 2).wait()

                at = pl.ds(pl.multiple_of(i % nz * band, 16), band)
                stage_w[i % 2] = dot_nn(flip[at, :], stage_a[group % 2]).astype(bf16)
                save_w(i).start()
                return 0

            lax.fori_loop(group * nz, (group + 1) * nz, body, 0)

        ratio = parts // groups

        def saves(group):
            slot = group % 2
            return (
                pltpu.make_async_copy(stage_u.at[slot], slope_out.at[group], s_st.at[0, slot]),
                pltpu.make_async_copy(stage_a.at[slot], act_out.at[group], s_st.at[1, slot]),
            )

        def feed(part, slot):
            group, place = part // ratio, part % ratio

            @pl.when((place == 0) & (group >= 2))
            def _():
                for cp in saves(group - 2):
                    cp.wait()

            left = n2_ref[...].reshape(tokens, width)
            u = dot_nn(left, wbig[slot].reshape(width, n_fc))
            u = u + vbuf[part // grid.ny, part % grid.ny][0:1, :n_fc]
            t = jnp.tanh(GELU_C * (u + GELU_A * u * u * u))
            act = (0.5 * u * (1.0 + t)).astype(bf16)
            slope = 0.5 * (1.0 + t) + 0.5 * u * (1.0 - t * t) * (GELU_C * (1.0 + 3.0 * GELU_A * u * u))
            slope = slope.astype(bf16)
            for r in range(ratio):

                @pl.when(place == r)
                def _():
                    stage_u[group % 2, :, r * n_fc : (r + 1) * n_fc] = slope
                    stage_a[group % 2, :, r * n_fc : (r + 1) * n_fc] = act

            @pl.when(place == ratio - 1)
            def _():
                for cp in saves(group):
                    cp.start()
                proj_terms(group)

        stream(gf, wbig, feed, {0: [nz + 10], 3: [nz + 11], 6: [nz + 12]})
        tick(nz + 13)
        save_vec = pltpu.make_async_copy(vbuf, vec_out, s_loc.at[1])
        save_vec.start()
        for group in range(groups - 2, groups):
            for cp in saves(group):
                cp.wait()
        for i in range(groups * nz - 2, groups * nz):
            save_w(i).wait()
        for cp in (keep, keep_x, *saved):
            cp.wait()
        save_vec.wait()
        complete(3)
        for kind in range(2):
            moved_out(kind)
        for cp in swaps:
            cp.wait_send()

        def finish(j, _):
            zz, up, down = passes_on(j)
            up, down = up | ((j == 0) & has_up), down | ((j == 0) & has_down)
            vy_copy(j).wait_send()
            for w in range(4):
                for kind in range(5):
                    part_copy(w, kind, j).wait_send()
                for way, flag in ((0, up), (1, down)):

                    @pl.when(flag)
                    def _():
                        z_copy(w, zz, way, j).wait_send()
                        if w == 0:
                            vz_copy(zz, way, j).wait_send()

            return 0

        lax.fori_loop(0, nz, finish, 0)

    any_, vm = pl.BlockSpec(memory_space=pl.ANY), pl.BlockSpec(memory_space=pltpu.VMEM)
    dma = pltpu.SemaphoreType.DMA
    columns = [
        jax.ShapeDtypeStruct((nz, grid.ny, grid.nx, 2, *w.shape), bf16) for w in weights[:3]
    ]
    wide_low = jax.ShapeDtypeStruct((2, rows, wide), bf16)
    wide_full = jax.ShapeDtypeStruct((2, rows, wide), f32)
    low = jax.ShapeDtypeStruct((2, rows, width), bf16)
    out_shape = [
        *columns,
        jax.ShapeDtypeStruct((grid.nx, 2, nz, grid.ny, *weights[3].shape), bf16),
        jax.ShapeDtypeStruct((nz, grid.ny, 8, n_vec), f32),
        jax.ShapeDtypeStruct((groups, tokens, ff), bf16),
        jax.ShapeDtypeStruct((groups, tokens, ff), bf16),
        jax.ShapeDtypeStruct((2, 2, rows, wide), bf16),
        low,
        low,
        *[jax.ShapeDtypeStruct((width, tokens), bf16)] * 3,
        jax.ShapeDtypeStruct((groups, width, ff), bf16),
        wide_low,
        wide_low,
        wide_low,
        wide_full,
        wide_full,
        jax.ShapeDtypeStruct((2, rows, width), f32),
    ]
    return pl.pallas_call(
        kernel,
        out_shape=out_shape,
        in_specs=[any_] * 7 + [vm] * 3,
        out_specs=[any_] * 20,
        scratch_shapes=[
            *[pltpu.VMEM((2, rows, wide), bf16)] * 3,
            *[pltpu.VMEM((2, rows, wide), f32)] * 2,
            pltpu.VMEM((2, rows, width), f32),
            pltpu.VMEM((2, rows, width), bf16),
            pltpu.VMEM((2, rows, width), bf16),
            pltpu.VMEM((2, rows, wide), bf16),
            pltpu.VMEM((width, tokens), bf16),
            pltpu.VMEM((2, 2, rows, wide), bf16),
            pltpu.VMEM((nz, grid.ny, 8, n_vec), f32),
            pltpu.VMEM((8, width), f32),
            pltpu.VMEM((8, 3 * width), f32),
            pltpu.VMEM((2, grid.nx, 2, slab, n_qkv), bf16),
            pltpu.VMEM((2, grid.nx, 2, slab, n_fc), bf16),
            pltpu.VMEM((2, grid.nx, 2, slab, n_out), bf16),
            pltpu.VMEM((2, tokens, ff), bf16),
            pltpu.VMEM((2, tokens, ff), bf16),
            pltpu.VMEM((2, width // nz, ff), bf16),
            *(pltpu.VMEM(w.shape, bf16) for w in weights),
            dma((4, 2, nz)),
            dma((4, nz)),
            dma((4, 5, nz)),
            dma((4, 5, nz)),
            dma((2, nz)),
            dma((nz,)),
            dma((nz,)),
            dma((nz,)),
            dma((2,)),
            dma((2,)),
            dma((5,)),
            dma((2,)),
            dma((2, 2)),
            dma((2, nz + 1)),
            dma((2, nz + 1)),
            dma((1,)),
            dma((6,)),
            dma((2,)),
        ],
        compiler_params=pltpu.CompilerParams(
            collective_id=4, has_side_effects=True, vmem_limit_bytes=VMEM_LIMIT
        ),
        cost_estimate=cost(30e9, 150e6),
        name="forward",
    )(x_in, g_in, *weights, vectors, seg_col, seg_row, seg_other)


def backward_sums(
    grid, grad, proj_terms, act, slope, w_proj, hidden, normed_t, w_fc, w_out, queries, keys, values, other,
    att_full, logs, x_in, first_t, att_t, w_qkv, vec_rows, seg_row, seg_col, seg_other,
):
    tokens, width = grad.shape
    rows = tokens // 2
    nz, parts, groups = grid.nz, grid.dp, grid.ctx
    wide = queries.shape[2]
    pairs = wide // LANES
    ff, n_fc, n_out = act.shape[2], w_fc.shape[2], w_out.shape[2]
    n_qkv = 3 * width // parts
    slab = width // groups
    cols = width // parts
    ratio = parts // groups
    h, n = cols * 2 // 5 // 16 * 16, ff
    low_half = slab // 2
    v_rows = 8 + parts
    chunk = min(rows, 64)
    units = 3 * nz

    def kernel(
        g_in, dw_in, act_in, u_in, wp_in, hid_in, nt_in, wf_in, wo_in, q_in, k_in, v_in, s_in, of_in, lse_in,
        x_in, n1t_in, at_in, wq_in, vr_ref, rq_ref, ck_ref, cs_ref,
        gp_out, gf_out, gq_out, sum_ref, y_out, di_out, dx_out, hg_out, bg_out, pg_out, ig_out,
        sa, sb, ga, gb, oa, ob, xa, yb, ta, tb, ya, xb, la, lb, za, zb, ra, rb, swap, v_send, v_got,
        ss, rs, zss, zrs, s_ld, s_st, s_tile, s_kv, s_vec, r_vec, s_back, r_back, s_out, s_dw,
    ):
        d, c = lax.axis_index("dp"), lax.axis_index("ctx")
        z, y = d // grid.ny, d % grid.ny
        x, core = c // 2, c % 2
        extra = 1 - core
        at_sib = (d, c + 1 - 2 * core)
        at_x = (d, (1 - x) * 2 + core)
        at_y = (z * grid.ny + 1 - y, c)
        at_cross = (d, (1 - x) * 2 + 1 - core)
        at_up = ((z + 1) * grid.ny + y, c)
        at_down = ((z - 1) * grid.ny + y, c)
        has_up, has_down = z < nz - 1, z > 0

        def remote(src, dst, send, recv, target):
            return pltpu.make_async_remote_copy(
                src_ref=src, dst_ref=dst, send_sem=send, recv_sem=recv, device_id=target, device_id_type=MESH
            )

        def copy(src, dst, kind, u, target):
            return remote(src, dst, ss.at[kind, u], rs.at[kind, u], target)

        def sib(u):
            return copy(sa, ga.at[u % 2], 0, u, at_sib), copy(sb, gb.at[u % 2], 1, u, at_sib)

        def first(u):
            return copy(oa.at[1 - x], xa.at[u % 2], 2, u, at_x), copy(ob.at[1 - y], yb.at[u % 2], 3, u, at_y)

        def second(u):
            return copy(ta, ya.at[u % 3], 4, u, at_y), copy(tb, xb.at[u % 3], 5, u, at_x)

        def line(u, to, up, place):
            group, k = divmod(u, nz)
            target = at_up if up else at_down
            return [
                remote(
                    (za, zb)[i].at[min(k, nz - 2)],
                    (ra, rb)[i].at[group % 2, place],
                    zss.at[i, u],
                    zrs.at[i, group, place],
                    target,
                )
                for i in range(2)
            ]

        def add_arrived(u, place):
            for cp in line(u, 0, True, place):
                cp.wait_recv()
            la[u % 2] += ra[u // nz % 2, place].astype(f32)
            lb[u % 2] += rb[u // nz % 2, place].astype(f32)

        def target_z(u):
            return far_first(u % nz, z, nz)

        def finish(u):
            at_end = jnp.logical_not(has_up & has_down)

            @pl.when(jnp.logical_not(at_end))
            def _():
                finish_unit(u)

            @pl.when(at_end)
            def _():
                if u % nz == nz - 1:
                    finish_unit(u)
                if (u + 1) % nz != nz - 1:
                    finish_unit(u + 1)

        def finish_unit(u):
            if 0 <= u < units:
                to = target_z(u)
                for cp in second(u):
                    cp.wait_recv()
                la[u % 2] += ya[u % 3].astype(f32)
                lb[u % 2] += xb[u % 3].astype(f32)
                if u % nz == nz - 1:

                    @pl.when(has_down)
                    def _():
                        add_arrived(u, z)

                    @pl.when(has_up)
                    def _():
                        add_arrived(u, nz)

                    out = (gp_out, gf_out, gq_out)[u // nz]
                    done = [
                        pltpu.make_async_copy(src, out.at[at], s_out.at[i])
                        for i, (src, at) in enumerate(
                            ((la.at[u % 2], pl.ds(0, h)), (lb.at[u % 2], pl.ds(h, cols - h)))
                        )
                    ]
                    for cp in done:
                        cp.start()
                    for cp in done:
                        cp.wait()
                else:
                    for up in (True, False):
                        going = (to > z) if up else (to < z)

                        @pl.when(going & (has_down if up else has_up))
                        def _():
                            add_arrived(u, to)

                        @pl.when(going)
                        def _():
                            if u >= nz:
                                for cp in line(u - nz, 0, up, 0):
                                    cp.wait_send()
                            za[u % nz] = la[u % 2].astype(bf16)
                            zb[u % nz] = lb[u % 2].astype(bf16)
                            place = to if up else jnp.where(to == z - 1, nz, to)
                            for cp in line(u, to, up, place):
                                cp.start()

        def second_stage(u):
            if 0 <= u < units:
                if u >= 1:
                    for cp in second(u - 1):
                        cp.wait_send()
                for cp in first(u):
                    cp.wait_recv()
                s = u % 2
                go_a, go_b = second(u)
                ta[...] = oa[x, 1 - y] + xa[s, 1 - y]
                go_a.start()
                tb[...] = ob[y, 1 - x] + yb[s, 1 - x]
                go_b.start()
                la[s] = oa[x, y].astype(f32) + xa[s, y].astype(f32)
                lb[s] = ob[y, x].astype(f32) + yb[s, x].astype(f32)
        def give(u, unit):
            if u >= 1:
                for cp in sib(u - 1):
                    cp.wait_send()

            def store(y_to, x_to, value):
                sa[x_to, y_to] = value[:h].astype(bf16)
                sb[y_to, x_to] = value[h:].astype(bf16)

            if u < nz:
                take_terms(u, 1 - core, sa, sb)
            else:
                unit(target_z(u), 1 - core, store)
            for cp in sib(u):
                cp.start()

        def take_terms(u, plane, to_a, to_b):
            loads = []
            for y_to in range(2):
                first_row = pl.multiple_of((target_z(u) * grid.ny + y_to) * cols, 8)
                for x_to in range(2):
                    src = dw_in.at[2 * x_to + plane]
                    loads += [
                        pltpu.make_async_copy(
                            src.at[pl.ds(first_row, h)], to_a.at[x_to, y_to], s_dw.at[0, y_to, x_to]
                        ),
                        pltpu.make_async_copy(
                            src.at[pl.ds(pl.multiple_of(first_row + h, 8), cols - h)],
                            to_b.at[y_to, x_to],
                            s_dw.at[1, y_to, x_to],
                        ),
                    ]
            for cp in loads:
                cp.start()
            for cp in loads:
                cp.wait()

        def begin_unit(u, unit):
            if u < units:
                s = u % 2
                if u % nz == 0:
                    give(u, unit)
                if u >= 1:
                    for cp in first(u - 1):
                        cp.wait_send()
                if u < nz:
                    take_terms(u, core, oa, ob)
                for cp in sib(u):
                    cp.wait_recv()

                def store(y_to, x_to, value):
                    oa[x_to, y_to] = (value[:h] + ga[s, x_to, y_to].astype(f32)).astype(bf16)
                    ob[y_to, x_to] = (value[h:] + gb[s, y_to, x_to].astype(f32)).astype(bf16)

                if u < nz:
                    oa[...] = oa[...] + ga[s]
                    ob[...] = ob[...] + gb[s]
                else:
                    unit(target_z(u), core, store)
                for cp in first(u):
                    cp.start()
                if (u + 1) % nz != 0:
                    give(u + 1, unit)

        def tick(t, unit=None):
            finish(t - 3)
            second_stage(t - 1)
            begin_unit(t, unit)

        def beside(term):
            return jnp.concatenate([term[:low_half], term[low_half:]], axis=1)

        barrier = pltpu.get_barrier_semaphore()
        for target in (at_sib, at_x, at_y, at_cross):
            pl.semaphore_signal(barrier, inc=1, device_id=target, device_id_type=MESH)

        @pl.when(has_up)
        def _():
            pl.semaphore_signal(barrier, inc=1, device_id=at_up, device_id_type=MESH)

        @pl.when(has_down)
        def _():
            pl.semaphore_signal(barrier, inc=1, device_id=at_down, device_id_type=MESH)

        pl.semaphore_wait(barrier, 4 + has_up.astype(jnp.int32) + has_down.astype(jnp.int32))

        def back_far(kind, src, dst, target):
            return remote(src.at[1 - x], dst.at[x], s_back.at[kind, 0], r_back.at[kind, 0], target)

        def back_near(kind, src, dst):
            return remote(src.at[1], dst.at[1], s_back.at[kind, 1], r_back.at[kind, 1], at_sib)

        def back_stay(kind, src, dst):
            return pltpu.make_async_copy(src.at[0], dst.at[0], s_back.at[kind, 1])

        def give_back(kind, src, dst):
            @pl.when(x == 0)
            def _():
                back_far(kind, src, dst, at_cross).start()
                back_stay(kind, src, dst).start()

            @pl.when(x == 1)
            def _():
                back_far(kind, src, dst, at_x).start()
                back_near(kind, src, dst).start()

        def given_back(kind, src, dst):
            back_far(kind, src, dst, at_x).wait_send()

            @pl.when(x == 0)
            def _():
                back_stay(kind, src, dst).wait()

            @pl.when(x == 1)
            def _():
                back_near(kind, src, dst).wait_send()

        def got_back(kind, src, dst):
            back_far(kind, src, dst, at_x).wait_recv()

            @pl.when(x == 1)
            def _():
                back_near(kind, src, dst).wait_recv()

        def vec_copy(i, target):
            return remote(v_send.at[i], v_got.at[i], s_vec.at[i], r_vec.at[i], target)

        def vec_step(i):
            targets = (at_sib, at_x, at_y)
            if 1 <= i <= 3:
                vec_copy(i - 1, targets[i - 1]).wait()
                sum_ref[...] += v_got[i - 1]
            if i < 3:
                v_send[i] = sum_ref[...]
                vec_copy(i, targets[i]).start()
                return
            if i == 3:
                ways = ((3, has_up, has_down, at_up), (4, has_down, has_up, at_down))
                for slot, going, behind, target in ways:
                    v_send[slot] = sum_ref[...]

                    @pl.when(going & jnp.logical_not(behind))
                    def _():
                        vec_copy(slot, target).start()

                for slot, going, behind, target in ways:

                    @pl.when(behind)
                    def _():
                        vec_copy(slot, target).wait_recv()
                        v_send[slot] += v_got[slot]

                    @pl.when(going & behind)
                    def _():
                        vec_copy(slot, target).start()

                return
            for slot, going, behind, target in ((3, has_up, has_down, at_up), (4, has_down, has_up, at_down)):

                @pl.when(behind)
                def _():
                    sum_ref[...] += v_got[slot]

                @pl.when(going)
                def _():
                    vec_copy(slot, target).wait_send()

        def load(src, dst, sem):
            return pltpu.make_async_copy(src, dst, s_ld.at[sem])

        def first_phase(g, acts, w, u, ig_st, total):
            begin = load(g_in, g, 3)
            begin.start()
            tick(0)

            def fetch(group):
                return load(wp_in.at[group], w, 4), load(u_in.at[group], u, 5)

            for cp in fetch(0):
                cp.start()
            begin.wait()
            sum_ref[0:1, :] = jnp.sum(g[...].astype(f32), axis=0, keepdims=True)
            hid = load(hid_in, total, 6)
            hid.start()
            hid.wait()

            def save(group):
                return pltpu.make_async_copy(ig_st, ig_out.at[pl.ds(group * ratio, ratio)], s_st.at[0])

            def body(group, _):
                for cp in fetch(group):
                    cp.wait()
                act_load = load(act_in.at[group], acts, 0)
                act_load.start()

                @pl.when(group > 0)
                def _():
                    save(group - 1).wait()

                out = (dot_nn(g[...], w[...]) * u[...].astype(f32)).astype(bf16)
                sums = jnp.sum(out.astype(f32), axis=0, keepdims=True)
                for r in range(ratio):
                    ig_st[r] = out[:, r * n_fc : (r + 1) * n_fc]
                    sum_ref[pl.ds(8 + group * ratio + r, 1), :n_fc] = sums[:, r * n_fc : (r + 1) * n_fc]
                save(group).start()
                act_load.wait()
                total[...] += dot_nt(acts[...], w[...])

                @pl.when(group + 1 < groups)
                def _():
                    for cp in fetch(group + 1):
                        cp.start()

                for i in range(nz - 1):

                    @pl.when(group == i)
                    def _():
                        tick(1 + i)

                return 0

            lax.fori_loop(0, groups, body, 0)
            save(groups - 1).wait()
            result = (total[...] + vr_ref[0:1, :]).astype(bf16)
            swap[0, :, :, :width] = result.reshape(2, rows, width)
            give_back(0, swap.at[0], y_out)

        low_rows = pltpu.VMEM((tokens, width), bf16)
        full_rows = pltpu.VMEM((tokens, width), f32)
        pl.run_scoped(
            first_phase,
            low_rows,
            pltpu.VMEM((tokens, ff), bf16),
            pltpu.VMEM((width, ff), bf16),
            pltpu.VMEM((tokens, ff), bf16),
            pltpu.VMEM((ratio, tokens, n_fc), bf16),
            full_rows,
        )

        def second_phase(nt, igs):
            def fc_unit(to, plane, store):
                loads = [load(ig_out.at[to * grid.ny + y_to], igs.at[y_to], y_to) for y_to in range(2)]
                for cp in loads:
                    cp.start()
                for cp in loads:
                    cp.wait()

                def body(i, _):
                    y_to, x_to = i // 2, i % 2
                    at = pl.ds(pl.multiple_of((2 * x_to + plane) * slab, 16), slab)
                    store(y_to, x_to, beside(dot_nn(nt[at, :], igs[y_to])))
                    return 0

                lax.fori_loop(0, 4, body, 0)

            begin = load(nt_in, nt, 2)
            begin.start()
            begin.wait()
            tick(nz, fc_unit)

            def second_norm(dn, hid):
                hid_load = load(hid_in, hid, 7)
                hid_load.start()
                dn[...] = jnp.zeros_like(dn)
                pl.run_scoped(
                    functools.partial(back_feed, dn),
                    pltpu.VMEM((2, width, n_fc), bf16),
                    pltpu.VMEM((2, tokens, n_fc), bf16),
                )
                finish_norm(dn, hid, hid_load)

            def back_feed(dn, w, ig2):
                def fetch(part):
                    s = part % 2
                    return load(wf_in.at[part], w.at[s], 3 + s), load(ig_out.at[part], ig2.at[s], 5 + s)

                for cp in fetch(0):
                    cp.start()

                def body(part, _):
                    for cp in fetch(part):
                        cp.wait()

                    @pl.when(part + 1 < parts)
                    def _():
                        for cp in fetch(part + 1):
                            cp.start()

                    dn[...] += dot_nt(ig2[part % 2], w[part % 2])

                    @pl.when(part == parts * 3 // 4)
                    def _():
                        tick(nz + 1, fc_unit)

                    return 0

                lax.fori_loop(0, parts, body, 0)

            def finish_norm(dn, hid, hid_load):
                hid_load.wait()
                for v in (1, 2, 3):
                    sum_ref[v : v + 1, :] = jnp.zeros((1, width), f32)

                def norm(i, _):
                    at = pl.ds(pl.multiple_of(i * chunk, chunk), chunk)
                    values = hid[at, :]
                    grads = dn[at, :]
                    center = values - jnp.mean(values, axis=-1, keepdims=True)
                    factor = lax.rsqrt(jnp.mean(center * center, axis=-1, keepdims=True) + EPS)
                    xhat = center * factor
                    sum_ref[2:3, :] += jnp.sum(grads * xhat, axis=0, keepdims=True)
                    sum_ref[3:4, :] += jnp.sum(grads, axis=0, keepdims=True)
                    scaled = grads * vr_ref[1:2, :]
                    back = factor * (
                        scaled
                        - jnp.mean(scaled, axis=-1, keepdims=True)
                        - xhat * jnp.mean(scaled * xhat, axis=-1, keepdims=True)
                    )
                    hid[at, :] = back
                    return 0

                lax.fori_loop(0, tokens // chunk, norm, 0)

                def branch(bg, gl):
                    grad_load = load(g_in, gl, 3)
                    grad_load.start()
                    grad_load.wait()
                    hid[...] += gl[...].astype(f32)
                    low_grad = hid[...].astype(bf16)
                    sum_ref[1:2, :] = jnp.sum(low_grad.astype(f32), axis=0, keepdims=True)
                    for part in range(parts):
                        bg[part] = low_grad[:, part * n_out : (part + 1) * n_out]
                    outs = [
                        pltpu.make_async_copy(hid, hg_out, s_st.at[0]),
                        pltpu.make_async_copy(bg, bg_out, s_st.at[1]),
                    ]
                    for cp in outs:
                        cp.start()
                    for cp in outs:
                        cp.wait()

                pl.run_scoped(branch, pltpu.VMEM((parts, tokens, n_out), bf16), low_rows)

            pl.run_scoped(second_norm, full_rows, full_rows)
            given_back(0, swap.at[0], y_out)
            tick(nz + 2, fc_unit)

            def attention(ag):
                def back_out(acc, w, bgs):
                    def fetch(part):
                        s = part % 2
                        return load(wo_in.at[part], w.at[s], 3 + s), load(bg_out.at[part], bgs.at[s], 5 + s)

                    for cp in fetch(0):
                        cp.start()
                    acc[...] = jnp.zeros_like(acc)

                    def body(part, _):
                        for cp in fetch(part):
                            cp.wait()

                        @pl.when(part + 1 < parts)
                        def _():
                            for cp in fetch(part + 1):
                                cp.start()

                        acc[...] += dot_nt(bgs[part % 2], w[part % 2])
                        return 0

                    lax.fori_loop(0, parts, body, 0)
                    ag[:, :, wide - LANES :] = jnp.zeros((2, rows, LANES), bf16)
                    ag[:, :, :width] = acc[...].astype(bf16).reshape(2, rows, width)

                pl.run_scoped(
                    back_out,
                    full_rows,
                    pltpu.VMEM((2, width, n_out), bf16),
                    pltpu.VMEM((2, tokens, n_out), bf16),
                )

                pl.run_scoped(
                    functools.partial(attend_back, ag),
                    wide_low,
                    pltpu.VMEM((2, 2, rows, wide), f32),
                    pltpu.VMEM((2, 2, rows, wide), bf16),
                )

            def attend_back(ag, dq, own, oth):
                def heads(tq, tk, tv, ts, tof, tls):
                    def tiles(p):
                        s = p % 2
                        lanes = pl.ds(pl.multiple_of(p * LANES, LANES), LANES)
                        return [
                            pltpu.make_async_copy(src.at[:, :, lanes], dst.at[s], s_tile.at[i, s])
                            for i, (src, dst) in enumerate(
                                ((q_in, tq), (k_in, tk), (v_in, tv), (of_in, tof), (lse_in, tls))
                            )
                        ] + [pltpu.make_async_copy(s_in.at[:, :, :, lanes], ts.at[s], s_tile.at[5, s])]

                    for cp in tiles(0):
                        cp.start()

                    def body(p, _):
                        s = p % 2
                        for cp in tiles(p):
                            cp.wait()

                        @pl.when(p + 1 < pairs)
                        def _():
                            for cp in tiles(p + 1):
                                cp.start()

                        lanes = pl.ds(pl.multiple_of(p * LANES, LANES), LANES)
                        got_q, got_own, got_oth = pair_backward(
                            extra,
                            lambda i: tq[s, i],
                            lambda i: tk[s, i],
                            lambda i: tv[s, i],
                            lambda i: ts[s, 0, i],
                            lambda i: ts[s, 1, i],
                            lambda i: ag[i, :, lanes],
                            lambda i: tof[s, i],
                            lambda i: tls[s, i],
                            lambda i: rq_ref[i],
                            lambda i: ck_ref[i],
                            lambda i: cs_ref[i],
                            pair_masks(p, width),
                        )
                        for slot in range(2):
                            dq[slot, :, lanes] = got_q[slot].astype(bf16)
                            for kind in range(2):
                                own[kind, slot, :, lanes] = got_own[slot][kind]
                                oth[kind, slot, :, lanes] = got_oth[slot][kind].astype(bf16)
                        @pl.when(p == 5)
                        def _():
                            tick(nz + 3, fc_unit)

                        @pl.when(p == 10)
                        def _():
                            finish(2 * nz - 3)
                            second_stage(2 * nz - 1)

                        return 0

                    lax.fori_loop(0, pairs, body, 0)

                low_tile, full_tile = pltpu.VMEM((2, 2, rows, LANES), bf16), pltpu.VMEM((2, 2, rows, LANES), f32)
                pl.run_scoped(
                    heads, low_tile, low_tile, low_tile, pltpu.VMEM((2, 2, 2, rows, LANES), bf16), full_tile, full_tile
                )
                give = remote(oth, swap, s_kv.at[0], s_kv.at[1], at_sib)
                give.start()
                give.wait_recv()
                give.wait_send()
                for kind in range(2):
                    oth[kind] = (own[kind] + swap[kind].astype(f32)).astype(bf16)
                sum_ref[4:5, :] = jnp.sum(dq[...].astype(f32), axis=(0, 1))[None, :width]
                sum_ref[5:6, :] = jnp.sum(oth[1].astype(f32), axis=(0, 1))[None, :width]

                def spread(st):
                    def save(part):
                        return pltpu.make_async_copy(st.at[part % 2], pg_out.at[part], s_st.at[part % 2])

                    for part in range(parts):
                        if part >= 2:
                            save(part - 2).wait()
                        lo_part, hi_part = part * n_qkv, (part + 1) * n_qkv
                        for g in range(3):
                            lo, hi = max(lo_part, g * width), min(hi_part, (g + 1) * width)
                            if lo < hi:
                                a, b = lo - g * width, hi - g * width
                                piece = dq[:, :, a:b] if g == 0 else oth[g - 1, :, :, a:b]
                                st[part % 2, :, lo - lo_part : hi - lo_part] = piece.reshape(tokens, b - a)
                        save(part).start()
                    for part in range(parts - 2, parts):
                        save(part).wait()

                pl.run_scoped(spread, pltpu.VMEM((2, tokens, n_qkv), bf16))

            wide_low = pltpu.VMEM((2, rows, wide), bf16)
            pl.run_scoped(attention, wide_low)

        pl.run_scoped(
            second_phase,
            pltpu.VMEM((width, tokens), bf16),
            pltpu.VMEM((2, tokens, n_fc), bf16),
        )

        def third_phase(nt, at_t, pgs, bgs, dn, w, pg2, xs, hg):
            def qkv_unit(to, plane, store):
                loads = [
                    load(src.at[to * grid.ny + y_to], dst.at[y_to], sem + y_to)
                    for src, dst, sem in ((pg_out, pgs, 0), (bg_out, bgs, 6))
                    for y_to in range(2)
                ]
                for cp in loads:
                    cp.start()
                for cp in loads:
                    cp.wait()

                def body(i, _):
                    y_to, x_to = i // 2, i % 2
                    at = pl.ds(pl.multiple_of((2 * x_to + plane) * slab, 16), slab)
                    term = jnp.concatenate(
                        [dot_nn(nt[at, :], pgs[y_to]), dot_nn(at_t[at, :], bgs[y_to])], axis=1
                    )
                    store(y_to, x_to, beside(term))
                    return 0

                lax.fori_loop(0, 4, body, 0)

            begin = [load(n1t_in, nt, 2), load(at_in, at_t, 3)]
            for cp in begin:
                cp.start()
            for cp in begin:
                cp.wait()
            finish(2 * nz - 2)
            begin_unit(2 * nz, qkv_unit)

            def fetch(part):
                s = part % 2
                return load(wq_in.at[part], w.at[s], 2 + s), load(pg_out.at[part], pg2.at[s], 4 + s)

            late = [pltpu.make_async_copy(x_in, xs, s_st.at[0]), pltpu.make_async_copy(hg_out, hg, s_st.at[1])]
            for cp in (*late, *fetch(0)):
                cp.start()
            dn[...] = jnp.zeros_like(dn)

            def body(part, _):
                for cp in fetch(part):
                    cp.wait()

                @pl.when(part + 1 < parts)
                def _():
                    for cp in fetch(part + 1):
                        cp.start()

                dn[...] += dot_nt(pg2[part % 2], w[part % 2])

                @pl.when(part == parts // 2)
                def _():
                    second_stage(2 * nz)
                    begin_unit(2 * nz + 1, qkv_unit)

                return 0

            lax.fori_loop(0, parts, body, 0)
            for cp in late:
                cp.wait()
            sum_ref[6:8, :] = jnp.zeros((2, width), f32)

            def norm(i, _):
                at = pl.ds(pl.multiple_of(i * chunk, chunk), chunk)
                values = xs[at, :].astype(f32)
                grads = dn[at, :]
                center = values - jnp.mean(values, axis=-1, keepdims=True)
                factor = lax.rsqrt(jnp.mean(center * center, axis=-1, keepdims=True) + EPS)
                xhat = center * factor
                sum_ref[6:7, :] += jnp.sum(grads * xhat, axis=0, keepdims=True)
                sum_ref[7:8, :] += jnp.sum(grads, axis=0, keepdims=True)
                scaled = grads * vr_ref[2:3, :]
                back = factor * (
                    scaled
                    - jnp.mean(scaled, axis=-1, keepdims=True)
                    - xhat * jnp.mean(scaled * xhat, axis=-1, keepdims=True)
                )
                total = hg[at, :] + back
                hg[at, :] = total
                per = rows // chunk
                inside = pl.ds(pl.multiple_of(i % per * chunk, chunk), chunk)
                swap[1, i // per, inside, :width] = total.astype(bf16)
                return 0

            lax.fori_loop(0, tokens // chunk, norm, 0)
            give_back(1, swap.at[1], di_out)
            keep = pltpu.make_async_copy(hg, dx_out, s_st.at[1])
            keep.start()
            vec_step(0)
            tick(2 * nz + 2, qkv_unit)
            vec_step(1)
            tick(2 * nz + 3, qkv_unit)
            vec_step(2)
            finish(units - 3)
            finish(units - 2)
            vec_step(3)
            keep.wait()

        pl.run_scoped(
            third_phase,
            pltpu.VMEM((width, tokens), bf16),
            pltpu.VMEM((width, tokens), bf16),
            pltpu.VMEM((2, tokens, n_qkv), bf16),
            pltpu.VMEM((2, tokens, n_out), bf16),
            full_rows,
            pltpu.VMEM((2, width, n_qkv), bf16),
            pltpu.VMEM((2, tokens, n_qkv), bf16),
            low_rows,
            full_rows,
        )
        second_stage(units - 1)
        vec_step(4)
        finish(units - 1)
        given_back(1, swap.at[1], di_out)
        for kind, out in ((0, y_out), (1, di_out)):
            got_back(kind, swap.at[kind], out)
        for cp in (*sib(units - 1), *first(units - 1), *second(units - 1)):
            cp.wait_send()
        for u in range(units - nz, units - 1):
            for cp in line(u, 0, True, 0):
                cp.wait_send()

    any_, vm = pl.BlockSpec(memory_space=pl.ANY), pl.BlockSpec(memory_space=pltpu.VMEM)
    dma = pltpu.SemaphoreType.DMA
    halves = (h, n), (cols - h, n)
    scratch = []
    for dims in ((2, 2), (2, 2, 2), (2, 2), (2, 2), (), (3,)):
        scratch += [pltpu.VMEM((*dims, *half), bf16) for half in halves]
    scratch += [pltpu.VMEM((2, *half), f32) for half in halves]
    scratch += [pltpu.VMEM((nz - 1, *half), bf16) for half in halves]
    scratch += [pltpu.VMEM((2, nz + 1, *half), bf16) for half in halves]
    scratch += [
        pltpu.VMEM((2, 2, rows, wide), bf16),
        pltpu.VMEM((5, v_rows, width), f32),
        pltpu.VMEM((5, v_rows, width), f32),
        dma((6, units)),
        dma((6, units)),
        dma((2, units)),
        dma((2, 3, nz + 1)),
        dma((8,)),
        dma((2,)),
        dma((6, 2)),
        dma((2,)),
        dma((5,)),
        dma((5,)),
        dma((2, 2)),
        dma((2, 2)),
        dma((2,)),
        dma((2, 2, 2)),
    ]
    shape = jax.ShapeDtypeStruct
    return pl.pallas_call(
        kernel,
        out_shape=[
            *[shape((cols, n), f32)] * 3,
            shape((v_rows, width), f32),
            shape((2, rows, wide), bf16),
            shape((2, rows, wide), bf16),
            shape((tokens, width), f32),
            shape((tokens, width), f32),
            shape((parts, tokens, n_out), bf16),
            shape((parts, tokens, n_qkv), bf16),
            shape((parts, tokens, n_fc), bf16),
        ],
        in_specs=[any_] * 19 + [vm] * 4,
        out_specs=[any_] * 3 + [vm] + [any_] * 7,
        scratch_shapes=scratch,
        compiler_params=pltpu.CompilerParams(
            collective_id=5, has_side_effects=True, vmem_limit_bytes=60 * 1024 * 1024
        ),
        cost_estimate=cost(60e9, 200e6),
        name="backward",
    )(
        grad, proj_terms, act, slope, w_proj, hidden, normed_t, w_fc, w_out, queries, keys, values, other,
        att_full, logs, x_in, first_t, att_t, w_qkv, vec_rows, seg_row, seg_col, seg_other,
    )


def pick(array, index, axis):
    return lax.dynamic_index_in_dim(array, index, axis, keepdims=False)


def add_low(first, second):
    return (first.astype(f32) + second.astype(f32)).astype(bf16)


class Grid:
    def __init__(self, dp, ctx):
        self.dp, self.ctx = dp, ctx
        self.nx = max(ctx // 2, 1)
        self.ny = self.nx
        self.nz = dp // self.ny
        self.paired = self.nx == 2 and ctx == 4 and dp % 2 == 0

    def place(self):
        d, c = lax.axis_index("dp"), lax.axis_index("ctx")
        self.d, self.c = d, c
        self.z, self.y = d // self.ny, d % self.ny
        self.x, self.core = c // 2, c % 2

    def swap_core(self, v):
        return lax.ppermute(v, "ctx", [(i, i ^ 1) for i in range(self.ctx)])

    ACROSS = ((0, 2), (1, 3), (2, 1), (3, 0))
    WITHIN = ((2, 3), (3, 2))

    def by_sequence(self, v):
        first = self.x == 0
        across = lax.ppermute(pick(v, 1 - self.x, 0), "ctx", self.ACROSS)
        within = lax.ppermute(v[1], "ctx", self.WITHIN)
        return jnp.stack([jnp.where(first, v[0], across), jnp.where(first, across, within)])

    def by_position(self, v):
        first = self.x == 0
        across = lax.ppermute(pick(v, 1 - self.x, 0), "ctx", [(b, a) for a, b in self.ACROSS])
        within = lax.ppermute(v[1], "ctx", self.WITHIN)
        return jnp.stack([jnp.where(first, v[0], across), jnp.where(first, across, within)])


def on_device(grid, *args):
    (
        layer_input,
        grad_out,
        segment_ids,
        qkv_weight,
        q_bias,
        v_bias,
        out_weight,
        out_bias,
        fc_weight,
        fc_bias,
        proj_weight,
        proj_bias,
        ln1_gain,
        ln1_bias,
        ln2_gain,
        ln2_bias,
    ) = args
    seqs, rows, width = layer_input.shape
    tokens = seqs * rows
    parts, groups = grid.dp, grid.ctx
    both = ("dp", "ctx")
    grid.place()

    n_qkv, n_out, n_fc = qkv_weight.shape[1], out_weight.shape[1], fc_weight.shape[1]
    slab, hidden_slab = qkv_weight.shape[0], proj_weight.shape[0]
    paired = grid.paired and seqs == 2
    seg_blocks = segment_ids.reshape(seqs, groups, rows)
    vectors = (fc_bias, q_bias, v_bias, out_bias, proj_bias, ln1_gain, ln1_bias, ln2_gain, ln2_bias)
    sizes = [v.shape[0] for v in vectors]

    def unpack(packed):
        spread, at = [], 0
        for size in sizes:
            spread.append(packed[:, at : at + size].astype(f32))
            at += size
        return [v.reshape(-1) for v in spread]

    if paired:
        extra = 1 - grid.core
        chip_seg = pick(seg_blocks, grid.x, 0)
        seg_own = jnp.stack([pick(chip_seg, grid.core, 0), pick(chip_seg, 3 - grid.core, 0)])
        seg_other = jnp.stack([pick(chip_seg, extra, 0), pick(chip_seg, 3 - extra, 0)])
        packed = jnp.concatenate(vectors).astype(f32)[None]
        (
            w_qkv, w_out, w_fc, w_proj, packed, slope, activated, other, x_seq, grad_seq, normed1_t, normed2_t, attended_t,
            proj_terms, queries, keys, vals, attended_f32, log_total, hidden,
        ) = forward_gather(
            grid,
            layer_input,
            grad_out,
            (qkv_weight, out_weight, fc_weight, proj_weight.T),
            jnp.broadcast_to(packed, (8, packed.shape[1])),
            seg_own[:, :, None],
            seg_own[:, None, :],
            seg_other[:, None, :],
        )
        _, _, _, _, pb_all, g1, b1, g2, b2 = unpack(packed[:, :, 0].reshape(parts, -1))
        w_qkv = w_qkv.reshape(parts, width, n_qkv)
        w_fc = w_fc.reshape(parts, width, n_fc)
        w_proj = w_proj.reshape(groups, width, hidden_slab)
    else:
        packed = lax.all_gather(jnp.concatenate(vectors), "dp", axis=0)
        fcb, q_all, v_all, ob_all, pb_all, g1, b1, g2, b2 = unpack(packed)

        def gather(block, axes):
            return lax.all_gather(block, axes, axis=0)

        w_qkv = gather(qkv_weight, both).reshape(parts, width, n_qkv)
        w_out = gather(out_weight, both).reshape(parts, width, n_out)
        w_fc = gather(fc_weight, both).reshape(parts, width, n_fc)
        w_proj = gather(proj_weight.T, ("ctx", "dp")).reshape(groups, width, hidden_slab)
        out_full = w_out.transpose(1, 0, 2).reshape(width, width)
        values = layer_input.reshape(tokens, width).astype(f32)
        normed1 = layer_norm(values, g1, b1).astype(bf16)
        joined = jnp.concatenate([q_all, jnp.zeros((width,), f32), v_all])
        queries, key_rows, value_rows = qkv_project(normed1, w_qkv, joined.reshape(parts, 1, n_qkv))
        queries = queries.reshape(seqs, rows, width)
        own = jnp.stack([key_rows, value_rows]).reshape(2, seqs, rows, width)
        pairs_full = lax.all_gather(own, "ctx", axis=0)
        seg_mine = pick(seg_blocks, grid.c, 1)
        needed = seg_blocks[:, :, -1] >= seg_mine[:, :1]
        start = jnp.minimum(jnp.argmax(needed, axis=1).astype(jnp.int32), grid.c)
        bounds = jnp.concatenate([grid.c[None].astype(jnp.int32), start])
        attended, attended_f32, log_total = attention_forward(
            bounds, queries, pairs_full, seg_mine[:, :, None], seg_blocks[:, :, None, :]
        )
        attended = attended.reshape(tokens, width)
        hidden = values + jnp.dot(attended, out_full, preferred_element_type=f32) + ob_all
        normed2 = layer_norm(hidden, g2, b2).astype(bf16)
        inner, activated = feed_in(normed2, w_fc, fcb.reshape(parts, 1, n_fc), groups)

    def tall_cut(size):
        return (size // 2 + 15) // 16 * 16

    def by_columns(refs, core, z, store):
        for y_to in range(2):
            for x_to in range(2):
                at = pl.ds(pl.multiple_of((2 * x_to + core) * slab, 16), slab)
                terms = [
                    dot_nn(left[at, :], right[z * grid.ny + y_to])
                    for left, right in zip(refs[::2], refs[1::2])
                ]
                store(y_to, x_to, jnp.concatenate(terms, axis=1) if len(terms) > 1 else terms[0])

    def by_rows(refs, core, z, store):
        left, right = refs
        cols = width // parts
        at = pl.ds(pl.multiple_of(z * (grid.ny * cols), 16), grid.ny * cols)
        for x_to in range(2):
            term = dot_nn(left[at, :], right[2 * x_to + core])
            for y_to in range(2):
                store(y_to, x_to, term[y_to * cols : (y_to + 1) * cols])

    def reduced(pairs, collective_id, name):
        if not paired:
            everything = jnp.arange(parts, dtype=jnp.int32)
            results = []
            for left, right in pairs:
                whole = weight_grad(left.T, right, everything)
                whole = whole.reshape(parts * groups, slab, right.shape[2])
                results.append(lax.psum_scatter(whole, both, scatter_dimension=0).astype(f32))
            return results
        operands, ends = [], [0]
        for left, right in pairs:
            n = right.shape[2]
            full = n if len(ends) == len(pairs) else pl.cdiv(n, LANES) * LANES
            operands += [left.T, jnp.pad(right, ((0, 0), (0, 0), (0, full - n)))]
            ends.append(ends[-1] + full)
        total = summed_grads(
            grid, collective_id, operands, by_columns, (slab, ends[-1]), tall_cut(slab), name
        )
        return [total[:, at : at + pair[1].shape[2]] for at, pair in zip(ends, pairs)]

    def reduced_proj(left, right):
        f = right.shape[2]
        cols = width // parts
        if not paired:
            whole = weight_grad(left.T, right, jnp.arange(groups, dtype=jnp.int32))
            whole = whole.reshape(groups * parts, cols, f)
            return lax.psum_scatter(whole, ("ctx", "dp"), scatter_dimension=0).astype(f32)
        return summed_grads(grid, 1, [left.T, right], by_rows, (cols, f), tall_cut(cols), "rs_proj")

    if paired:
        proj_halves, fc_halves, last_halves, sums, output, far, near, *_ = backward_sums(
            grid,
            grad_seq.reshape(tokens, width),
            proj_terms,
            activated,
            slope,
            w_proj,
            hidden.reshape(tokens, width),
            normed2_t,
            w_fc,
            w_out.reshape(parts, width, n_out),
            queries,
            keys,
            vals,
            other,
            attended_f32,
            log_total,
            x_seq.reshape(tokens, width),
            normed1_t,
            attended_t,
            w_qkv,
            jnp.stack([pb_all, g2, g1] + [jnp.zeros_like(g1)] * 5),
            seg_own[:, None, :],
            seg_own[:, :, None],
            seg_other[:, :, None],
        )
        proj_weight_grad = proj_halves.T
        fc_weight_grad = jnp.concatenate([fc_halves[:, :n_fc], fc_halves[:, n_fc:]], axis=0)
        last = jnp.concatenate([last_halves[:, :n_fc], last_halves[:, n_fc:]], axis=0)
        qkv_weight_grad, out_weight_grad = last[:, :n_qkv], last[:, n_qkv:]
        far = far[:, :, :width].astype(f32)
        near = near.reshape(2, rows, width)
        stays = (grid.x == 0) & (jnp.arange(2) == 0)
        input_grad = jnp.where(stays[:, None, None], near, far)
        own = pick(sums[:8].reshape(8, parts, n_out), grid.d, 1)
        fc_own = pick(sums[8:, :n_fc], grid.d, 0)
        return (
            output[:, :, :width],
            input_grad,
            qkv_weight_grad,
            own[4],
            own[5],
            out_weight_grad,
            own[1],
            fc_weight_grad,
            fc_own,
            proj_weight_grad,
            own[0],
            own[6],
            own[7],
            own[2],
            own[3],
        )
    else:
        mlp_grad = grad_out.reshape(tokens, width)
        cotangent = mlp_grad.astype(f32)
        output = feed_out(activated, w_proj, hidden, pb_all[None])
        proj_bias_grad = jnp.sum(cotangent, axis=0)
        inner_grad, fc_bias_grad = feed_back(mlp_grad, w_proj, inner, parts)
        proj_weight_grad = reduced_proj(mlp_grad, activated).T
        (fc_weight_grad,) = reduced([(normed2, inner_grad)], 2, "rs_fc")
        normed2_grad = back_project(inner_grad, w_fc)
        norm2_out, norm2_pull = jax.vjp(layer_norm, hidden, g2, b2)
        hidden_ln, g2_grad, b2_grad = norm2_pull(normed2_grad)
        hidden_grad = cotangent + hidden_ln
        branch_grad = hidden_grad.astype(bf16)
        out_bias_grad = jnp.sum(branch_grad, axis=0, dtype=f32)
        attended_grad = jnp.einsum(
            "nd,ed->ne", branch_grad, out_full, preferred_element_type=f32
        ).astype(bf16)
        branch_parts = branch_grad.reshape(tokens, parts, n_out).transpose(1, 0, 2)
        query_grad, pairs_grad = attention_backward(
            bounds,
            queries,
            pairs_full,
            seg_blocks[:, :, :, None],
            seg_mine[:, None, :],
            attended_grad.reshape(seqs, rows, width),
            attended_f32,
            log_total,
        )
        pair_grad = lax.psum_scatter(pairs_grad, "ctx", scatter_dimension=0)
        pair_grad = pair_grad.reshape(2, tokens, width)
        projected_grad = jnp.concatenate(
            [query_grad.reshape(tokens, width), pair_grad[0], pair_grad[1]], axis=1
        )
        q_bias_grad = jnp.sum(query_grad.reshape(tokens, width), axis=0, dtype=f32)
        v_bias_grad = jnp.sum(pair_grad[1], axis=0, dtype=f32)
        by_part = projected_grad.reshape(tokens, parts, n_qkv).transpose(1, 0, 2)
    out_weight_grad, qkv_weight_grad = reduced(
        [(attended, branch_parts), (normed1, by_part)], 3, "rs_qkv"
    )
    normed1_grad = back_project(by_part, w_qkv)
    norm1_out, norm1_pull = jax.vjp(layer_norm, values, g1, b1)
    values_ln, g1_grad, b1_grad = norm1_pull(normed1_grad)
    input_grad = hidden_grad + values_ln

    output, input_grad = (v.reshape(seqs, rows, width) for v in (output, input_grad))
    sums = [
        fc_bias_grad,
        q_bias_grad,
        v_bias_grad,
        out_bias_grad,
        proj_bias_grad,
        g1_grad,
        b1_grad,
        g2_grad,
        b2_grad,
    ]
    stacked = jnp.concatenate([v.reshape(parts, -1) for v in sums], axis=1)
    total = pick(lax.psum(stacked, both), grid.d, 0)
    vec, at = [], 0
    for size in sizes:
        vec.append(total[at : at + size])
        at += size
    return (
        output,
        input_grad,
        qkv_weight_grad,
        vec[1],
        vec[2],
        out_weight_grad,
        vec[3],
        fc_weight_grad,
        vec[0],
        proj_weight_grad,
        vec[4],
        vec[5],
        vec[6],
        vec[7],
        vec[8],
    )


def solution(mesh):
    rows3, mat, vec = P("dp", "ctx", None), P("ctx", "dp"), P("dp")
    grid = Grid(mesh.shape["dp"], mesh.shape["ctx"])
    return jax.shard_map(
        functools.partial(on_device, grid),
        mesh=mesh,
        in_specs=(
            rows3,
            rows3,
            P("dp", None),
            mat,
            vec,
            vec,
            mat,
            vec,
            mat,
            vec,
            mat,
            vec,
            vec,
            vec,
            vec,
            vec,
        ),
        out_specs=(
            rows3,
            rows3,
            mat,
            vec,
            vec,
            mat,
            vec,
            mat,
            vec,
            mat,
            vec,
            vec,
            vec,
            vec,
            vec,
        ),
        check_vma=False,
    )
```
